256 devices in a mesh: ctx: 32 (over y, z), head: 8 (over x, core).
Axes of the slice: x: 4, y: 4, z: 8, core: 2. Of those that a mesh axis runs over, the one named last changes fastest.
Arguments:
- lin_q: bfloat16 [4096, 32, 128], P('ctx', 'head'), may hold values from -4 to 4
- lin_k: bfloat16 [4096, 32, 128], P('ctx', 'head'), may hold values from -4 to 4
- lin_v: bfloat16 [4096, 32, 128], P('ctx', 'head'), may hold values from -16 to 16
- lin_decay: float32 [32, 4096], P('head', 'ctx'), may hold values from -1.5 to 0
- norm_gain: float32 [32, 128], P('head'), may hold values from 0.1 to 1.9
- soft_q: bfloat16 [4096, 32, 128], P('ctx', 'head'), may hold values from -5 to 5
- soft_k: bfloat16 [4096, 32, 128], P('ctx', 'head'), may hold values from -5 to 5
- soft_v: bfloat16 [4096, 32, 128], P('ctx', 'head'), may hold values from -5 to 5
- out_grad: bfloat16 [4096, 32, 128], P('ctx', 'head'), may hold values from -5 to 5
- block_lists: int32 [32, 16], P('ctx'), may hold values from 0 to 30, as said below
- block_counts: int32 [32], P('ctx'), may hold values from 0 to 16, as said below
Outputs:
- lin_dq: bfloat16 [4096, 32, 128], P('ctx', 'head')
- lin_dk: bfloat16 [4096, 32, 128], P('ctx', 'head')
- lin_dv: bfloat16 [4096, 32, 128], P('ctx', 'head')
- soft_dq: bfloat16 [4096, 32, 128], P('ctx', 'head')
- soft_dk: bfloat16 [4096, 32, 128], P('ctx', 'head')
- soft_dv: bfloat16 [4096, 32, 128], P('ctx', 'head')
The draws below stay inside these ranges and needn't reach their ends.
Inputs may be any that keep to these rules, and one draw needn't show every extreme that they name: `block_lists`: entries past block_counts[b] are 0. The first block_counts[b] entries of query block b are distinct blocks that lie before the span of 128 tokens holding b. All query blocks of one span name together at most one block of each other span. In every span after the first, some query block names every block that its span names; from the second span on these include block 0, and from the third on also the last block before the span. `block_counts`: in span i of 128 tokens some query block has the count min(i, 16); every count is at most that; counts are 0 only in the first span.
All inputs are finite; a program needn't handle non-finite values.
Results may differ from the reference program's by a relative error of at most 0.011.
Values may be sent and summed in bfloat16 or wider, within the bound.
A program may use at most 128 MiB of HBM per device.

```python
import math
import jax
import jax.numpy as jnp
from jax import lax

H = 32
HD = 128
BLK = 128
NSEL = 16
TOK_DEV = 128
TOKENS = 4096
QB_DEV = 1
NQB = 32
N_CTX = 32


def draw_lin_v(key, part):
    base_key = jax.random.fold_in(key, 41)
    first_key = jax.random.fold_in(base_key, 0)
    ramp = jnp.arange(H, dtype=jnp.float32) / max(H - 1, 1)
    shape = (TOKENS, H, HD)
    values = jax.random.truncated_normal(first_key, -4.0, 4.0, shape, jnp.float32) * (3.0 ** ramp)[None, :, None]
    return values.astype(jnp.bfloat16)


def draw_lin_decay(key, part):
    base_key = jax.random.fold_in(key, 11)
    keys_here = jax.random.split(base_key, 7)
    slow_share = 0.5
    slow = jax.random.bernoulli(keys_here[0], slow_share, (H,))
    slow_rate = jnp.exp(jax.random.uniform(keys_here[1], (H,), jnp.float32, math.log(8e-06), math.log(4e-05)))
    fast_rate = jnp.exp(jax.random.uniform(keys_here[2], (H,), jnp.float32, math.log(0.02), math.log(0.035)))
    base_rate = jnp.where(slow, slow_rate, fast_rate)
    span_total = TOKENS // TOK_DEV
    span_factor = jnp.exp(jax.random.uniform(keys_here[3], (H, span_total), jnp.float32, math.log(0.6), math.log(1.7)))
    token_factor = jnp.exp(jax.random.uniform(keys_here[4], (H, TOKENS), jnp.float32, math.log(0.7), math.log(1.4)))
    decay_speed = base_rate[:, None] * jnp.repeat(span_factor, TOK_DEV, axis=1) * token_factor
    slot_spots = jax.random.randint(keys_here[5], (2,), 0, TOKENS)
    loss_values = jax.random.uniform(keys_here[6], (H, 2), jnp.float32, 0.22, 0.69)
    token_offsets = jnp.arange(TOKENS)
    spike_factor = jnp.where(token_offsets[None, :] == slot_spots[0], loss_values[:, 0:1], 0.0) + jnp.where(token_offsets[None, :] == slot_spots[1], loss_values[:, 1:2], 0.0)
    return (-decay_speed - spike_factor).astype(jnp.float32)


def drawn_pairs(key):
    base_key = jax.random.fold_in(key, 23)
    first_key, second_key = jax.random.split(base_key, 2)
    shape = (TOKENS, H, HD)
    queries = jax.random.truncated_normal(first_key, -4.5, 4.5, shape, jnp.float32)
    keys_drawn = jax.random.truncated_normal(second_key, -4.5, 4.5, shape, jnp.float32)
    return (queries, keys_drawn)


def draw_soft_q(key, part):
    return drawn_pairs(key)[0].astype(jnp.bfloat16)


def draw_soft_k(key, part):
    return drawn_pairs(key)[1].astype(jnp.bfloat16)


def span_routes(key):
    base_key = jax.random.fold_in(key, 31)
    span_total = TOKENS // TOK_DEV

    def one_span(span_index):
        keys_here = jax.random.split(jax.random.fold_in(base_key, span_index), 5)
        shuffled = jax.random.permutation(keys_here[0], span_total).astype(jnp.int32)
        usable = (shuffled >= 1) & (shuffled < span_index - 1)
        order = jnp.argsort(jnp.where(usable, 0, 1), stable=True)
        others = jnp.concatenate([shuffled[order], jnp.zeros((NSEL,), jnp.int32)])[:NSEL - 2]
        owners = jnp.concatenate([jnp.zeros((1,), jnp.int32), jnp.reshape(span_index - 1, (1,)).astype(jnp.int32), others])
        picked_blocks = jax.random.randint(keys_here[1], (NSEL,), 0, QB_DEV).astype(jnp.int32)
        picked_blocks = picked_blocks.at[0].set(0).at[1].set(QB_DEV - 1)
        block_ids = owners * QB_DEV + picked_blocks
        live_total = jnp.minimum(span_index, NSEL)
        counts = jax.random.randint(keys_here[2], (QB_DEV,), 0, NSEL) % jnp.maximum(live_total, 1) + 1
        full_one = jax.random.randint(keys_here[3], (), 0, QB_DEV)
        counts = jnp.where(jnp.arange(QB_DEV) == full_one, live_total, counts)
        counts = jnp.where(live_total == 0, 0, counts).astype(jnp.int32)

        def one_block(sub_key, count_here):
            ranking = jax.random.permutation(sub_key, NSEL).astype(jnp.int32)
            inside = ranking < live_total
            ranked = ranking[jnp.argsort(jnp.where(inside, 0, 1), stable=True)]
            return jnp.where(jnp.arange(NSEL) < count_here, block_ids[ranked], 0)
        block_keys = jax.random.split(keys_here[4], QB_DEV)
        lists = jax.vmap(one_block)(block_keys, counts)
        return (lists, counts)
    lists, counts = jax.vmap(one_span)(jnp.arange(span_total, dtype=jnp.int32))
    return (lists.reshape(NQB, NSEL).astype(jnp.int32), counts.reshape(NQB).astype(jnp.int32))


def draw_block_lists(key, part):
    return span_routes(key)[0]


def draw_block_counts(key, part):
    return span_routes(key)[1]


def shard_levels(key, extent, cuts, low, top_value):
    level = 1.0
    for dim, shards_of in cuts:
        steps = jax.random.uniform(jax.random.fold_in(jax.random.fold_in(key, 6), dim), (shards_of,), jnp.float32, low / len(cuts), top_value / len(cuts))
        level = level * jnp.repeat(jnp.exp(steps), extent[dim] // shards_of).reshape((-1,) + (1,) * (len(extent) - 1 - dim))
    return level


def centred(key, shape, scale, limit, pieces=(), held_as=jnp.bfloat16):
    values = jax.random.normal(key, shape, jnp.float32) * scale
    if len(pieces) > 0:
        values = shard_levels(key, shape, pieces, -0.22, 0.18) * values
    return jnp.clip(values, min=-limit, max=limit).astype(held_as)


def setup_inputs(seed: int = 0) -> dict:
    streams_of = jax.random.split(jax.random.key(seed), 12)
    return {
        "lin_q": centred(streams_of[0], (TOKENS, H, HD), 1.0, 4.0, ((0, 32), (1, 8))),
        "lin_k": centred(streams_of[1], (TOKENS, H, HD), 1.0, 4.0, ((0, 32), (1, 8))),
        "lin_v": draw_lin_v(jax.random.fold_in(streams_of[11], 71), 0),
        "lin_decay": draw_lin_decay(jax.random.fold_in(streams_of[11], 71), 0),
        "norm_gain": jnp.clip(1.0 + 0.18 * jax.random.normal(streams_of[4], (H, HD), jnp.float32), 0.1, 1.9),
        "soft_q": draw_soft_q(jax.random.fold_in(streams_of[11], 71), 0),
        "soft_k": draw_soft_k(jax.random.fold_in(streams_of[11], 71), 0),
        "soft_v": centred(streams_of[7], (TOKENS, H, HD), 1.0, 5.0, ((0, 32), (1, 8))),
        "out_grad": centred(streams_of[8], (TOKENS, H, HD), 1.0, 5.0, ((0, 32), (1, 8))),
        "block_lists": draw_block_lists(jax.random.fold_in(streams_of[11], 71), 0),
        "block_counts": draw_block_counts(jax.random.fold_in(streams_of[11], 71), 0),
    }


epsilon = 1e-05
exact_precision = lax.Precision.HIGHEST

def decay_tables(decays):
    running = jnp.cumsum(decays, axis=1)
    finish = running[:, -1]
    length = decays.shape[1]
    below_diag = (jnp.arange(length)[:, None] >= jnp.arange(length)[None, :])[None]
    spread = running[:, :, None] - running[:, None, :]
    within = jnp.where(below_diag, jnp.exp(jnp.where(below_diag, spread, 0.0)), 0.0)
    return (jnp.exp(finish), jnp.exp(finish[:, None] - running), jnp.exp(running), within)

def sparse_grads(queries, grads_out, key_rows, value_rows, allowed):
    score_scale = queries.shape[-1] ** (-0.5)
    scores = jnp.einsum('bqhd,bkhd->bhqk', queries.astype(jnp.float32), key_rows.astype(jnp.float32)) * score_scale
    key_mask = allowed[:, None]
    scores = jnp.where(key_mask, scores, -1e+30)
    row_max = lax.optimization_barrier(jnp.max(scores, axis=-1, keepdims=True))
    weights = jnp.where(key_mask, jnp.exp(scores - row_max), 0.0)
    softmax_probs = weights / lax.optimization_barrier(jnp.sum(weights, axis=-1, keepdims=True))
    rounded = softmax_probs.astype(jnp.bfloat16)
    outputs = jnp.einsum('bhqk,bkhd->bqhd', rounded.astype(jnp.float32), value_rows.astype(jnp.float32))
    row_delta = lax.optimization_barrier(jnp.sum(grads_out.astype(jnp.float32) * outputs, axis=-1))
    grad_probs = jnp.einsum('bqhd,bkhd->bhqk', grads_out.astype(jnp.float32), value_rows.astype(jnp.float32))
    grad_scores = (softmax_probs * (grad_probs - jnp.transpose(row_delta, (0, 2, 1))[..., None])).astype(jnp.bfloat16)
    query_gradient = jnp.einsum('bhqk,bkhd->bqhd', grad_scores.astype(jnp.float32), key_rows.astype(jnp.float32)) * score_scale
    key_gradient = jnp.einsum('bhqk,bqhd->bkhd', grad_scores.astype(jnp.float32), queries.astype(jnp.float32)) * score_scale
    value_gradient = jnp.einsum('bhqk,bqhd->bkhd', rounded.astype(jnp.float32), grads_out.astype(jnp.float32))
    return (query_gradient, key_gradient, value_gradient)

def reference(lin_q, lin_k, lin_v, lin_decay, norm_gain, soft_q, soft_k, soft_v, out_grad, block_lists, block_counts):
    query_spans = lin_q.astype(jnp.float32).reshape(N_CTX, TOK_DEV, H, HD)
    key_spans = lin_k.astype(jnp.float32).reshape(N_CTX, TOK_DEV, H, HD)
    value_spans = lin_v.astype(jnp.float32).reshape(N_CTX, TOK_DEV, H, HD)
    decay_spans = jnp.transpose(lin_decay.reshape(H, N_CTX, TOK_DEV), (1, 0, 2))

    def forward_step(carried_state, slices):
        current_query, current_key, current_value, decay_here = slices
        carry_decay, trailing_decay, leading_decay, within = decay_tables(decay_here)
        pair_weights = jnp.einsum('thk,shk->hts', current_query, current_key, precision=exact_precision) * within
        span_output = jnp.einsum('hts,shv->thv', pair_weights, current_value, precision=exact_precision)
        span_output = span_output + leading_decay.T[:, :, None] * jnp.einsum('wfg,fgl->wfl', current_query, carried_state, precision=exact_precision)
        segment_state = jnp.einsum('boz,bor->ozr', current_key * trailing_decay.T[:, :, None], current_value, precision=exact_precision)
        return (carry_decay[:, None, None] * carried_state + segment_state, (carried_state, span_output))
    zero_state = jnp.zeros((H, HD, HD), jnp.float32)
    _, (states_in, span_outs) = lax.scan(forward_step, zero_state, (query_spans, key_spans, value_spans, decay_spans))
    layer_out = span_outs.reshape(TOKENS, H, HD)
    root_mean = jnp.sqrt(lax.optimization_barrier(jnp.sum(layer_out * layer_out, axis=(1, 2))) / (H * HD) + epsilon)
    query_blocks = soft_q.reshape(NQB, BLK, H, HD)
    key_blocks = soft_k.reshape(NQB, BLK, H, HD)
    value_blocks = soft_v.reshape(NQB, BLK, H, HD)
    grad_blocks = out_grad.reshape(NQB, BLK, H, HD)
    span_lists = block_lists.reshape(N_CTX, QB_DEV, NSEL)
    span_counts = block_counts.reshape(N_CTX, QB_DEV)
    causal = jnp.arange(BLK)[:, None] >= jnp.arange(BLK)[None, :]
    entries = QB_DEV * NSEL

    def sparse_step(accum, span_index):
        acc_key, acc_value = accum
        first = (span_index * QB_DEV).astype(jnp.int32)
        query_rows = lax.dynamic_slice_in_dim(query_blocks, first, QB_DEV, 0)
        grad_rows = lax.dynamic_slice_in_dim(grad_blocks, first, QB_DEV, 0)
        own_keys = lax.dynamic_slice_in_dim(key_blocks, first, QB_DEV, 0)
        own_values = lax.dynamic_slice_in_dim(value_blocks, first, QB_DEV, 0)
        my_lists = span_lists[span_index]
        my_counts = span_counts[span_index]
        my_live = jnp.arange(NSEL)[None, :] < my_counts[:, None]
        listed_keys = key_blocks[my_lists].reshape(QB_DEV, NSEL * BLK, H, HD)
        listed_values = value_blocks[my_lists].reshape(QB_DEV, NSEL * BLK, H, HD)
        key_rows = jnp.concatenate([own_keys, listed_keys], axis=1)
        value_rows = jnp.concatenate([own_values, listed_values], axis=1)
        remote_mask = jnp.broadcast_to(jnp.repeat(my_live, BLK, axis=1)[:, None, :], (QB_DEV, BLK, NSEL * BLK))
        allowed = jnp.concatenate([jnp.broadcast_to(causal, (QB_DEV, BLK, BLK)), remote_mask], axis=2)
        query_gradient, key_gradient, value_gradient = sparse_grads(query_rows, grad_rows, key_rows, value_rows, allowed)
        flat_ids = my_lists.reshape(entries)
        flat_live = my_live.reshape(entries)
        flat_owner = flat_ids // QB_DEV
        segment = jnp.where(flat_live, flat_owner, N_CTX).astype(jnp.int32)
        remote_key = key_gradient[:, BLK:].reshape(entries, BLK, H, HD)
        remote_value = value_gradient[:, BLK:].reshape(entries, BLK, H, HD)
        part_key = jax.ops.segment_sum(remote_key, segment, num_segments=N_CTX + 1)[:N_CTX].astype(jnp.bfloat16)
        part_value = jax.ops.segment_sum(remote_value, segment, num_segments=N_CTX + 1)[:N_CTX].astype(jnp.bfloat16)
        part_key = lax.optimization_barrier(part_key).astype(jnp.float32)
        part_value = lax.optimization_barrier(part_value).astype(jnp.float32)
        owners = jnp.arange(N_CTX, dtype=jnp.int32)
        matches = flat_live[None, :] & (flat_owner[None, :] == owners[:, None])
        target = lax.optimization_barrier(jnp.max(jnp.where(matches, flat_ids[None, :], -1), axis=1))
        dest = jnp.where(target >= 0, target, NQB).astype(jnp.int32)
        acc_key = acc_key.at[dest].add(part_key)
        acc_value = acc_value.at[dest].add(part_value)
        return ((acc_key, acc_value), (query_gradient, key_gradient[:, :BLK], value_gradient[:, :BLK]))
    empty = jnp.zeros((NQB + 1, BLK, H, HD), jnp.float32)
    (acc_key, acc_value), (query_gradient, own_key, own_value) = lax.scan(sparse_step, (empty, empty), jnp.arange(N_CTX, dtype=jnp.int32))
    soft_dq = query_gradient.reshape(TOKENS, H, HD).astype(jnp.bfloat16)
    soft_dk = (own_key.reshape(TOKENS, H, HD) + acc_key[:NQB].reshape(TOKENS, H, HD)).astype(jnp.bfloat16)
    value_total = own_value.reshape(TOKENS, H, HD) + acc_value[:NQB].reshape(TOKENS, H, HD)
    soft_dv = value_total.astype(jnp.bfloat16)
    cotangent = out_grad.astype(jnp.float32) + value_total
    scaled = norm_gain[None] * cotangent
    inner = lax.optimization_barrier(jnp.sum(scaled * layer_out, axis=(1, 2)))
    linear_cotangent = scaled / root_mean[:, None, None] - layer_out * (inner / (H * HD * root_mean ** 3))[:, None, None]
    cot_spans = linear_cotangent.reshape(N_CTX, TOK_DEV, H, HD)

    def backward_step(carried_state, slices):
        current_query, current_key, current_value, decay_here, local_cotangent, incoming_state = slices
        carry_decay, trailing_decay, leading_decay, within = decay_tables(decay_here)
        grad_pair = jnp.einsum('thv,shv->hts', local_cotangent, current_value, precision=exact_precision) * within
        pair_weights = jnp.einsum('thk,shk->hts', current_query, current_key, precision=exact_precision) * within
        query_gradient = jnp.einsum('hts,shk->thk', grad_pair, current_key, precision=exact_precision)
        query_gradient = query_gradient + leading_decay.T[:, :, None] * jnp.einsum('fqs,qrs->fqr', local_cotangent, incoming_state, precision=exact_precision)
        key_gradient = jnp.einsum('hts,thk->shk', grad_pair, current_query, precision=exact_precision)
        key_gradient = key_gradient + trailing_decay.T[:, :, None] * jnp.einsum('fut,ujt->fuj', current_value, carried_state, precision=exact_precision)
        value_gradient = jnp.einsum('hts,thv->shv', pair_weights, local_cotangent, precision=exact_precision)
        value_gradient = value_gradient + trailing_decay.T[:, :, None] * jnp.einsum('zpu,pux->zpx', current_key, carried_state, precision=exact_precision)
        segment_state = jnp.einsum('boz,bor->ozr', current_query * leading_decay.T[:, :, None], local_cotangent, precision=exact_precision)
        return (segment_state + carry_decay[:, None, None] * carried_state, (query_gradient, key_gradient, value_gradient))
    _, (lin_dq, lin_dk, lin_dv) = lax.scan(backward_step, zero_state, (query_spans, key_spans, value_spans, decay_spans, cot_spans, states_in), reverse=True)
    lin_dq = lin_dq.reshape(TOKENS, H, HD).astype(jnp.bfloat16)
    lin_dk = lin_dk.reshape(TOKENS, H, HD).astype(jnp.bfloat16)
    lin_dv = lin_dv.reshape(TOKENS, H, HD).astype(jnp.bfloat16)
    return (lin_dq, lin_dk, lin_dv, soft_dq, soft_dk, soft_dv)
```

```python
import functools

import jax
import jax.numpy as jnp
from jax import lax
from jax.experimental import pallas as pl
from jax.experimental.pallas import tpu as pltpu
from jax.sharding import PartitionSpec as P

NY = 4
HL = 4
B = 128
NSEL = 16
EPS = 1e-05
SCALE = 128 ** (-0.5)
NEG = -1e30
BIG = 1e30
F32 = jnp.float32
BF16 = jnp.bfloat16
MESH = pl.DeviceIdType.MESH
HIGH = lax.Precision.HIGHEST


def mm(a, b):
    return lax.dot_general(a, b, (((1,), (0,)), ((), ())), preferred_element_type=F32)


def mm_t(a, b):
    return lax.dot_general(a, b, (((1,), (1,)), ((), ())), preferred_element_type=F32)


def t_mm(a, b):
    return lax.dot_general(a, b, (((0,), (0,)), ((), ())), preferred_element_type=F32)


def iota(dim):
    return lax.broadcasted_iota(jnp.int32, (B, B), dim)


def col_of(row):
    return jnp.transpose(jnp.broadcast_to(row, (B, B)))


def row_of(col):
    return jnp.transpose(jnp.broadcast_to(col, (B, B)))[0:1]


def running_of(decay):
    upper = (iota(0) <= iota(1)).astype(F32)
    return lax.dot_general(
        decay, upper, (((1,), (0,)), ((), ())), precision=HIGH, preferred_element_type=F32
    )


def within_of(row, col):
    keep = iota(0) >= iota(1)
    return jnp.where(keep, jnp.exp(jnp.where(keep, col - row, 0.0)), 0.0)


def slot_of(r, y):
    return jnp.where(lax.rem(y + 3, NY) == r, 0, jnp.where(lax.rem(y + 1, NY) == r, 1, 2))


def place(nz):
    own = lax.axis_index("ctx")
    return own // nz, lax.rem(own, nz)


def start_remote(src, dst, send, recv, ctx, head):
    pltpu.make_async_remote_copy(
        src_ref=src, dst_ref=dst, send_sem=send, recv_sem=recv, device_id=(ctx, head), device_id_type=MESH
    ).start()


def wait_recv(ref, recv, ctx, head):
    pltpu.make_async_remote_copy(
        src_ref=ref, dst_ref=ref, send_sem=recv, recv_sem=recv, device_id=(ctx, head), device_id_type=MESH
    ).wait_recv()


def wait_send(ref, send, ctx, head):
    pltpu.make_async_remote_copy(
        src_ref=ref, dst_ref=ref, send_sem=send, recv_sem=send, device_id=(ctx, head), device_id_type=MESH
    ).wait_send()


def prep_kernel(lq, lk, lv, sq, sk, sv, og, dec, own, lin, state, fin, tmp):
    def heads(ref, store):
        tmp[...] = ref[...].astype(F32)
        for h in range(HL):
            store(h, tmp[pl.ds(h, B, stride=HL), :].astype(BF16))

    def into(dst, a):
        def store(h, value):
            dst[h, a] = value

        return store

    heads(sk, into(own, 0))
    heads(sv, into(own, 1))
    heads(sq, into(own, 2))
    heads(og, into(own, 3))
    heads(lq, into(lin, 0))
    heads(lk, into(lin, 1))
    heads(lv, into(lin, 2))
    run = running_of(dec[...])
    finish = run[:, B - 1 : B]
    fin[...] = jnp.concatenate([jnp.broadcast_to(finish, (HL, B))] * 2, axis=0)
    trailing = jnp.exp(finish - run)
    for h in range(HL):
        k = lin[h, 1].astype(F32) * col_of(trailing[h : h + 1])
        state[pl.ds(h * B, B), :] = t_mm(k.astype(BF16), lin[h, 2]).astype(BF16)


def prep(arrays, decay):
    full = pl.BlockSpec(memory_space=pltpu.VMEM)
    return pl.pallas_call(
        prep_kernel,
        out_shape=(
            jax.ShapeDtypeStruct((HL, 4, B, B), BF16),
            jax.ShapeDtypeStruct((HL, 3, B, B), BF16),
            jax.ShapeDtypeStruct((HL * B, B), BF16),
            jax.ShapeDtypeStruct((2 * HL, B), F32),
        ),
        in_specs=[full] * 8,
        out_specs=(full,) * 4,
        scratch_shapes=[pltpu.VMEM((HL * B, B), F32)],
    )(*arrays, decay)


def scan_scratch(nz):
    rs = HL * B // nz
    return [
        pltpu.VMEM((nz, rs, B), BF16),
        pltpu.VMEM((nz, rs, B), F32),
        pltpu.VMEM((NY, rs, B), F32),
        pltpu.VMEM((rs, B), F32),
        pltpu.VMEM((nz, rs, B), BF16),
        pltpu.SemaphoreType.DMA((6, nz)),
        pltpu.SemaphoreType.DMA((2,)),
    ]


def scan_start(nz, head, local, bufs):
    zbuf, sems, lsem = bufs[0], bufs[5], bufs[6]
    rs = HL * B // nz
    y, z = place(nz)
    for d in range(1, nz):
        zz = lax.rem(z + d, nz)
        start_remote(
            local.at[pl.ds(zz * rs, rs)], zbuf.at[z], sems.at[0, zz], sems.at[1, z], y * nz + zz, head
        )
    pltpu.make_async_copy(local.at[pl.ds(z * rs, rs)], zbuf.at[z], lsem.at[0]).start()


def scan_rows(nz, head, local, fin, bufs, reverse):
    zbuf, ebuf, tbuf, tsrc, _, sems, lsem = bufs
    rs = HL * B // nz
    y, z = place(nz)
    own = y * nz + z
    hz = z * rs // B
    pltpu.make_async_copy(local.at[pl.ds(z * rs, rs)], zbuf.at[z], lsem.at[0]).wait()
    for d in range(1, nz):
        zz = lax.rem(z + d, nz)
        wait_recv(zbuf.at[zz], sems.at[1, zz], own, head)

    total = jnp.zeros((rs, B), F32)
    for lap in range(nz):
        m = nz - 1 - lap if reverse else lap
        ebuf[m] = total
        total = total * jnp.exp(fin[y, m, pl.ds(hz, 1), :]) + zbuf[m].astype(F32)
    tsrc[...] = total
    for d in range(1, NY):
        yy = lax.rem(y + d, NY)
        start_remote(tsrc, tbuf.at[y], sems.at[2, yy], sems.at[3, y], yy * nz + z, head)
    for d in range(1, nz):
        zz = lax.rem(z + d, nz)
        wait_send(zbuf.at[0], sems.at[0, zz], own, head)


def scan_spread(nz, head, fin, out, bufs, reverse):
    _, ebuf, tbuf, tsrc, sbuf, sems, lsem = bufs
    rs = HL * B // nz
    y, z = place(nz)
    own = y * nz + z
    hz = z * rs // B
    for d in range(1, NY):
        yy = lax.rem(y + d, NY)
        wait_recv(tbuf.at[yy], sems.at[3, yy], own, head)
        wait_send(tsrc, sems.at[2, yy], own, head)
    carry = jnp.zeros((rs, B), F32)
    for lap in range(NY):
        r = NY - 1 - lap if reverse else lap
        use = (r > y) if reverse else (r < y)
        span = jnp.zeros((1, B), F32)
        for m in range(nz):
            span = span + fin[r, m, pl.ds(hz, 1), :]
        carry = jnp.where(use, carry * jnp.exp(span) + tbuf[r], carry)
    for lap in range(nz):
        m = nz - 1 - lap if reverse else lap
        sbuf[m] = (ebuf[m] + carry).astype(BF16)
        carry = carry * jnp.exp(fin[y, m, pl.ds(hz, 1), :])
    for d in range(1, nz):
        zz = lax.rem(z + d, nz)
        start_remote(
            sbuf.at[zz], out.at[pl.ds(z * rs, rs)], sems.at[4, zz], sems.at[5, z], y * nz + zz, head
        )
    pltpu.make_async_copy(sbuf.at[z], out.at[pl.ds(z * rs, rs)], lsem.at[1]).start()


def scan_finish(nz, head, out, bufs):
    sbuf, sems, lsem = bufs[4], bufs[5], bufs[6]
    rs = HL * B // nz
    y, z = place(nz)
    own = y * nz + z
    for d in range(1, nz):
        zz = lax.rem(z + d, nz)
        wait_recv(out.at[pl.ds(zz * rs, rs)], sems.at[5, zz], own, head)
        wait_send(sbuf.at[zz], sems.at[4, zz], own, head)
    pltpu.make_async_copy(sbuf.at[z], out.at[pl.ds(z * rs, rs)], lsem.at[1]).wait()


def small_start(nz, head, src, dst, sems):
    y, z = place(nz)
    for d in range(1, nz):
        zz = lax.rem(z + d, nz)
        start_remote(src, dst.at[y, z], sems.at[0, zz], sems.at[1, z], y * nz + zz, head)
    pltpu.make_async_copy(src, dst.at[y, z], sems.at[2, 0]).start()


def small_rows(nz, head, src, dst, sems):
    y, z = place(nz)
    own = y * nz + z
    for d in range(1, nz):
        zz = lax.rem(z + d, nz)
        wait_recv(dst.at[y, zz], sems.at[1, zz], own, head)
    pltpu.make_async_copy(src, dst.at[y, z], sems.at[2, 0]).wait()
    for d in range(1, NY):
        yy = lax.rem(y + d, NY)
        start_remote(dst.at[y], dst.at[y], sems.at[3, yy], sems.at[4, y], yy * nz + z, head)


def small_finish(nz, head, src, dst, sems):
    y, z = place(nz)
    own = y * nz + z
    for d in range(1, NY):
        yy = lax.rem(y + d, NY)
        wait_recv(dst.at[yy], sems.at[4, yy], own, head)


def small_drain(nz, head, src, dst, sems):
    y, z = place(nz)
    own = y * nz + z
    for d in range(1, nz):
        zz = lax.rem(z + d, nz)
        wait_send(src, sems.at[0, zz], own, head)
    for d in range(1, NY):
        yy = lax.rem(y + d, NY)
        wait_send(dst.at[y], sems.at[3, yy], own, head)


def greet(nz, head, nh):
    y, z = place(nz)
    barrier = pltpu.get_barrier_semaphore()
    for d in range(1, nz):
        pl.semaphore_signal(
            barrier, inc=1, device_id=(y * nz + lax.rem(z + d, nz), head), device_id_type=MESH
        )
    for d in range(1, NY):
        pl.semaphore_signal(
            barrier, inc=1, device_id=(lax.rem(y + d, NY) * nz + z, head), device_id_type=MESH
        )
    for d in range(1, nh):
        pl.semaphore_signal(
            barrier, inc=1, device_id=(y * nz + z, lax.rem(head + d, nh)), device_id_type=MESH
        )
    pl.semaphore_wait(barrier, nz - 1 + NY - 1 + nh - 1)


def exchange_kernel(
    nz, own, state, fin_own, pairs, state_in, fin, ring_s, ring_r, bun_s, bun_r, up_s, dn_s, col_r, rel_s, fsem, *bufs
):
    head = lax.axis_index("head")
    y, z = place(nz)
    me = y * nz + z
    right, left = y * nz + lax.rem(z + 1, nz), y * nz + lax.rem(z + nz - 1, nz)
    above, below = lax.rem(y + 1, NY) * nz + z, lax.rem(y + NY - 1, NY) * nz + z
    part_up = jnp.where(y < NY - 1, 0, 1)
    part_dn = jnp.where(y > 0, 1, 0)
    inner = (y == 1) | (y == 2)
    greet(nz, head, 1)
    small_start(nz, head, fin_own, fin, fsem)
    scan_start(nz, head, state, bufs)

    def ring_own(h, to):
        start_remote(own.at[h], pairs.at[z, h, pl.ds(3, 2)], ring_s.at[z, h], ring_r.at[z, h], to, head)

    def ring_on(zz, h, to):
        ref = pairs.at[zz, h, pl.ds(3, 2)]
        start_remote(ref, ref, ring_s.at[zz, h], ring_r.at[zz, h], to, head)

    def ring_wait(zz, h):
        wait_recv(pairs.at[zz, h, pl.ds(3, 2)], ring_r.at[zz, h], me, head)

    def bundle_on(zz, h, to):
        ref = pairs.at[zz, h, pl.ds(0, 3)]
        start_remote(ref, ref, bun_s.at[zz, h - 2], bun_r.at[zz, h - 2], to, head)

    def bundle_wait(zz, h):
        wait_recv(pairs.at[zz, h, pl.ds(0, 3)], bun_r.at[zz, h - 2], me, head)

    def column_own(h):
        start_remote(own.at[h, part_up], pairs.at[z, h, 0], up_s.at[z, h], col_r.at[z, h, 0], above, head)
        start_remote(own.at[h, part_dn], pairs.at[z, h, 1], dn_s.at[z, h], col_r.at[z, h, 1], below, head)

    def column_on(zz, h):
        start_remote(
            pairs.at[zz, h, 3 + part_up], pairs.at[zz, h, 0], up_s.at[zz, h], col_r.at[zz, h, 0], above, head
        )
        start_remote(
            pairs.at[zz, h, 3 + part_dn], pairs.at[zz, h, 1], dn_s.at[zz, h], col_r.at[zz, h, 1], below, head
        )

    def relay(zz, h):
        wait_recv(pairs.at[zz, h, 0], col_r.at[zz, h, 0], me, head)
        wait_recv(pairs.at[zz, h, 1], col_r.at[zz, h, 1], me, head)

        @pl.when(inner)
        def _():
            start_remote(
                pairs.at[zz, h, 0], pairs.at[zz, h, 2], rel_s.at[zz, h, 0], col_r.at[zz, h, 2], above, head
            )
            start_remote(
                pairs.at[zz, h, 1], pairs.at[zz, h, 2], rel_s.at[zz, h, 1], col_r.at[zz, h, 2], below, head
            )

    def opposite_wait(zz, h):
        wait_recv(pairs.at[zz, h, 2], col_r.at[zz, h, 2], me, head)

    ring_own(0, right)
    ring_own(1, left)
    column_own(2)
    column_own(3)
    ring_own(2, right)
    ring_own(3, left)
    column_own(0)
    column_own(1)
    relay(z, 2)
    relay(z, 3)
    opposite_wait(z, 2)
    bundle_on(z, 2, right)
    opposite_wait(z, 3)
    bundle_on(z, 3, left)

    def lap(s, last):
        zr, zl = lax.rem(z + nz - s, nz), lax.rem(z + s, nz)
        pr, pml = lax.rem(z + nz - s + 1, nz), lax.rem(z + s - 1, nz)
        for h, zz, to in ((0, zr, right), (1, zl, left)):
            ring_wait(zz, h)
            if not last:
                ring_on(zz, h, to)
            column_on(zz, h)
        for h, zz, to in ((2, zr, right), (3, zl, left)):
            ring_wait(zz, h)
            if not last:
                ring_on(zz, h, to)
        for h, zz in ((0, pr), (1, pml)):
            relay(zz, h)
        for h, zz, to in ((2, zr, right), (3, zl, left)):
            bundle_wait(zz, h)
            if not last:
                bundle_on(zz, h, to)

    lap(1, False)
    small_rows(nz, head, fin_own, fin, fsem)
    scan_rows(nz, head, state, fin, bufs, False)
    lap(2, False)
    small_finish(nz, head, fin_own, fin, fsem)
    scan_spread(nz, head, fin, state_in, bufs, False)

    @pl.loop(3, nz - 1)
    def _(s):
        lap(s, False)

    lap(nz - 1, True)
    for h, zz in ((0, lax.rem(z + 1, nz)), (1, lax.rem(z + nz - 1, nz))):
        relay(zz, h)
    scan_finish(nz, head, state_in, bufs)
    small_drain(nz, head, fin_own, fin, fsem)

    @pl.loop(0, nz)
    def _(zz):
        for h in range(2):
            opposite_wait(zz, h)
            wait_send(pairs.at[zz, h, 0], up_s.at[zz, h], me, head)
            wait_send(pairs.at[zz, h, 1], dn_s.at[zz, h], me, head)

            @pl.when(inner)
            def _():
                wait_send(pairs.at[zz, h, 0], rel_s.at[zz, h, 0], me, head)
                wait_send(pairs.at[zz, h, 1], rel_s.at[zz, h, 1], me, head)

    for h in range(2, HL):
        wait_send(pairs.at[z, h, 0], up_s.at[z, h], me, head)
        wait_send(pairs.at[z, h, 1], dn_s.at[z, h], me, head)

        @pl.when(inner)
        def _():
            wait_send(pairs.at[z, h, 0], rel_s.at[z, h, 0], me, head)
            wait_send(pairs.at[z, h, 1], rel_s.at[z, h, 1], me, head)

    @pl.loop(0, nz - 1)
    def _(s):
        for h in range(HL):
            zz = lax.rem(z + nz - s, nz) if h % 2 == 0 else lax.rem(z + s, nz)
            wait_send(pairs.at[zz, h, pl.ds(3, 2)], ring_s.at[zz, h], me, head)
            if h >= 2:
                wait_send(pairs.at[zz, h, pl.ds(0, 3)], bun_s.at[zz, h - 2], me, head)


def exchange(nz, own, state, fin):
    full = pl.BlockSpec(memory_space=pltpu.VMEM)
    hbm = pl.BlockSpec(memory_space=pl.ANY)
    sem = pltpu.SemaphoreType.DMA
    return pl.pallas_call(
        functools.partial(exchange_kernel, nz),
        out_shape=(
            jax.ShapeDtypeStruct((nz, HL, 5, 2, B, B), BF16),
            jax.ShapeDtypeStruct((HL * B, B), BF16),
            jax.ShapeDtypeStruct((NY, nz, 2 * HL, B), F32),
        ),
        in_specs=[hbm, full, full],
        out_specs=(hbm, full, full),
        scratch_shapes=[
            sem((nz, HL)),
            sem((nz, HL)),
            sem((nz, 2)),
            sem((nz, 2)),
            sem((nz, HL)),
            sem((nz, HL)),
            sem((nz, HL, 3)),
            sem((nz, HL, 2)),
            sem((5, max(nz, NY))),
        ]
        + scan_scratch(nz),
        compiler_params=pltpu.CompilerParams(collective_id=0, has_side_effects=True),
    )(own.reshape(HL, 2, 2, B, B), state, fin)


def query_kernel(
    nz, lists, count, own, pairs, lin, dec, state_in, dq_out, stats, lo_out, sq_out, sc, dpc, mx, ls, acc, tmp
):
    y, z = place(nz)
    n = count[0]
    causal = iota(0) >= iota(1)
    for h in range(HL):
        s = jnp.where(causal, mm_t(own[h, 1, 0], own[h, 0, 0]) * SCALE, NEG)
        sc[NSEL, h] = s
        mx[h] = s

    def where_is(e):
        j = lists[0, e]
        r, zz = j // nz, lax.rem(j, nz)
        return zz, jnp.where(r == y, 3, slot_of(r, y))

    def scores(e, _):
        zz, slot = where_is(e)
        for h in range(HL):
            s = mm_t(own[h, 1, 0], pairs[zz, h, slot, 0]) * SCALE
            sc[e, h] = s
            mx[h] = jnp.maximum(mx[h], s)
        return 0

    lax.fori_loop(0, n, scores, 0)
    for h in range(HL):
        m = jnp.broadcast_to(jnp.max(mx[h], axis=1, keepdims=True), (B, B))
        mx[h] = m
        p = jnp.exp(sc[NSEL, h] - m)
        sc[NSEL, h] = p
        ls[h] = p
        acc[h] = mm(p.astype(BF16), own[h, 0, 1])
        dpc[NSEL, h] = mm_t(own[h, 1, 1], own[h, 0, 1])

    def values(e, _):
        zz, slot = where_is(e)
        for h in range(HL):
            p = jnp.exp(sc[e, h] - mx[h])
            sc[e, h] = p
            ls[h] = ls[h] + p
            v = pairs[zz, h, slot, 1]
            acc[h] = acc[h] + mm(p.astype(BF16), v)
            dpc[e, h] = mm_t(own[h, 1, 1], v)
        return 0

    lax.fori_loop(0, n, values, 0)
    stats[...] = jnp.zeros_like(stats)
    lane = lax.broadcasted_iota(jnp.int32, (1, B), 1)

    def mark(e, row):
        return jnp.where(lane == lists[0, e], 1.0, row)

    stats[2 * HL : 2 * HL + 1, :] = lax.fori_loop(0, n, mark, jnp.zeros((1, B), F32))
    inv = []
    for h in range(HL):
        total = jnp.sum(ls[h], axis=1, keepdims=True)
        inv.append(1.0 / total)
        out = acc[h] * inv[h]
        delta = jnp.sum(own[h, 1, 1].astype(F32) * out, axis=1, keepdims=True)
        stats[h : h + 1, :] = row_of(mx[h][:, 0:1] + jnp.log(total))
        stats[HL + h : HL + h + 1, :] = row_of(delta)
        delta = jnp.broadcast_to(delta, (B, B))
        mx[h] = delta
        ds = (sc[NSEL, h] * (dpc[NSEL, h] - delta)).astype(BF16)
        acc[h] = mm(ds, own[h, 0, 0])

    def back(e, _):
        zz, slot = where_is(e)
        for h in range(HL):
            ds = (sc[e, h] * (dpc[e, h] - mx[h])).astype(BF16)
            acc[h] = acc[h] + mm(ds, pairs[zz, h, slot, 0])
        return 0

    lax.fori_loop(0, n, back, 0)
    for h in range(HL):
        tmp[pl.ds(h, B, stride=HL), :] = acc[h] * (inv[h] * SCALE)
    dq_out[...] = tmp[...].astype(BF16)

    run = running_of(dec[...])
    squares = jnp.zeros((B, 1), F32)
    for h in range(HL):
        row = run[h : h + 1]
        col = col_of(row)
        w = (mm_t(lin[h, 0], lin[h, 1]) * within_of(row, col)).astype(BF16)
        lo = mm(w, lin[h, 2]) + jnp.exp(col) * mm(lin[h, 0], state_in[pl.ds(h * B, B), :])
        lo_out[h] = lo
        squares = squares + jnp.sum(lo * lo, axis=1, keepdims=True)
    sq_out[...] = jnp.broadcast_to(row_of(squares), (8, B))


def queries(nz, lists, count, own, pairs, lin, dec, state_in):
    full = pl.BlockSpec(memory_space=pltpu.VMEM)
    smem = pl.BlockSpec(memory_space=pltpu.SMEM)
    return pl.pallas_call(
        functools.partial(query_kernel, nz),
        out_shape=(
            jax.ShapeDtypeStruct((HL * B, B), BF16),
            jax.ShapeDtypeStruct((16, B), F32),
            jax.ShapeDtypeStruct((HL, B, B), F32),
            jax.ShapeDtypeStruct((8, B), F32),
        ),
        in_specs=[smem, smem] + [full] * 5,
        out_specs=(full,) * 4,
        scratch_shapes=[
            pltpu.VMEM((NSEL + 1, HL, B, B), F32),
            pltpu.VMEM((NSEL + 1, HL, B, B), F32),
            pltpu.VMEM((HL, B, B), F32),
            pltpu.VMEM((HL, B, B), F32),
            pltpu.VMEM((HL, B, B), F32),
            pltpu.VMEM((HL * B, B), F32),
        ],
        compiler_params=pltpu.CompilerParams(vmem_limit_bytes=56 << 20),
    )(lists, count, own.reshape(HL, 2, 2, B, B), pairs, lin, dec, state_in)


def tail_kernel(
    nz,
    nh,
    own,
    pairs,
    lin,
    dec,
    fin,
    gain,
    stats_own,
    lo_in,
    sq_in,
    dk_out,
    dv_out,
    cot_out,
    rev_out,
    stats,
    dk,
    dv,
    cot,
    local,
    hbuf,
    isrc,
    hsem,
    ssem,
    *bufs,
):
    head = lax.axis_index("head")
    y, z = place(nz)
    me = y * nz + z
    greet(nz, head, nh)
    small_start(nz, head, stats_own, stats, ssem)

    def heads_start(k, src):
        for d in range(1, nh):
            hh = lax.rem(head + d, nh)
            start_remote(src, hbuf.at[k, head], hsem.at[2 * k, hh], hsem.at[2 * k + 1, head], me, hh)

    def heads_total(k, src):
        total = src[...]
        for d in range(1, nh):
            hh = lax.rem(head + d, nh)
            wait_recv(hbuf.at[k, hh], hsem.at[2 * k + 1, hh], me, head)
            total = total + hbuf[k, hh]
            wait_send(src, hsem.at[2 * k, hh], me, head)
        return total[0:1]

    heads_start(0, sq_in)
    for h in range(HL):
        keep = iota(0) <= iota(1)
        s = mm_t(own[h, 0, 0], own[h, 1, 0]) * SCALE
        p = jnp.where(keep, jnp.exp(jnp.where(keep, s - stats_own[h : h + 1, :], 0.0)), 0.0)
        dv[h] = mm(p.astype(BF16), own[h, 1, 1])
        dp = mm_t(own[h, 0, 1], own[h, 1, 1])
        ds = (p * (dp - stats_own[HL + h : HL + h + 1, :])).astype(BF16)
        dk[h] = mm(ds, own[h, 1, 0])

    lane = lax.broadcasted_iota(jnp.int32, (1, B), 1)

    def one(i, slot):
        r, zz = i // nz, lax.rem(i, nz)
        here = jnp.sum(jnp.where(lane == me, stats[r, zz, 2 * HL : 2 * HL + 1, :], 0.0), axis=1, keepdims=True)
        for h in range(HL):
            lse = jnp.where(here > 0.5, stats[r, zz, h : h + 1, :], BIG)
            q, g = pairs[zz, h, slot, 0], pairs[zz, h, slot, 1]
            s = mm_t(own[h, 0, 0], q) * SCALE
            p = jnp.exp(s - lse)
            dv[h] = dv[h] + mm(p.astype(BF16), g)
            dp = mm_t(own[h, 0, 1], g)
            ds = (p * (dp - stats[r, zz, HL + h : HL + h + 1, :])).astype(BF16)
            dk[h] = dk[h] + mm(ds, q)

    small_rows(nz, head, stats_own, stats, ssem)

    @pl.loop(me + 1, (y + 1) * nz)
    def _(i):
        one(i, 4)

    small_finish(nz, head, stats_own, stats, ssem)

    @pl.loop((y + 1) * nz, NY * nz)
    def _(i):
        one(i, slot_of(i // nz, y))

    partial = jnp.zeros((B, 1), F32)
    for h in range(HL):
        dk_out[h] = (dk[h] * SCALE).astype(BF16)
        dv_out[h] = dv[h].astype(BF16)
        c = (dv[h] + own[h, 1, 1].astype(F32)) * gain[h : h + 1, :]
        cot[h] = c
        partial = partial + jnp.sum(c * lo_in[h], axis=1, keepdims=True)
    isrc[...] = jnp.broadcast_to(row_of(partial), (8, B))
    heads_start(1, isrc)
    width = HL * nh * B
    root = jnp.sqrt(heads_total(0, sq_in) / width + EPS)
    inner = heads_total(1, isrc)
    factor = col_of(inner / (width * root * root * root))
    inv = col_of(1.0 / root)
    run = running_of(dec[...])
    leading = jnp.exp(run)
    for h in range(HL):
        lc = (cot[h] * inv - lo_in[h] * factor).astype(BF16)
        cot_out[h] = lc
        q = (lin[h, 0].astype(F32) * col_of(leading[h : h + 1])).astype(BF16)
        local[pl.ds(h * B, B), :] = t_mm(q, lc).astype(BF16)
    scan_start(nz, head, local, bufs)
    scan_rows(nz, head, local, fin, bufs, True)
    scan_spread(nz, head, fin, rev_out, bufs, True)
    scan_finish(nz, head, rev_out, bufs)
    small_drain(nz, head, stats_own, stats, ssem)


def tail(nz, nh, own, pairs, lin, dec, fin, gain, stats, lo, sq):
    full = pl.BlockSpec(memory_space=pltpu.VMEM)
    sem = pltpu.SemaphoreType.DMA
    return pl.pallas_call(
        functools.partial(tail_kernel, nz, nh),
        out_shape=(
            jax.ShapeDtypeStruct((HL, B, B), BF16),
            jax.ShapeDtypeStruct((HL, B, B), BF16),
            jax.ShapeDtypeStruct((HL, B, B), BF16),
            jax.ShapeDtypeStruct((HL * B, B), BF16),
        ),
        in_specs=[full] * 9,
        out_specs=(full,) * 4,
        scratch_shapes=[
            pltpu.VMEM((NY, nz, 16, B), F32),
            pltpu.VMEM((HL, B, B), F32),
            pltpu.VMEM((HL, B, B), F32),
            pltpu.VMEM((HL, B, B), F32),
            pltpu.VMEM((HL * B, B), BF16),
            pltpu.VMEM((2, nh, 8, B), F32),
            pltpu.VMEM((8, B), F32),
            sem((4, nh)),
            sem((5, max(nz, NY))),
        ]
        + scan_scratch(nz),
        compiler_params=pltpu.CompilerParams(
            collective_id=1, has_side_effects=True, vmem_limit_bytes=56 << 20
        ),
    )(own.reshape(HL, 2, 2, B, B), pairs, lin, dec, fin, gain, stats, lo, sq)


def last_kernel(lin, dec, state_in, cot, rev, dk_in, dv_in, dq_o, dk_o, dv_o, sk_o, sv_o, tmp):
    run = running_of(dec[...])
    trail = jnp.exp(run[:, B - 1 : B] - run)
    keep = iota(0) <= iota(1)

    def put(ref, value):
        for h in range(HL):
            tmp[pl.ds(h, B, stride=HL), :] = value(h)
        ref[...] = tmp[...].astype(BF16)

    def dq(h):
        row = run[h : h + 1]
        col = col_of(row)
        pair = (mm_t(cot[h], lin[h, 2]) * within_of(row, col)).astype(BF16)
        return mm(pair, lin[h, 1]) + jnp.exp(col) * mm_t(cot[h], state_in[pl.ds(h * B, B), :])

    def within_t(h):
        row = run[h : h + 1]
        return jnp.where(keep, jnp.exp(jnp.where(keep, row - col_of(row), 0.0)), 0.0)

    def dk(h):
        pair = (mm_t(lin[h, 2], cot[h]) * within_t(h)).astype(BF16)
        return mm(pair, lin[h, 0]) + col_of(trail[h : h + 1]) * mm_t(lin[h, 2], rev[pl.ds(h * B, B), :])

    def dv(h):
        pair = (mm_t(lin[h, 1], lin[h, 0]) * within_t(h)).astype(BF16)
        return mm(pair, cot[h]) + col_of(trail[h : h + 1]) * mm(lin[h, 1], rev[pl.ds(h * B, B), :])

    put(dq_o, dq)
    put(dk_o, dk)
    put(dv_o, dv)
    put(sk_o, lambda h: dk_in[h].astype(F32))
    put(sv_o, lambda h: dv_in[h].astype(F32))


def last(lin, dec, state_in, cot, rev, dk, dv):
    full = pl.BlockSpec(memory_space=pltpu.VMEM)
    return pl.pallas_call(
        last_kernel,
        out_shape=(jax.ShapeDtypeStruct((HL * B, B), BF16),) * 5,
        in_specs=[full] * 7,
        out_specs=(full,) * 5,
        scratch_shapes=[pltpu.VMEM((HL * B, B), F32)],
    )(lin, dec, state_in, cot, rev, dk, dv)


def local(nz, nh, lin_q, lin_k, lin_v, decay, gain, soft_q, soft_k, soft_v, out_grad, lists, counts):
    flat = [a.reshape(B * HL, B) for a in (lin_q, lin_k, lin_v, soft_q, soft_k, soft_v, out_grad)]
    own, lin, state, fin_own = prep(flat, decay)
    pairs, state_in, fin = exchange(nz, own, state, fin_own)
    dq, stats, lo, sq = queries(nz, lists, counts, own, pairs, lin, decay, state_in)
    dk, dv, cot, rev = tail(nz, nh, own, pairs, lin, decay, fin, gain, stats, lo, sq)
    lin_dq, lin_dk, lin_dv, soft_dk, soft_dv = last(lin, decay, state_in, cot, rev, dk, dv)
    return tuple(a.reshape(B, HL, B) for a in (lin_dq, lin_dk, lin_dv, dq, soft_dk, soft_dv))


def solution(mesh):
    nz = mesh.shape["ctx"] // NY
    tokens = P("ctx", "head", None)
    in_specs = (
        (tokens,) * 3 + (P("head", "ctx"), P("head", None)) + (tokens,) * 4 + (P("ctx", None), P("ctx"))
    )
    return jax.shard_map(
        functools.partial(local, nz, mesh.shape["head"]),
        mesh=mesh,
        in_specs=in_specs,
        out_specs=(tokens,) * 6,
        check_vma=False,
    )
```

```python
import functools

import jax
import jax.numpy as jnp
from jax import lax
from jax.experimental import pallas as pl
from jax.experimental.pallas import tpu as pltpu
from jax.sharding import PartitionSpec as P

NY = 4
HL = 4
B = 128
NSEL = 16
EPS = 1e-05
SCALE = 128 ** (-0.5)
NEG = -1e30
BIG = 1e30
F32 = jnp.float32
BF16 = jnp.bfloat16
MESH = pl.DeviceIdType.MESH
HIGH = lax.Precision.HIGHEST


def mm(a, b):
    return lax.dot_general(a, b, (((1,), (0,)), ((), ())), preferred_element_type=F32)


def mm_t(a, b):
    return lax.dot_general(a, b, (((1,), (1,)), ((), ())), preferred_element_type=F32)


def t_mm(a, b):
    return lax.dot_general(a, b, (((0,), (0,)), ((), ())), preferred_element_type=F32)


def iota(dim):
    return lax.broadcasted_iota(jnp.int32, (B, B), dim)


def col_of(row):
    return jnp.transpose(jnp.broadcast_to(row, (B, B)))


def row_of(col):
    return jnp.transpose(jnp.broadcast_to(col, (B, B)))[0:1]


def running_of(decay):
    upper = (iota(0) <= iota(1)).astype(F32)
    return lax.dot_general(
        decay, upper, (((1,), (0,)), ((), ())), precision=HIGH, preferred_element_type=F32
    )


def within_of(row, col):
    keep = iota(0) >= iota(1)
    return jnp.where(keep, jnp.exp(jnp.where(keep, col - row, 0.0)), 0.0)


def slot_of(r, y):
    return jnp.where(lax.rem(y + 3, NY) == r, 0, jnp.where(lax.rem(y + 1, NY) == r, 1, 2))


def place(nz):
    own = lax.axis_index("ctx")
    return own // nz, lax.rem(own, nz)


def start_remote(src, dst, send, recv, ctx, head):
    pltpu.make_async_remote_copy(
        src_ref=src, dst_ref=dst, send_sem=send, recv_sem=recv, device_id=(ctx, head), device_id_type=MESH
    ).start()


def wait_recv(ref, recv, ctx, head):
    pltpu.make_async_remote_copy(
        src_ref=ref, dst_ref=ref, send_sem=recv, recv_sem=recv, device_id=(ctx, head), device_id_type=MESH
    ).wait_recv()


def wait_send(ref, send, ctx, head):
    pltpu.make_async_remote_copy(
        src_ref=ref, dst_ref=ref, send_sem=send, recv_sem=send, device_id=(ctx, head), device_id_type=MESH
    ).wait_send()


def prep_kernel(nz, lists, count, lq, lk, lv, sq, sk, sv, og, dec, own, lin, state, fin, bias, mask, tmp):
    def heads(ref, store):
        tmp[...] = ref[...].astype(F32)
        for h in range(HL):
            store(h, tmp[pl.ds(h, B, stride=HL), :].astype(BF16))

    def into(dst, a):
        def store(h, value):
            dst[h, a] = value

        return store

    y, _ = place(nz)
    bias[...] = jnp.full_like(bias, NEG)
    lane = lax.broadcasted_iota(jnp.int32, (8, B), 1)

    def mark(e, row):
        j = lists[0, e]
        r = j // nz
        k = jnp.where(r == y, 3, slot_of(r, y))
        bias[k, pl.ds(lax.rem(j, nz), 1), :] = jnp.zeros((1, B), F32)
        return jnp.where(lane == j, 1.0, row)

    mask[...] = lax.fori_loop(0, count[0], mark, jnp.zeros((8, B), F32))
    heads(sk, into(own, 0))
    heads(sv, into(own, 1))
    heads(sq, into(own, 2))
    heads(og, into(own, 3))
    heads(lq, into(lin, 0))
    heads(lk, into(lin, 1))
    heads(lv, into(lin, 2))
    run = running_of(dec[...])
    finish = run[:, B - 1 : B]
    fin[...] = jnp.concatenate([jnp.broadcast_to(finish, (HL, B))] * 2, axis=0)
    trailing = jnp.exp(finish - run)
    for h in range(HL):
        k = lin[h, 1].astype(F32) * col_of(trailing[h : h + 1])
        state[pl.ds(h * B, B), :] = t_mm(k.astype(BF16), lin[h, 2]).astype(BF16)


def prep(nz, lists, counts, arrays, decay):
    full = pl.BlockSpec(memory_space=pltpu.VMEM)
    smem = pl.BlockSpec(memory_space=pltpu.SMEM)
    return pl.pallas_call(
        functools.partial(prep_kernel, nz),
        out_shape=(
            jax.ShapeDtypeStruct((HL, 4, B, B), BF16),
            jax.ShapeDtypeStruct((HL, 3, B, B), BF16),
            jax.ShapeDtypeStruct((HL * B, B), BF16),
            jax.ShapeDtypeStruct((2 * HL, B), F32),
            jax.ShapeDtypeStruct((4, nz, B), F32),
            jax.ShapeDtypeStruct((8, B), F32),
        ),
        in_specs=[smem, smem] + [full] * 8,
        out_specs=(full,) * 6,
        scratch_shapes=[pltpu.VMEM((HL * B, B), F32)],
    )(lists, counts, *arrays, decay)


def scan_scratch(nz):
    rs = HL * B // nz
    return [
        pltpu.VMEM((nz, rs, B), BF16),
        pltpu.VMEM((nz, rs, B), F32),
        pltpu.VMEM((NY, rs, B), F32),
        pltpu.VMEM((rs, B), F32),
        pltpu.VMEM((nz, rs, B), BF16),
        pltpu.SemaphoreType.DMA((6, nz)),
        pltpu.SemaphoreType.DMA((2,)),
    ]


def scan_start(nz, head, local, bufs):
    zbuf, sems, lsem = bufs[0], bufs[5], bufs[6]
    rs = HL * B // nz
    y, z = place(nz)
    for d in range(1, nz):
        zz = lax.rem(z + d, nz)
        start_remote(
            local.at[pl.ds(zz * rs, rs)], zbuf.at[z], sems.at[0, zz], sems.at[1, z], y * nz + zz, head
        )
    pltpu.make_async_copy(local.at[pl.ds(z * rs, rs)], zbuf.at[z], lsem.at[0]).start()


def scan_rows(nz, head, local, fin, bufs, reverse):
    zbuf, ebuf, tbuf, tsrc, _, sems, lsem = bufs
    rs = HL * B // nz
    y, z = place(nz)
    own = y * nz + z
    hz = z * rs // B
    pltpu.make_async_copy(local.at[pl.ds(z * rs, rs)], zbuf.at[z], lsem.at[0]).wait()
    for d in range(1, nz):
        zz = lax.rem(z + d, nz)
        wait_recv(zbuf.at[zz], sems.at[1, zz], own, head)

    total = jnp.zeros((rs, B), F32)
    for lap in range(nz):
        m = nz - 1 - lap if reverse else lap
        ebuf[m] = total
        total = total * jnp.exp(fin[y, m, pl.ds(hz, 1), :]) + zbuf[m].astype(F32)
    tsrc[...] = total
    for d in range(1, NY):
        yy = lax.rem(y + d, NY)
        start_remote(tsrc, tbuf.at[y], sems.at[2, yy], sems.at[3, y], yy * nz + z, head)
    for d in range(1, nz):
        zz = lax.rem(z + d, nz)
        wait_send(zbuf.at[0], sems.at[0, zz], own, head)


def scan_spread(nz, head, fin, out, bufs, reverse):
    _, ebuf, tbuf, tsrc, sbuf, sems, lsem = bufs
    rs = HL * B // nz
    y, z = place(nz)
    own = y * nz + z
    hz = z * rs // B
    for d in range(1, NY):
        yy = lax.rem(y + d, NY)
        wait_recv(tbuf.at[yy], sems.at[3, yy], own, head)
        wait_send(tsrc, sems.at[2, yy], own, head)
    carry = jnp.zeros((rs, B), F32)
    for lap in range(NY):
        r = NY - 1 - lap if reverse else lap
        use = (r > y) if reverse else (r < y)
        span = jnp.zeros((1, B), F32)
        for m in range(nz):
            span = span + fin[r, m, pl.ds(hz, 1), :]
        carry = jnp.where(use, carry * jnp.exp(span) + tbuf[r], carry)
    for lap in range(nz):
        m = nz - 1 - lap if reverse else lap
        sbuf[m] = (ebuf[m] + carry).astype(BF16)
        carry = carry * jnp.exp(fin[y, m, pl.ds(hz, 1), :])
    for d in range(1, nz):
        zz = lax.rem(z + d, nz)
        start_remote(
            sbuf.at[zz], out.at[pl.ds(z * rs, rs)], sems.at[4, zz], sems.at[5, z], y * nz + zz, head
        )
    pltpu.make_async_copy(sbuf.at[z], out.at[pl.ds(z * rs, rs)], lsem.at[1]).start()


def scan_finish(nz, head, out, bufs):
    sbuf, sems, lsem = bufs[4], bufs[5], bufs[6]
    rs = HL * B // nz
    y, z = place(nz)
    own = y * nz + z
    for d in range(1, nz):
        zz = lax.rem(z + d, nz)
        wait_recv(out.at[pl.ds(zz * rs, rs)], sems.at[5, zz], own, head)
        wait_send(sbuf.at[zz], sems.at[4, zz], own, head)
    pltpu.make_async_copy(sbuf.at[z], out.at[pl.ds(z * rs, rs)], lsem.at[1]).wait()


def small_start(nz, head, src, dst, sems):
    y, z = place(nz)
    for d in range(1, nz):
        zz = lax.rem(z + d, nz)
        start_remote(src, dst.at[y, z], sems.at[0, zz], sems.at[1, z], y * nz + zz, head)
    pltpu.make_async_copy(src, dst.at[y, z], sems.at[2, 0]).start()


def small_rows(nz, head, src, dst, sems):
    y, z = place(nz)
    own = y * nz + z
    for d in range(1, nz):
        zz = lax.rem(z + d, nz)
        wait_recv(dst.at[y, zz], sems.at[1, zz], own, head)
    pltpu.make_async_copy(src, dst.at[y, z], sems.at[2, 0]).wait()
    for d in range(1, NY):
        yy = lax.rem(y + d, NY)
        start_remote(dst.at[y], dst.at[y], sems.at[3, yy], sems.at[4, y], yy * nz + z, head)


def small_finish(nz, head, src, dst, sems):
    y, z = place(nz)
    own = y * nz + z
    for d in range(1, NY):
        yy = lax.rem(y + d, NY)
        wait_recv(dst.at[yy], sems.at[4, yy], own, head)


def small_drain(nz, head, src, dst, sems):
    y, z = place(nz)
    own = y * nz + z
    for d in range(1, nz):
        zz = lax.rem(z + d, nz)
        wait_send(src, sems.at[0, zz], own, head)
    for d in range(1, NY):
        yy = lax.rem(y + d, NY)
        wait_send(dst.at[y], sems.at[3, yy], own, head)


def greet(nz, head, nh):
    y, z = place(nz)
    barrier = pltpu.get_barrier_semaphore()
    for d in range(1, nz):
        pl.semaphore_signal(
            barrier, inc=1, device_id=(y * nz + lax.rem(z + d, nz), head), device_id_type=MESH
        )
    for d in range(1, NY):
        pl.semaphore_signal(
            barrier, inc=1, device_id=(lax.rem(y + d, NY) * nz + z, head), device_id_type=MESH
        )
    for d in range(1, nh):
        pl.semaphore_signal(
            barrier, inc=1, device_id=(y * nz + z, lax.rem(head + d, nh)), device_id_type=MESH
        )
    pl.semaphore_wait(barrier, nz - 1 + NY - 1 + nh - 1)


def fused_kernel(
    nz,
    nh,
    own,
    lin,
    dec,
    gain,
    state,
    fin_own,
    bias,
    mask,
    dq_out,
    dk_out,
    dv_out,
    cot_out,
    rev_out,
    state_in,
    pairs,
    a1,
    a2,
    mx,
    ls,
    acc,
    dv,
    dkq,
    lcol,
    dcol,
    lo,
    cot,
    rev_local,
    fin,
    stats_own,
    stats,
    hbuf,
    hsrc,
    ring_s,
    ring_r,
    bun_s,
    bun_r,
    up_s,
    dn_s,
    col_r,
    rel_s,
    fsem,
    ssem,
    hsem,
    *scans,
):
    fwd, bwd = scans[: len(scans) // 2], scans[len(scans) // 2 :]
    head = lax.axis_index("head")
    y, z = place(nz)
    me = y * nz + z
    right, left = y * nz + lax.rem(z + 1, nz), y * nz + lax.rem(z + nz - 1, nz)
    above, below = lax.rem(y + 1, NY) * nz + z, lax.rem(y + NY - 1, NY) * nz + z
    part_up = jnp.where(y < NY - 1, 0, 1)
    part_dn = jnp.where(y > 0, 1, 0)
    inner_row = (y == 1) | (y == 2)
    greet(nz, head, nh)
    small_start(nz, head, fin_own, fin, fsem)
    scan_start(nz, head, state, fwd)

    def ring_own(h, to):
        start_remote(own.at[h], pairs.at[z, h, pl.ds(3, 2)], ring_s.at[z, h], ring_r.at[z, h], to, head)

    def ring_on(zz, h, to):
        ref = pairs.at[zz, h, pl.ds(3, 2)]
        start_remote(ref, ref, ring_s.at[zz, h], ring_r.at[zz, h], to, head)

    def ring_wait(zz, h):
        wait_recv(pairs.at[zz, h, pl.ds(3, 2)], ring_r.at[zz, h], me, head)

    def bundle_on(zz, h, to):
        ref = pairs.at[zz, h, pl.ds(0, 3)]
        start_remote(ref, ref, bun_s.at[zz, h - 2], bun_r.at[zz, h - 2], to, head)

    def bundle_wait(zz, h):
        wait_recv(pairs.at[zz, h, pl.ds(0, 3)], bun_r.at[zz, h - 2], me, head)

    def column_own(h):
        start_remote(own.at[h, part_up], pairs.at[z, h, 0], up_s.at[z, h], col_r.at[z, h, 0], above, head)
        start_remote(own.at[h, part_dn], pairs.at[z, h, 1], dn_s.at[z, h], col_r.at[z, h, 1], below, head)

    def column_on(zz, h):
        start_remote(
            pairs.at[zz, h, 3 + part_up], pairs.at[zz, h, 0], up_s.at[zz, h], col_r.at[zz, h, 0], above, head
        )
        start_remote(
            pairs.at[zz, h, 3 + part_dn], pairs.at[zz, h, 1], dn_s.at[zz, h], col_r.at[zz, h, 1], below, head
        )

    def relay(zz, h):
        wait_recv(pairs.at[zz, h, 0], col_r.at[zz, h, 0], me, head)
        wait_recv(pairs.at[zz, h, 1], col_r.at[zz, h, 1], me, head)

        @pl.when(inner_row)
        def _():
            start_remote(
                pairs.at[zz, h, 0], pairs.at[zz, h, 2], rel_s.at[zz, h, 0], col_r.at[zz, h, 2], above, head
            )
            start_remote(
                pairs.at[zz, h, 1], pairs.at[zz, h, 2], rel_s.at[zz, h, 1], col_r.at[zz, h, 2], below, head
            )

    def opposite_wait(zz, h):
        wait_recv(pairs.at[zz, h, 2], col_r.at[zz, h, 2], me, head)

    def diagonal(h):
        s = jnp.where(iota(0) >= iota(1), mm_t(own[h, 1, 0], own[h, 0, 0]) * SCALE, NEG)
        m = jnp.broadcast_to(jnp.max(s, axis=1, keepdims=True), (B, B))
        p = jnp.exp(s - m)
        mx[h] = m
        ls[h] = p
        acc[h] = mm(p.astype(BF16), own[h, 0, 1])

    def block(zz, h, with_row):
        scores, values = [], []
        for k, off in ((0, NY - 1), (1, 1), (2, 2)):
            t = jnp.where(lax.rem(y + off, NY) < y, 1, 0)
            v = pairs[zz, h, k, 1]
            s = mm_t(own[h, t, 0], pairs[zz, h, k, 0]) * SCALE
            a1[zz, h, k] = s
            a2[zz, h, k] = mm_t(own[h, t, 1], v)
            scores.append(s + bias[k, pl.ds(zz, 1), :])
            values.append(v)
        if with_row:
            t = jnp.where(zz < z, 1, 0)
            v = pairs[zz, h, 4 - t, 1]
            s = mm_t(own[h, t, 0], pairs[zz, h, 4 - t, 0]) * SCALE
            a1[zz, h, 3] = s
            a2[zz, h, 3] = mm_t(own[h, t, 1], v)
            scores.append(s + bias[3, pl.ds(zz, 1), :])
            values.append(v)
        top = functools.reduce(jnp.maximum, scores)
        m = jnp.maximum(mx[h], jnp.broadcast_to(jnp.max(top, axis=1, keepdims=True), (B, B)))
        scale = jnp.exp(mx[h] - m)
        probs = [jnp.exp(s - m) for s in scores]
        mx[h] = m
        ls[h] = ls[h] * scale + functools.reduce(jnp.add, probs)
        low = jnp.concatenate([p.astype(BF16) for p in probs], axis=1)
        acc[h] = acc[h] * scale + mm(low, jnp.concatenate(values, axis=0))

    ring_own(0, right)
    ring_own(1, left)
    column_own(2)
    column_own(3)
    ring_own(2, right)
    ring_own(3, left)
    column_own(0)
    column_own(1)
    for h in range(HL):
        diagonal(h)

    def at(s, h):
        return lax.rem(z + nz - s, nz) if h % 2 == 0 else lax.rem(z + s, nz)

    def to_next(h):
        return right if h % 2 == 0 else left

    def lap(s, first=False, second=False, last=False):
        for h in range(HL):
            ring_wait(at(s, h), h)
            if not last:
                ring_on(at(s, h), h, to_next(h))
            if h < 2:
                column_on(at(s, h), h)
        if first:
            relay(z, 2)
            relay(z, 3)
            for h in (2, 3):
                opposite_wait(z, h)
                bundle_on(z, h, to_next(h))
        for h in (0, 1):
            relay(at(s - 1, h), h)
        if first:
            for h in (2, 3):
                block(z, h, False)
        for h in (2, 3):
            bundle_wait(at(s, h), h)
            if not last:
                bundle_on(at(s, h), h, to_next(h))
        for h in (2, 3):
            block(at(s, h), h, True)
        if not first:
            for h in (0, 1):
                opposite_wait(at(s - 2, h), h)
            for h in (0, 1):
                block(at(s - 2, h), h, not second)

    lap(1, first=True)
    small_rows(nz, head, fin_own, fin, fsem)
    scan_rows(nz, head, state, fin, fwd, False)
    lap(2, second=True)
    small_finish(nz, head, fin_own, fin, fsem)
    scan_spread(nz, head, fin, state_in, fwd, False)

    @pl.loop(3, nz - 1)
    def _(s):
        lap(s)

    lap(nz - 1, last=True)
    for h in (0, 1):
        relay(at(nz - 1, h), h)
    for s in (nz - 2, nz - 1):
        for h in (0, 1):
            opposite_wait(at(s, h), h)
            block(at(s, h), h, True)

    stats_own[...] = jnp.zeros_like(stats_own)
    stats_own[2 * HL : 2 * HL + 1, :] = mask[0:1, :]
    for h in range(HL):
        total = jnp.sum(ls[h], axis=1, keepdims=True)
        lse = mx[h] + jnp.log(total)
        delta = jnp.sum(own[h, 1, 1].astype(F32) * acc[h], axis=1, keepdims=True) / total
        delta = jnp.broadcast_to(delta, (B, B))
        lcol[h] = lse
        dcol[h] = delta
        stats_own[h : h + 1, :] = jnp.transpose(lse)[0:1]
        stats_own[HL + h : HL + h + 1, :] = jnp.transpose(delta)[0:1]
    small_start(nz, head, stats_own, stats, ssem)

    def heads_start(k):
        for d in range(1, nh):
            hh = lax.rem(head + d, nh)
            start_remote(hsrc.at[k], hbuf.at[k, head], hsem.at[2 * k, hh], hsem.at[2 * k + 1, head], me, hh)

    def heads_total(k):
        total = hsrc[k]
        for d in range(1, nh):
            hh = lax.rem(head + d, nh)
            wait_recv(hbuf.at[k, hh], hsem.at[2 * k + 1, hh], me, head)
            total = total + hbuf[k, hh]
            wait_send(hsrc.at[k], hsem.at[2 * k, hh], me, head)
        return total[0:1]

    scan_finish(nz, head, state_in, fwd)
    run = running_of(dec[...])
    squares = jnp.zeros((B, 1), F32)
    for h in range(HL):
        row = run[h : h + 1]
        col = col_of(row)
        w = (mm_t(lin[h, 0], lin[h, 1]) * within_of(row, col)).astype(BF16)
        o = mm(w, lin[h, 2]) + jnp.exp(col) * mm(lin[h, 0], state_in[pl.ds(h * B, B), :])
        lo[h] = o
        squares = squares + jnp.sum(o * o, axis=1, keepdims=True)
    hsrc[0] = jnp.broadcast_to(row_of(squares), (8, B))
    heads_start(0)
    for h in range(HL):
        keep = iota(0) <= iota(1)
        s = mm_t(own[h, 0, 0], own[h, 1, 0]) * SCALE
        p = jnp.where(keep, jnp.exp(jnp.where(keep, s - stats_own[h : h + 1, :], 0.0)), 0.0)
        dv[h] = mm(p.astype(BF16), own[h, 1, 1])
        dp = mm_t(own[h, 0, 1], own[h, 1, 1])
        ds = (p * (dp - stats_own[HL + h : HL + h + 1, :])).astype(BF16)
        dkq[0, h] = mm(ds, own[h, 1, 0])

    lane = lax.broadcasted_iota(jnp.int32, (1, B), 1)

    def value_block(i, k, slot):
        r, zz = i // nz, lax.rem(i, nz)
        here = jnp.sum(jnp.where(lane == me, stats[r, zz, 2 * HL : 2 * HL + 1, :], 0.0), axis=1, keepdims=True)
        for h in range(HL):
            lse = jnp.where(here > 0.5, stats[r, zz, h : h + 1, :], BIG)
            p = jnp.exp(a1[zz, h, k] - lse)
            a1[zz, h, k] = p
            dv[h] = dv[h] + mm(p.astype(BF16), pairs[zz, h, slot, 1])

    small_rows(nz, head, stats_own, stats, ssem)

    @pl.loop(me + 1, (y + 1) * nz)
    def _(i):
        value_block(i, 3, 4)

    small_finish(nz, head, stats_own, stats, ssem)

    @pl.loop((y + 1) * nz, NY * nz)
    def _(i):
        k = slot_of(i // nz, y)
        value_block(i, k, k)

    partial = jnp.zeros((B, 1), F32)
    for h in range(HL):
        dv_out[h] = dv[h].astype(BF16)
        c = (dv[h] + own[h, 1, 1].astype(F32)) * gain[h : h + 1, :]
        cot[h] = c
        partial = partial + jnp.sum(c * lo[h], axis=1, keepdims=True)
    hsrc[1] = jnp.broadcast_to(row_of(partial), (8, B))
    heads_start(1)
    width = HL * nh * B
    root = jnp.sqrt(heads_total(0) / width + EPS)

    for h in range(HL):
        s = jnp.where(iota(0) >= iota(1), mm_t(own[h, 1, 0], own[h, 0, 0]) * SCALE, NEG)
        p = jnp.exp(s - lcol[h])
        ds = (p * (mm_t(own[h, 1, 1], own[h, 0, 1]) - dcol[h])).astype(BF16)
        dkq[1, h] = mm(ds, own[h, 0, 0])

    def grads(lo_i, hi_i):
        @pl.loop(lo_i, jnp.minimum(hi_i, me))
        def _(i):
            r, zz = i // nz, lax.rem(i, nz)
            k = jnp.where(r == y, 3, slot_of(r, y))
            for h in range(HL):
                p = jnp.exp(a1[zz, h, k] + bias[k, pl.ds(zz, 1), :] - lcol[h])
                ds = (p * (a2[zz, h, k] - dcol[h])).astype(BF16)
                dkq[1, h] = dkq[1, h] + mm(ds, pairs[zz, h, k, 0])

        @pl.loop(jnp.maximum(lo_i, me + 1), hi_i)
        def _(i):
            r, zz = i // nz, lax.rem(i, nz)
            k = jnp.where(r == y, 3, slot_of(r, y))
            slot = jnp.where(r == y, 4, k)
            for h in range(HL):
                ds = (a1[zz, h, k] * (a2[zz, h, k] - stats[r, zz, HL + h : HL + h + 1, :])).astype(BF16)
                dkq[0, h] = dkq[0, h] + mm(ds, pairs[zz, h, slot, 0])

    inner = heads_total(1)
    factor = col_of(inner / (width * root * root * root))
    inv = col_of(1.0 / root)
    leading = jnp.exp(run)
    for h in range(HL):
        lc = (cot[h] * inv - lo[h] * factor).astype(BF16)
        cot_out[h] = lc
        q = (lin[h, 0].astype(F32) * col_of(leading[h : h + 1])).astype(BF16)
        rev_local[pl.ds(h * B, B), :] = t_mm(q, lc).astype(BF16)
    scan_start(nz, head, rev_local, bwd)
    n = NY * nz
    grads(0, n * 3 // 8)
    scan_rows(nz, head, rev_local, fin, bwd, True)
    grads(n * 3 // 8, n * 5 // 8)
    scan_spread(nz, head, fin, rev_out, bwd, True)
    grads(n * 5 // 8, n)
    for h in range(HL):
        dk_out[h] = (dkq[0, h] * SCALE).astype(BF16)
        dq_out[h] = (dkq[1, h] * SCALE).astype(BF16)
    scan_finish(nz, head, rev_out, bwd)

    small_drain(nz, head, fin_own, fin, fsem)
    small_drain(nz, head, stats_own, stats, ssem)

    @pl.loop(0, nz)
    def _(zz):
        for h in range(2):
            wait_send(pairs.at[zz, h, 0], up_s.at[zz, h], me, head)
            wait_send(pairs.at[zz, h, 1], dn_s.at[zz, h], me, head)

            @pl.when(inner_row)
            def _():
                wait_send(pairs.at[zz, h, 0], rel_s.at[zz, h, 0], me, head)
                wait_send(pairs.at[zz, h, 1], rel_s.at[zz, h, 1], me, head)

    for h in range(2, HL):
        wait_send(pairs.at[z, h, 0], up_s.at[z, h], me, head)
        wait_send(pairs.at[z, h, 1], dn_s.at[z, h], me, head)

        @pl.when(inner_row)
        def _():
            wait_send(pairs.at[z, h, 0], rel_s.at[z, h, 0], me, head)
            wait_send(pairs.at[z, h, 1], rel_s.at[z, h, 1], me, head)

    @pl.loop(0, nz - 1)
    def _(s):
        for h in range(HL):
            zz = at(s, h)
            wait_send(pairs.at[zz, h, pl.ds(3, 2)], ring_s.at[zz, h], me, head)
            if h >= 2:
                wait_send(pairs.at[zz, h, pl.ds(0, 3)], bun_s.at[zz, h - 2], me, head)


def fused(nz, nh, own, lin, decay, gain, state, fin, bias, mask):
    full = pl.BlockSpec(memory_space=pltpu.VMEM)
    sem = pltpu.SemaphoreType.DMA
    per_head = pltpu.VMEM((HL, B, B), F32)
    return pl.pallas_call(
        functools.partial(fused_kernel, nz, nh),
        out_shape=(jax.ShapeDtypeStruct((HL, B, B), BF16),) * 4
        + (jax.ShapeDtypeStruct((HL * B, B), BF16),) * 2,
        in_specs=[full] * 8,
        out_specs=(full,) * 6,
        scratch_shapes=[
            pltpu.VMEM((nz, HL, 5, 2, B, B), BF16),
            pltpu.VMEM((nz, HL, 4, B, B), F32),
            pltpu.VMEM((nz, HL, 4, B, B), F32),
            per_head,
            per_head,
            per_head,
            per_head,
            pltpu.VMEM((2, HL, B, B), F32),
            per_head,
            per_head,
            per_head,
            per_head,
            pltpu.VMEM((HL * B, B), BF16),
            pltpu.VMEM((NY, nz, 2 * HL, B), F32),
            pltpu.VMEM((16, B), F32),
            pltpu.VMEM((NY, nz, 16, B), F32),
            pltpu.VMEM((2, nh, 8, B), F32),
            pltpu.VMEM((2, 8, B), F32),
            sem((nz, HL)),
            sem((nz, HL)),
            sem((nz, 2)),
            sem((nz, 2)),
            sem((nz, HL)),
            sem((nz, HL)),
            sem((nz, HL, 3)),
            sem((nz, HL, 2)),
            sem((5, max(nz, NY))),
            sem((5, max(nz, NY))),
            sem((4, nh)),
        ]
        + scan_scratch(nz) * 2,
        compiler_params=pltpu.CompilerParams(
            collective_id=0, has_side_effects=True, vmem_limit_bytes=56 << 20
        ),
    )(own.reshape(HL, 2, 2, B, B), lin, decay, gain, state, fin, bias, mask)


def last_kernel(lin, dec, state_in, cot, rev, dq_in, dk_in, dv_in, dq_o, dk_o, dv_o, sq_o, sk_o, sv_o, tmp):
    run = running_of(dec[...])
    trail = jnp.exp(run[:, B - 1 : B] - run)
    keep = iota(0) <= iota(1)

    def put(ref, value):
        for h in range(HL):
            tmp[pl.ds(h, B, stride=HL), :] = value(h)
        ref[...] = tmp[...].astype(BF16)

    def dq(h):
        row = run[h : h + 1]
        col = col_of(row)
        pair = (mm_t(cot[h], lin[h, 2]) * within_of(row, col)).astype(BF16)
        return mm(pair, lin[h, 1]) + jnp.exp(col) * mm_t(cot[h], state_in[pl.ds(h * B, B), :])

    def within_t(h):
        row = run[h : h + 1]
        return jnp.where(keep, jnp.exp(jnp.where(keep, row - col_of(row), 0.0)), 0.0)

    def dk(h):
        pair = (mm_t(lin[h, 2], cot[h]) * within_t(h)).astype(BF16)
        return mm(pair, lin[h, 0]) + col_of(trail[h : h + 1]) * mm_t(lin[h, 2], rev[pl.ds(h * B, B), :])

    def dv(h):
        pair = (mm_t(lin[h, 1], lin[h, 0]) * within_t(h)).astype(BF16)
        return mm(pair, cot[h]) + col_of(trail[h : h + 1]) * mm(lin[h, 1], rev[pl.ds(h * B, B), :])

    put(dq_o, dq)
    put(dk_o, dk)
    put(dv_o, dv)
    put(sq_o, lambda h: dq_in[h].astype(F32))
    put(sk_o, lambda h: dk_in[h].astype(F32))
    put(sv_o, lambda h: dv_in[h].astype(F32))


def last(lin, dec, state_in, cot, rev, dq, dk, dv):
    full = pl.BlockSpec(memory_space=pltpu.VMEM)
    return pl.pallas_call(
        last_kernel,
        out_shape=(jax.ShapeDtypeStruct((HL * B, B), BF16),) * 6,
        in_specs=[full] * 8,
        out_specs=(full,) * 6,
        scratch_shapes=[pltpu.VMEM((HL * B, B), F32)],
    )(lin, dec, state_in, cot, rev, dq, dk, dv)


def local(nz, nh, lin_q, lin_k, lin_v, decay, gain, soft_q, soft_k, soft_v, out_grad, lists, counts):
    flat = [a.reshape(B * HL, B) for a in (lin_q, lin_k, lin_v, soft_q, soft_k, soft_v, out_grad)]
    own, lin, state, fin, bias, mask = prep(nz, lists, counts, flat, decay)
    dq, dk, dv, cot, rev, state_in = fused(nz, nh, own, lin, decay, gain, state, fin, bias, mask)
    grads = last(lin, decay, state_in, cot, rev, dq, dk, dv)
    return tuple(a.reshape(B, HL, B) for a in grads)


def solution(mesh):
    nz = mesh.shape["ctx"] // NY
    tokens = P("ctx", "head", None)
    in_specs = (
        (tokens,) * 3 + (P("head", "ctx"), P("head", None)) + (tokens,) * 4 + (P("ctx", None), P("ctx"))
    )
    return jax.shard_map(
        functools.partial(local, nz, mesh.shape["head"]),
        mesh=mesh,
        in_specs=in_specs,
        out_specs=(tokens,) * 6,
        check_vma=False,
    )
```

```python
import functools

import jax
import jax.numpy as jnp
from jax import lax
from jax.experimental import pallas as pl
from jax.experimental.pallas import tpu as pltpu
from jax.sharding import PartitionSpec as P

NY = 4
HL = 4
B = 128
NSEL = 16
FR = 48
EPS = 1e-05
SCALE = 128 ** (-0.5)
NEG = -1e30
BIG = 1e30
F32 = jnp.float32
BF16 = jnp.bfloat16
MESH = pl.DeviceIdType.MESH
HIGH = lax.Precision.HIGHEST


def mm(a, b):
    return lax.dot_general(a, b, (((1,), (0,)), ((), ())), preferred_element_type=F32)


def mm_t(a, b):
    return lax.dot_general(a, b, (((1,), (1,)), ((), ())), preferred_element_type=F32)


def t_mm(a, b):
    return lax.dot_general(a, b, (((0,), (0,)), ((), ())), preferred_element_type=F32)


def iota(dim):
    return lax.broadcasted_iota(jnp.int32, (B, B), dim)


def col_of(row):
    return jnp.transpose(jnp.broadcast_to(row, (B, B)))


def row_of(col):
    return jnp.transpose(jnp.broadcast_to(col, (B, B)))[0:1]


def running_of(decay):
    upper = (iota(0) <= iota(1)).astype(F32)
    return lax.dot_general(
        decay, upper, (((1,), (0,)), ((), ())), precision=HIGH, preferred_element_type=F32
    )


def within_of(row, col):
    keep = iota(0) >= iota(1)
    return jnp.where(keep, jnp.exp(jnp.where(keep, col - row, 0.0)), 0.0)


def slot_of(r, y):
    return jnp.where(lax.rem(y + NY - 1, NY) == r, 0, jnp.where(lax.rem(y + 1, NY) == r, 1, 2))


def place(nz):
    own = lax.axis_index("ctx")
    return own // nz, lax.rem(own, nz)


def start_remote(src, dst, send, recv, ctx, head):
    pltpu.make_async_remote_copy(
        src_ref=src, dst_ref=dst, send_sem=send, recv_sem=recv, device_id=(ctx, head), device_id_type=MESH
    ).start()


def wait_recv(ref, recv, ctx, head):
    pltpu.make_async_remote_copy(
        src_ref=ref, dst_ref=ref, send_sem=recv, recv_sem=recv, device_id=(ctx, head), device_id_type=MESH
    ).wait_recv()


def wait_send(ref, send, ctx, head):
    pltpu.make_async_remote_copy(
        src_ref=ref, dst_ref=ref, send_sem=send, recv_sem=send, device_id=(ctx, head), device_id_type=MESH
    ).wait_send()


def scan_scratch(nz):
    rs = HL * B // nz
    return [
        pltpu.VMEM((nz, rs, B), BF16),
        pltpu.VMEM((nz, rs, B), F32),
        pltpu.VMEM((NY, rs, B), F32),
        pltpu.VMEM((rs, B), F32),
        pltpu.VMEM((nz, rs, B), BF16),
        pltpu.SemaphoreType.DMA((6, nz)),
        pltpu.SemaphoreType.DMA((2,)),
    ]


def scan_start(nz, head, local, bufs):
    zbuf, sems, lsem = bufs[0], bufs[5], bufs[6]
    rs = HL * B // nz
    y, z = place(nz)
    for d in range(1, nz):
        zz = lax.rem(z + d, nz)
        start_remote(
            local.at[pl.ds(zz * rs, rs)], zbuf.at[z], sems.at[0, zz], sems.at[1, z], y * nz + zz, head
        )
    pltpu.make_async_copy(local.at[pl.ds(z * rs, rs)], zbuf.at[z], lsem.at[0]).start()


def scan_rows(nz, head, local, fin, bufs, reverse):
    zbuf, ebuf, tbuf, tsrc, _, sems, lsem = bufs
    rs = HL * B // nz
    y, z = place(nz)
    own = y * nz + z
    hz = z * rs // B
    pltpu.make_async_copy(local.at[pl.ds(z * rs, rs)], zbuf.at[z], lsem.at[0]).wait()
    for d in range(1, nz):
        zz = lax.rem(z + d, nz)
        wait_recv(zbuf.at[zz], sems.at[1, zz], own, head)

    total = jnp.zeros((rs, B), F32)
    for lap in range(nz):
        m = nz - 1 - lap if reverse else lap
        ebuf[m] = total
        total = total * jnp.exp(fin[y, m, pl.ds(hz, 1), :]) + zbuf[m].astype(F32)
    tsrc[...] = total
    for d in range(1, NY):
        yy = lax.rem(y + d, NY)
        start_remote(tsrc, tbuf.at[y], sems.at[2, yy], sems.at[3, y], yy * nz + z, head)
    for d in range(1, nz):
        zz = lax.rem(z + d, nz)
        wait_send(zbuf.at[0], sems.at[0, zz], own, head)


def scan_spread(nz, head, fin, out, bufs, reverse):
    _, ebuf, tbuf, tsrc, sbuf, sems, lsem = bufs
    rs = HL * B // nz
    y, z = place(nz)
    own = y * nz + z
    hz = z * rs // B
    for d in range(1, NY):
        yy = lax.rem(y + d, NY)
        wait_recv(tbuf.at[yy], sems.at[3, yy], own, head)
        wait_send(tsrc, sems.at[2, yy], own, head)
    carry = jnp.zeros((rs, B), F32)
    for lap in range(NY):
        r = NY - 1 - lap if reverse else lap
        use = (r > y) if reverse else (r < y)
        span = jnp.zeros((1, B), F32)
        for m in range(nz):
            span = span + fin[r, m, pl.ds(hz, 1), :]
        carry = jnp.where(use, carry * jnp.exp(span) + tbuf[r], carry)
    for lap in range(nz):
        m = nz - 1 - lap if reverse else lap
        sbuf[m] = (ebuf[m] + carry).astype(BF16)
        carry = carry * jnp.exp(fin[y, m, pl.ds(hz, 1), :])
    for d in range(1, nz):
        zz = lax.rem(z + d, nz)
        start_remote(
            sbuf.at[zz], out.at[pl.ds(z * rs, rs)], sems.at[4, zz], sems.at[5, z], y * nz + zz, head
        )
    pltpu.make_async_copy(sbuf.at[z], out.at[pl.ds(z * rs, rs)], lsem.at[1]).start()


def scan_finish(nz, head, out, bufs):
    sbuf, sems, lsem = bufs[4], bufs[5], bufs[6]
    rs = HL * B // nz
    y, z = place(nz)
    own = y * nz + z
    for d in range(1, nz):
        zz = lax.rem(z + d, nz)
        wait_recv(out.at[pl.ds(zz * rs, rs)], sems.at[5, zz], own, head)
        wait_send(sbuf.at[zz], sems.at[4, zz], own, head)
    pltpu.make_async_copy(sbuf.at[z], out.at[pl.ds(z * rs, rs)], lsem.at[1]).wait()


def small_start(nz, head, src, dst, sems):
    y, z = place(nz)
    for d in range(1, nz):
        zz = lax.rem(z + d, nz)
        start_remote(src, dst.at[y, z], sems.at[0, zz], sems.at[1, z], y * nz + zz, head)
    pltpu.make_async_copy(src, dst.at[y, z], sems.at[2, 0]).start()


def small_rows(nz, head, src, dst, sems):
    y, z = place(nz)
    own = y * nz + z
    for d in range(1, nz):
        zz = lax.rem(z + d, nz)
        wait_recv(dst.at[y, zz], sems.at[1, zz], own, head)
    pltpu.make_async_copy(src, dst.at[y, z], sems.at[2, 0]).wait()
    for d in range(1, NY):
        yy = lax.rem(y + d, NY)
        start_remote(dst.at[y], dst.at[y], sems.at[3, yy], sems.at[4, y], yy * nz + z, head)


def small_finish(nz, head, src, dst, sems):
    y, z = place(nz)
    own = y * nz + z
    for d in range(1, NY):
        yy = lax.rem(y + d, NY)
        wait_recv(dst.at[yy], sems.at[4, yy], own, head)


def small_drain(nz, head, src, dst, sems):
    y, z = place(nz)
    own = y * nz + z
    for d in range(1, nz):
        zz = lax.rem(z + d, nz)
        wait_send(src, sems.at[0, zz], own, head)
    for d in range(1, NY):
        yy = lax.rem(y + d, NY)
        wait_send(dst.at[y], sems.at[3, yy], own, head)


def greet(nz, head, nh):
    y, z = place(nz)
    barrier = pltpu.get_barrier_semaphore()
    for d in range(1, nz):
        pl.semaphore_signal(
            barrier, inc=1, device_id=(y * nz + lax.rem(z + d, nz), head), device_id_type=MESH
        )
    for d in range(1, NY):
        pl.semaphore_signal(
            barrier, inc=1, device_id=(lax.rem(y + d, NY) * nz + z, head), device_id_type=MESH
        )
    for d in range(1, nh):
        pl.semaphore_signal(
            barrier, inc=1, device_id=(y * nz + z, lax.rem(head + d, nh)), device_id_type=MESH
        )


def greeted(nz, nh):
    pl.semaphore_wait(pltpu.get_barrier_semaphore(), nz - 1 + NY - 1 + nh - 1)


def fused_kernel(
    nz,
    nh,
    lists,
    count,
    lq,
    lk,
    lv,
    sq,
    sk,
    sv,
    og,
    dec,
    gain,
    dq_out,
    dk_out,
    dv_out,
    lin_dq,
    part_dk,
    part_dv,
    rev_out,
    lin,
    own,
    pairs,
    a1,
    a2,
    mx,
    ls,
    acc,
    dkq,
    lcol,
    dcol,
    lo,
    cot,
    bias,
    state,
    state_in,
    fin_own,
    fin,
    lse_own,
    lse_all,
    del_own,
    del_all,
    hbuf,
    hsrc,
    tmp,
    ring_s,
    ring_r,
    bun_s,
    bun_r,
    up_s,
    dn_s,
    col_r,
    rel_s,
    fsem,
    lsem,
    dsem,
    hsem,
    *scans,
):
    fwd, bwd = scans[: len(scans) // 2], scans[len(scans) // 2 :]
    head = lax.axis_index("head")
    y, z = place(nz)
    me = y * nz + z
    n = NY * nz
    right, left = y * nz + lax.rem(z + 1, nz), y * nz + lax.rem(z + nz - 1, nz)
    above, below = lax.rem(y + 1, NY) * nz + z, lax.rem(y + NY - 1, NY) * nz + z
    part_up = jnp.where(y < NY - 1, 0, 1)
    part_dn = jnp.where(y > 0, 1, 0)
    inner_row = (y == 1) | (y == 2)
    greet(nz, head, nh)

    def heads(ref, store):
        tmp[...] = ref[...].astype(F32)
        for h in range(HL):
            store(h, tmp[pl.ds(h, B, stride=HL), :].astype(BF16))

    def own_at(t, a):
        def store(h, value):
            own[h, t, a] = value

        return store

    def lin_at(i):
        def store(h, value):
            lin[h, i] = value

        return store

    heads(sk, own_at(0, 0))
    heads(sq, own_at(1, 0))
    heads(sv, own_at(0, 1))
    heads(og, own_at(1, 1))
    greeted(nz, nh)

    def at(s, h):
        return lax.rem(z + nz - s, nz) if h % 2 == 0 else lax.rem(z + s, nz)

    def to_next(h):
        return right if h % 2 == 0 else left

    def ring(a, zz, h):
        return pairs.at[zz, h, pl.ds(3, 2), a]

    def ring_on(a, zz, h, src=None):
        start_remote(
            ring(a, zz, h) if src is None else src,
            ring(a, zz, h),
            ring_s.at[a, zz, h],
            ring_r.at[a, zz, h],
            to_next(h),
            head,
        )

    def bundle(a, zz, h):
        return pairs.at[zz, h, pl.ds(0, 3), a, pl.ds(FR, B - FR)]

    def bundle_on(a, zz, h):
        ref = bundle(a, zz, h)
        start_remote(ref, ref, bun_s.at[a, zz, h - 2], bun_r.at[a, zz, h - 2], to_next(h), head)

    def cell(a, zz, h, slot, rows):
        return pairs.at[zz, h, slot, a, pl.ds(0, rows)]

    def column_on(a, zz, h, up, dn, rows):
        start_remote(up, cell(a, zz, h, 0, rows), up_s.at[a, zz, h], col_r.at[a, zz, h, 0], above, head)
        start_remote(dn, cell(a, zz, h, 1, rows), dn_s.at[a, zz, h], col_r.at[a, zz, h, 1], below, head)

    def rows_of(h):
        return B if h < 2 else FR

    def begin(a):
        def column_own(h):
            column_on(a, z, h, own.at[h, part_up, a], own.at[h, part_dn, a], B)

        for h in (0, 1):
            ring_on(a, z, h, own.at[h, pl.ds(0, 2), a])
        for h in (2, 3):
            column_own(h)
        for h in (2, 3):
            ring_on(a, z, h, own.at[h, pl.ds(0, 2), a])
        for h in (0, 1):
            column_own(h)

    def relay(a, zz, h, rows):
        for k in (0, 1):
            wait_recv(cell(a, zz, h, k, rows), col_r.at[a, zz, h, k], me, head)

        @pl.when(inner_row)
        def _():
            for k, to in ((0, above), (1, below)):
                start_remote(
                    cell(a, zz, h, k, rows),
                    cell(a, zz, h, 2, rows),
                    rel_s.at[a, zz, h, k],
                    col_r.at[a, zz, h, 2],
                    to,
                    head,
                )

    def opposite(a, zz, h, rows):
        wait_recv(cell(a, zz, h, 2, rows), col_r.at[a, zz, h, 2], me, head)

    def lap(a, s, first=False, second=False, last=False):
        for h in range(HL):
            zz = at(s, h)
            wait_recv(ring(a, zz, h), ring_r.at[a, zz, h], me, head)
            if not last:
                ring_on(a, zz, h)
            rows = rows_of(h)
            column_on(a, zz, h, cell(a, zz, h, 3 + part_up, rows), cell(a, zz, h, 3 + part_dn, rows), rows)
        if first:
            for h in (2, 3):
                relay(a, z, h, B)
            for h in (2, 3):
                opposite(a, z, h, B)
                bundle_on(a, z, h)
            for h in (0, 1):
                relay(a, z, h, B)
        else:
            for h in range(HL):
                relay(a, at(s - 1, h), h, rows_of(h))
        for h in (2, 3):
            zz = at(s, h)
            wait_recv(bundle(a, zz, h), bun_r.at[a, zz, h - 2], me, head)
            if not last:
                bundle_on(a, zz, h)
        if second:
            for h in (0, 1):
                opposite(a, z, h, B)
        elif not first:
            for h in range(HL):
                opposite(a, at(s - 2, h), h, rows_of(h))

    lane = lax.broadcasted_iota(jnp.int32, (1, B), 1)
    causal = iota(0) >= iota(1)

    def kinds(zz, with_row):
        found = []
        for k, off in ((0, NY - 1), (1, 1), (2, 2)):
            r = lax.rem(y + off, NY)
            found.append((k, k, jnp.where(r < y, 1, 0), r))
        if with_row:
            t = jnp.where(zz < z, 1, 0)
            found.append((3, 4 - t, t, y))
        return found

    def score(zz, h, with_row):
        scores = []
        for k, slot, t, _ in kinds(zz, with_row):
            s = mm_t(own[h, t, 0], pairs[zz, h, slot, 0]) * SCALE
            a1[zz, h, k] = s
            scores.append(s + bias[k, pl.ds(zz, 1), :])
        top = functools.reduce(jnp.maximum, scores)
        m = jnp.maximum(mx[h], jnp.broadcast_to(jnp.max(top, axis=1, keepdims=True), (B, B)))
        total = ls[h] * jnp.exp(mx[h] - m)
        for s in scores:
            total = total + jnp.exp(s - m)
        mx[h] = m
        ls[h] = total

    def weigh(zz, h, with_row):
        for k, slot, t, r in kinds(zz, with_row):
            here = jnp.sum(
                jnp.where(lane == me, fin[r, zz, HL : HL + 1, :], 0.0), axis=1, keepdims=True
            )
            theirs = jnp.where(here > 0.5, lse_all[r, zz, h : h + 1, :], BIG)
            lse = jnp.where(t == 1, lcol[h] - bias[k, pl.ds(zz, 1), :], theirs)
            v = pairs[zz, h, slot, 1]
            p = jnp.exp(a1[zz, h, k] - lse)
            a1[zz, h, k] = p
            a2[zz, h, k] = mm_t(own[h, t, 1], v)
            acc[t, h] = acc[t, h] + mm(p.astype(BF16), v)

    begin(0)

    for h in range(HL):
        s = jnp.where(causal, mm_t(own[h, 1, 0], own[h, 0, 0]) * SCALE, NEG)
        m = jnp.broadcast_to(jnp.max(s, axis=1, keepdims=True), (B, B))
        mx[h] = m
        ls[h] = jnp.exp(s - m)
    column = lax.broadcasted_iota(jnp.int32, (nz, B), 0)
    named = jnp.zeros((1, B), F32)
    for e in range(NSEL):
        named = jnp.where((lane == lists[0, e]) & (e < count[0]), 1.0, named)
    for k, off in ((0, NY - 1), (1, 1), (2, 2), (3, 0)):
        block = lax.rem(y + off, NY) * nz + column
        b = jnp.full((nz, B), NEG, F32)
        for e in range(NSEL):
            b = jnp.where((block == lists[0, e]) & (e < count[0]), 0.0, b)
        bias[k] = b
    heads(lk, lin_at(1))
    heads(lv, lin_at(2))
    heads(lq, lin_at(0))
    run = running_of(dec[...])
    finish = run[:, B - 1 : B]
    fin_own[...] = jnp.concatenate(
        [jnp.broadcast_to(finish, (HL, B)), named, jnp.zeros((HL - 1, B), F32)], axis=0
    )
    trailing = jnp.exp(finish - run)
    for h in range(HL):
        k = lin[h, 1].astype(F32) * col_of(trailing[h : h + 1])
        state[pl.ds(h * B, B), :] = t_mm(k.astype(BF16), lin[h, 2]).astype(BF16)

    lap(0, 1, first=True)
    small_start(nz, head, fin_own, fin, fsem)
    scan_start(nz, head, state, fwd)
    lap(0, 2, second=True)
    for h in range(HL):
        score(z, h, False)
    small_rows(nz, head, fin_own, fin, fsem)
    scan_rows(nz, head, state, fin, fwd, False)

    @pl.loop(3, nz - 1)
    def _(s):
        lap(0, s)
        for h in range(HL):
            score(at(s - 2, h), h, True)

    begin(1)
    lap(0, nz - 1, last=True)
    for h in range(HL):
        score(at(nz - 3, h), h, True)
    for h in range(HL):
        relay(0, at(nz - 1, h), h, rows_of(h))
    lap(1, 1, first=True)
    for s in (nz - 2, nz - 1):
        for h in range(HL):
            opposite(0, at(s, h), h, rows_of(h))
        for h in range(HL):
            score(at(s, h), h, True)
    lse_own[...] = jnp.zeros_like(lse_own)
    for h in range(HL):
        lse = mx[h] + jnp.log(jnp.sum(ls[h], axis=1, keepdims=True))
        lcol[h] = lse
        lse_own[h : h + 1, :] = jnp.transpose(lse)[0:1]
    small_start(nz, head, lse_own, lse_all, lsem)
    small_finish(nz, head, fin_own, fin, fsem)
    scan_spread(nz, head, fin, state_in, fwd, False)
    lap(1, 2, second=True)
    small_rows(nz, head, lse_own, lse_all, lsem)
    for h in range(HL):
        p = jnp.where(causal, jnp.exp(mm_t(own[h, 1, 0], own[h, 0, 0]) * SCALE - lcol[h]), 0.0)
        dp = mm_t(own[h, 1, 1], own[h, 0, 1])
        a1[z, h, 3] = p
        a2[z, h, 3] = dp
        low = p.astype(BF16)
        acc[1, h] = mm(low, own[h, 0, 1])
        acc[0, h] = t_mm(low, own[h, 1, 1])
    lap(1, 3)
    small_finish(nz, head, lse_own, lse_all, lsem)
    for h in range(HL):
        weigh(z, h, False)
    for h in range(HL):
        weigh(at(1, h), h, True)

    def heads_start(k):
        for d in range(1, nh):
            hh = lax.rem(head + d, nh)
            start_remote(hsrc.at[k], hbuf.at[k, head], hsem.at[2 * k, hh], hsem.at[2 * k + 1, head], me, hh)

    def heads_total(k):
        total = hsrc[k]
        for d in range(1, nh):
            hh = lax.rem(head + d, nh)
            wait_recv(hbuf.at[k, hh], hsem.at[2 * k + 1, hh], me, head)
            total = total + hbuf[k, hh]
            wait_send(hsrc.at[k], hsem.at[2 * k, hh], me, head)
        return total[0:1]

    if nz > 4:
        lap(1, 4)
        for h in range(HL):
            weigh(at(2, h), h, True)

    scan_finish(nz, head, state_in, fwd)
    squares = jnp.zeros((B, 1), F32)
    for h in range(HL):
        row = run[h : h + 1]
        col = col_of(row)
        w = (mm_t(lin[h, 0], lin[h, 1]) * within_of(row, col)).astype(BF16)
        o = mm(w, lin[h, 2]) + jnp.exp(col) * mm(lin[h, 0], state_in[pl.ds(h * B, B), :])
        lo[h] = o
        squares = squares + jnp.sum(o * o, axis=1, keepdims=True)
    hsrc[0] = jnp.broadcast_to(row_of(squares), (8, B))
    heads_start(0)

    if nz > 4:

        @pl.loop(5, nz - 1)
        def _(s):
            lap(1, s)
            for h in range(HL):
                weigh(at(s - 2, h), h, True)

        lap(1, nz - 1, last=True)
        for h in range(HL):
            weigh(at(nz - 3, h), h, True)
    for h in range(HL):
        relay(1, at(nz - 1, h), h, rows_of(h))
    for s in (nz - 2, nz - 1):
        for h in range(HL):
            opposite(1, at(s, h), h, rows_of(h))
        for h in range(HL):
            weigh(at(s, h), h, True)

    partial = jnp.zeros((B, 1), F32)
    for h in range(HL):
        c = (acc[0, h] + own[h, 1, 1].astype(F32)) * gain[h : h + 1, :]
        cot[h] = c
        partial = partial + jnp.sum(c * lo[h], axis=1, keepdims=True)
    hsrc[1] = jnp.broadcast_to(row_of(partial), (8, B))
    heads_start(1)

    del_own[...] = jnp.zeros_like(del_own)
    for h in range(HL):
        dv_out[h] = acc[0, h].astype(BF16)
        delta = jnp.sum(own[h, 1, 1].astype(F32) * acc[1, h], axis=1, keepdims=True)
        delta = jnp.broadcast_to(delta, (B, B))
        dcol[h] = delta
        del_own[h : h + 1, :] = jnp.transpose(delta)[0:1]
    small_start(nz, head, del_own, del_all, dsem)
    for h in range(HL):
        ds = (a1[z, h, 3] * (a2[z, h, 3] - dcol[h])).astype(BF16)
        dkq[1, h] = mm(ds, own[h, 0, 0])
        dkq[0, h] = t_mm(ds, own[h, 1, 0])

    def key_grads(lo_i, hi_i):
        @pl.loop(lo_i, jnp.minimum(hi_i, me))
        def _(i):
            r, zz = i // nz, lax.rem(i, nz)
            k = jnp.where(r == y, 3, slot_of(r, y))
            for h in range(HL):
                ds = (a1[zz, h, k] * (a2[zz, h, k] - dcol[h])).astype(BF16)
                dkq[1, h] = dkq[1, h] + mm(ds, pairs[zz, h, k, 0])

    def query_grads(lo_i, hi_i):
        @pl.loop(jnp.maximum(lo_i, me + 1), hi_i)
        def _(i):
            r, zz = i // nz, lax.rem(i, nz)
            k = jnp.where(r == y, 3, slot_of(r, y))
            slot = jnp.where(r == y, 4, k)
            for h in range(HL):
                ds = (a1[zz, h, k] * (a2[zz, h, k] - del_all[r, zz, h : h + 1, :])).astype(BF16)
                dkq[0, h] = dkq[0, h] + mm(ds, pairs[zz, h, slot, 0])

    width = HL * nh * B
    root = jnp.sqrt(heads_total(0) / width + EPS)
    inner = heads_total(1)
    factor = col_of(inner / (width * root * root * root))
    inv = col_of(1.0 / root)
    leading = jnp.exp(run)
    for h in range(HL):
        lc = cot[h] * inv - lo[h] * factor
        cot[h] = lc
        q = (lin[h, 0].astype(F32) * col_of(leading[h : h + 1])).astype(BF16)
        state[pl.ds(h * B, B), :] = t_mm(q, lc.astype(BF16)).astype(BF16)
    scan_start(nz, head, state, bwd)
    key_grads(0, n // 2)
    small_rows(nz, head, del_own, del_all, dsem)
    scan_rows(nz, head, state, fin, bwd, True)
    for h in range(HL):
        row = run[h : h + 1]
        col = col_of(row)
        within = within_of(row, col)
        c = cot[h].astype(BF16)
        pair = (mm_t(c, lin[h, 2]) * within).astype(BF16)
        w = (mm_t(lin[h, 0], lin[h, 1]) * within).astype(BF16)
        o = mm(pair, lin[h, 1]) + jnp.exp(col) * mm_t(c, state_in[pl.ds(h * B, B), :])
        lin_dq[h] = o.astype(BF16)
        part_dk[h] = t_mm(pair, lin[h, 0])
        part_dv[h] = t_mm(w, c)
    small_finish(nz, head, del_own, del_all, dsem)
    scan_spread(nz, head, fin, rev_out, bwd, True)
    key_grads(n // 2, n)
    query_grads(0, n)
    for h in range(HL):
        dk_out[h] = (dkq[0, h] * SCALE).astype(BF16)
        dq_out[h] = (dkq[1, h] * SCALE).astype(BF16)
    scan_finish(nz, head, rev_out, bwd)

    small_drain(nz, head, fin_own, fin, fsem)
    small_drain(nz, head, lse_own, lse_all, lsem)
    small_drain(nz, head, del_own, del_all, dsem)

    for a in range(2):

        def column_left(zz, h, rows):
            wait_send(cell(a, zz, h, 0, rows), up_s.at[a, zz, h], me, head)
            wait_send(cell(a, zz, h, 1, rows), dn_s.at[a, zz, h], me, head)

            @pl.when(inner_row)
            def _():
                for k in (0, 1):
                    wait_send(cell(a, zz, h, k, rows), rel_s.at[a, zz, h, k], me, head)

        for h in range(HL):
            column_left(z, h, B)

        @pl.loop(0, nz - 1)
        def _(s):
            for h in range(HL):
                zz = at(s, h)
                wait_send(ring(a, zz, h), ring_s.at[a, zz, h], me, head)
                if h >= 2:
                    wait_send(bundle(a, zz, h), bun_s.at[a, zz, h - 2], me, head)
                column_left(at(s + 1, h), h, rows_of(h))


def fused(nz, nh, lists, counts, arrays, decay, gain):
    full = pl.BlockSpec(memory_space=pltpu.VMEM)
    smem = pl.BlockSpec(memory_space=pltpu.SMEM)
    sem = pltpu.SemaphoreType.DMA
    per_head = pltpu.VMEM((HL, B, B), F32)
    small = pltpu.VMEM((2 * HL, B), F32)
    small_all = pltpu.VMEM((NY, nz, 2 * HL, B), F32)
    low = jax.ShapeDtypeStruct((HL, B, B), BF16)
    wide = jax.ShapeDtypeStruct((HL, B, B), F32)
    return pl.pallas_call(
        functools.partial(fused_kernel, nz, nh),
        out_shape=(low,) * 4
        + (wide,) * 2
        + (jax.ShapeDtypeStruct((HL * B, B), BF16), jax.ShapeDtypeStruct((HL, 3, B, B), BF16)),
        in_specs=[smem, smem] + [full] * 9,
        out_specs=(full,) * 8,
        scratch_shapes=[
            pltpu.VMEM((HL, 2, 2, B, B), BF16),
            pltpu.VMEM((nz, HL, 5, 2, B, B), BF16),
            pltpu.VMEM((nz, HL, 4, B, B), F32),
            pltpu.VMEM((nz, HL, 4, B, B), F32),
            per_head,
            per_head,
            pltpu.VMEM((2, HL, B, B), F32),
            pltpu.VMEM((2, HL, B, B), F32),
            per_head,
            per_head,
            per_head,
            per_head,
            pltpu.VMEM((4, nz, B), F32),
            pltpu.VMEM((HL * B, B), BF16),
            pltpu.VMEM((HL * B, B), BF16),
            small,
            small_all,
            small,
            small_all,
            small,
            small_all,
            pltpu.VMEM((2, nh, 8, B), F32),
            pltpu.VMEM((2, 8, B), F32),
            pltpu.VMEM((HL * B, B), F32),
            sem((2, nz, HL)),
            sem((2, nz, HL)),
            sem((2, nz, 2)),
            sem((2, nz, 2)),
            sem((2, nz, HL)),
            sem((2, nz, HL)),
            sem((2, nz, HL, 3)),
            sem((2, nz, HL, 2)),
            sem((5, max(nz, NY))),
            sem((5, max(nz, NY))),
            sem((5, max(nz, NY))),
            sem((4, nh)),
        ]
        + scan_scratch(nz) * 2,
        compiler_params=pltpu.CompilerParams(
            collective_id=0, has_side_effects=True, vmem_limit_bytes=56 << 20
        ),
    )(lists, counts, *arrays, decay, gain)


def last_kernel(lin, dec, rev, dq, dk, dv, lq, pdk, pdv, o_lq, o_lk, o_lv, o_q, o_k, o_v, tmp):
    run = running_of(dec[...])
    trail = jnp.exp(run[:, B - 1 : B] - run)

    def put(ref, value):
        for h in range(HL):
            tmp[pl.ds(h, B, stride=HL), :] = value(h)
        ref[...] = tmp[...].astype(BF16)

    def lin_dk(h):
        return pdk[h] + col_of(trail[h : h + 1]) * mm_t(lin[h, 2], rev[pl.ds(h * B, B), :])

    def lin_dv(h):
        return pdv[h] + col_of(trail[h : h + 1]) * mm(lin[h, 1], rev[pl.ds(h * B, B), :])

    put(o_lq, lambda h: lq[h].astype(F32))
    put(o_lk, lin_dk)
    put(o_lv, lin_dv)
    put(o_q, lambda h: dq[h].astype(F32))
    put(o_k, lambda h: dk[h].astype(F32))
    put(o_v, lambda h: dv[h].astype(F32))


def last(lin, decay, rev, *parts):
    full = pl.BlockSpec(memory_space=pltpu.VMEM)
    return pl.pallas_call(
        last_kernel,
        out_shape=(jax.ShapeDtypeStruct((HL * B, B), BF16),) * 6,
        in_specs=[full] * 9,
        out_specs=(full,) * 6,
        scratch_shapes=[pltpu.VMEM((HL * B, B), F32)],
    )(lin, decay, rev, *parts)


def local(nz, nh, lin_q, lin_k, lin_v, decay, gain, soft_q, soft_k, soft_v, out_grad, lists, counts):
    flat = [a.reshape(B * HL, B) for a in (lin_q, lin_k, lin_v, soft_q, soft_k, soft_v, out_grad)]
    dq, dk, dv, lin_dq, part_dk, part_dv, rev, lin = fused(nz, nh, lists, counts, flat, decay, gain)
    grads = last(lin, decay, rev, dq, dk, dv, lin_dq, part_dk, part_dv)
    return tuple(a.reshape(B, HL, B) for a in grads)


def solution(mesh):
    nz = mesh.shape["ctx"] // NY
    tokens = P("ctx", "head", None)
    in_specs = (
        (tokens,) * 3 + (P("head", "ctx"), P("head", None)) + (tokens,) * 4 + (P("ctx", None), P("ctx"))
    )
    return jax.shard_map(
        functools.partial(local, nz, mesh.shape["head"]),
        mesh=mesh,
        in_specs=in_specs,
        out_specs=(tokens,) * 6,
        check_vma=False,
    )
```

```python
import functools

import jax
import jax.numpy as jnp
from jax import lax
from jax.experimental import pallas as pl
from jax.experimental.pallas import tpu as pltpu
from jax.sharding import PartitionSpec as P

NY = 4
HL = 4
B = 128
NSEL = 16
EPS = 1e-05
SCALE = 128 ** (-0.5)
NEG = -1e30
BIG = 1e30
F32 = jnp.float32
BF16 = jnp.bfloat16
MESH = pl.DeviceIdType.MESH
HIGH = lax.Precision.HIGHEST


def mm(a, b):
    return lax.dot_general(a, b, (((1,), (0,)), ((), ())), preferred_element_type=F32)


def mm_t(a, b):
    return lax.dot_general(a, b, (((1,), (1,)), ((), ())), preferred_element_type=F32)


def t_mm(a, b):
    return lax.dot_general(a, b, (((0,), (0,)), ((), ())), preferred_element_type=F32)


def iota(dim):
    return lax.broadcasted_iota(jnp.int32, (B, B), dim)


def col_of(row):
    return jnp.transpose(jnp.broadcast_to(row, (B, B)))


def row_of(col):
    return jnp.transpose(jnp.broadcast_to(col, (B, B)))[0:1]


def running_of(decay):
    upper = (iota(0) <= iota(1)).astype(F32)
    return lax.dot_general(
        decay, upper, (((1,), (0,)), ((), ())), precision=HIGH, preferred_element_type=F32
    )


def within_of(row, col):
    keep = iota(0) >= iota(1)
    return jnp.where(keep, jnp.exp(jnp.where(keep, col - row, 0.0)), 0.0)


def slot_of(r, y):
    return jnp.where(lax.rem(y + NY - 1, NY) == r, 0, jnp.where(lax.rem(y + 1, NY) == r, 1, 2))


def place(nz):
    own = lax.axis_index("ctx")
    return own // nz, lax.rem(own, nz)


def start_remote(src, dst, send, recv, ctx, head):
    pltpu.make_async_remote_copy(
        src_ref=src, dst_ref=dst, send_sem=send, recv_sem=recv, device_id=(ctx, head), device_id_type=MESH
    ).start()


def wait_recv(ref, recv, ctx, head):
    pltpu.make_async_remote_copy(
        src_ref=ref, dst_ref=ref, send_sem=recv, recv_sem=recv, device_id=(ctx, head), device_id_type=MESH
    ).wait_recv()


def wait_send(ref, send, ctx, head):
    pltpu.make_async_remote_copy(
        src_ref=ref, dst_ref=ref, send_sem=send, recv_sem=send, device_id=(ctx, head), device_id_type=MESH
    ).wait_send()


def scan_scratch(nz):
    rs = HL * B // nz
    return [
        pltpu.VMEM((nz, rs, B), BF16),
        pltpu.VMEM((nz, rs, B), F32),
        pltpu.VMEM((NY, rs, B), F32),
        pltpu.VMEM((rs, B), F32),
        pltpu.VMEM((nz, rs, B), BF16),
        pltpu.SemaphoreType.DMA((6, nz)),
        pltpu.SemaphoreType.DMA((2,)),
    ]


def scan_start(nz, head, local, bufs):
    zbuf, sems, lsem = bufs[0], bufs[5], bufs[6]
    rs = HL * B // nz
    y, z = place(nz)
    for d in range(1, nz):
        zz = lax.rem(z + d, nz)
        start_remote(
            local.at[pl.ds(zz * rs, rs)], zbuf.at[z], sems.at[0, zz], sems.at[1, z], y * nz + zz, head
        )
    pltpu.make_async_copy(local.at[pl.ds(z * rs, rs)], zbuf.at[z], lsem.at[0]).start()


def scan_rows(nz, head, local, fin, bufs, reverse):
    zbuf, ebuf, tbuf, tsrc, _, sems, lsem = bufs
    rs = HL * B // nz
    y, z = place(nz)
    own = y * nz + z
    hz = z * rs // B
    pltpu.make_async_copy(local.at[pl.ds(z * rs, rs)], zbuf.at[z], lsem.at[0]).wait()
    for d in range(1, nz):
        zz = lax.rem(z + d, nz)
        wait_recv(zbuf.at[zz], sems.at[1, zz], own, head)

    total = jnp.zeros((rs, B), F32)
    for lap in range(nz):
        m = nz - 1 - lap if reverse else lap
        ebuf[m] = total
        total = total * jnp.exp(fin[y, m, pl.ds(hz, 1), :]) + zbuf[m].astype(F32)
    tsrc[...] = total
    for d in range(1, NY):
        yy = lax.rem(y + d, NY)
        start_remote(tsrc, tbuf.at[y], sems.at[2, yy], sems.at[3, y], yy * nz + z, head)
    for d in range(1, nz):
        zz = lax.rem(z + d, nz)
        wait_send(zbuf.at[0], sems.at[0, zz], own, head)


def scan_spread(nz, head, fin, out, bufs, reverse):
    _, ebuf, tbuf, tsrc, sbuf, sems, lsem = bufs
    rs = HL * B // nz
    y, z = place(nz)
    own = y * nz + z
    hz = z * rs // B
    for d in range(1, NY):
        yy = lax.rem(y + d, NY)
        wait_recv(tbuf.at[yy], sems.at[3, yy], own, head)
        wait_send(tsrc, sems.at[2, yy], own, head)
    carry = jnp.zeros((rs, B), F32)
    for lap in range(NY):
        r = NY - 1 - lap if reverse else lap
        use = (r > y) if reverse else (r < y)
        span = jnp.zeros((1, B), F32)
        for m in range(nz):
            span = span + fin[r, m, pl.ds(hz, 1), :]
        carry = jnp.where(use, carry * jnp.exp(span) + tbuf[r], carry)
    for lap in range(nz):
        m = nz - 1 - lap if reverse else lap
        sbuf[m] = (ebuf[m] + carry).astype(BF16)
        carry = carry * jnp.exp(fin[y, m, pl.ds(hz, 1), :])
    for d in range(1, nz):
        zz = lax.rem(z + d, nz)
        start_remote(
            sbuf.at[zz], out.at[pl.ds(z * rs, rs)], sems.at[4, zz], sems.at[5, z], y * nz + zz, head
        )
    pltpu.make_async_copy(sbuf.at[z], out.at[pl.ds(z * rs, rs)], lsem.at[1]).start()


def scan_finish(nz, head, out, bufs):
    sbuf, sems, lsem = bufs[4], bufs[5], bufs[6]
    rs = HL * B // nz
    y, z = place(nz)
    own = y * nz + z
    for d in range(1, nz):
        zz = lax.rem(z + d, nz)
        wait_recv(out.at[pl.ds(zz * rs, rs)], sems.at[5, zz], own, head)
        wait_send(sbuf.at[zz], sems.at[4, zz], own, head)
    pltpu.make_async_copy(sbuf.at[z], out.at[pl.ds(z * rs, rs)], lsem.at[1]).wait()


def small_start(nz, head, src, dst, sems):
    y, z = place(nz)
    for d in range(1, nz):
        zz = lax.rem(z + d, nz)
        start_remote(src, dst.at[y, z], sems.at[0, zz], sems.at[1, z], y * nz + zz, head)
    pltpu.make_async_copy(src, dst.at[y, z], sems.at[2, 0]).start()


def small_rows(nz, head, src, dst, sems):
    y, z = place(nz)
    own = y * nz + z
    for d in range(1, nz):
        zz = lax.rem(z + d, nz)
        wait_recv(dst.at[y, zz], sems.at[1, zz], own, head)
    pltpu.make_async_copy(src, dst.at[y, z], sems.at[2, 0]).wait()
    for d in range(1, NY):
        yy = lax.rem(y + d, NY)
        start_remote(dst.at[y], dst.at[y], sems.at[3, yy], sems.at[4, y], yy * nz + z, head)


def small_finish(nz, head, src, dst, sems):
    y, z = place(nz)
    own = y * nz + z
    for d in range(1, NY):
        yy = lax.rem(y + d, NY)
        wait_recv(dst.at[yy], sems.at[4, yy], own, head)


def small_drain(nz, head, src, dst, sems):
    y, z = place(nz)
    own = y * nz + z
    for d in range(1, nz):
        zz = lax.rem(z + d, nz)
        wait_send(src, sems.at[0, zz], own, head)
    for d in range(1, NY):
        yy = lax.rem(y + d, NY)
        wait_send(dst.at[y], sems.at[3, yy], own, head)


def greet(nz, head, nh):
    y, z = place(nz)
    barrier = pltpu.get_barrier_semaphore()
    for d in range(1, nz):
        pl.semaphore_signal(
            barrier, inc=1, device_id=(y * nz + lax.rem(z + d, nz), head), device_id_type=MESH
        )
    for d in range(1, NY):
        pl.semaphore_signal(
            barrier, inc=1, device_id=(lax.rem(y + d, NY) * nz + z, head), device_id_type=MESH
        )
    for d in range(1, nh):
        pl.semaphore_signal(
            barrier, inc=1, device_id=(y * nz + z, lax.rem(head + d, nh)), device_id_type=MESH
        )


def greeted(nz, nh):
    pl.semaphore_wait(pltpu.get_barrier_semaphore(), nz - 1 + NY - 1 + nh - 1)


def fused_kernel(
    nz,
    nh,
    lists,
    count,
    lq,
    lk,
    lv,
    sq,
    sk,
    sv,
    og,
    dec,
    gain,
    dq_out,
    dk_out,
    dv_out,
    lin_dq,
    part_dk,
    part_dv,
    rev_out,
    lin,
    own,
    pairs,
    a1,
    a2,
    mx,
    ls,
    acc,
    dkq,
    lcol,
    dcol,
    lo,
    cot,
    bias,
    state,
    state_in,
    fin_own,
    fin,
    lse_own,
    lse_all,
    del_own,
    del_all,
    hbuf,
    hsrc,
    tmp,
    ring_s,
    ring_r,
    opp_s,
    opp_r,
    up_s,
    dn_s,
    col_r,
    rel_s,
    fsem,
    lsem,
    dsem,
    hsem,
    *scans,
):
    fwd, bwd = scans[: len(scans) // 2], scans[len(scans) // 2 :]
    head = lax.axis_index("head")
    y, z = place(nz)
    me = y * nz + z
    n = NY * nz
    right, left = y * nz + lax.rem(z + 1, nz), y * nz + lax.rem(z + nz - 1, nz)
    above, below = lax.rem(y + 1, NY) * nz + z, lax.rem(y + NY - 1, NY) * nz + z
    part_up = jnp.where(y < NY - 1, 0, 1)
    part_dn = jnp.where(y > 0, 1, 0)
    inner_row = (y == 1) | (y == 2)
    greet(nz, head, nh)

    def heads(ref, store):
        tmp[...] = ref[...].astype(F32)
        for h in range(HL):
            store(h, tmp[pl.ds(h, B, stride=HL), :].astype(BF16))

    def own_at(t, a):
        def store(h, value):
            own[h, t, a] = value

        return store

    def lin_at(i):
        def store(h, value):
            lin[h, i] = value

        return store

    heads(sk, own_at(0, 0))
    heads(sq, own_at(1, 0))
    heads(sv, own_at(0, 1))
    heads(og, own_at(1, 1))
    greeted(nz, nh)

    def at(s, h):
        return lax.rem(z + nz - s, nz) if h % 2 == 0 else lax.rem(z + s, nz)

    def to_next(h):
        return right if h % 2 == 0 else left

    def ring(a, zz, h):
        return pairs.at[zz, h, pl.ds(3, 2), a]

    def ring_on(a, zz, h, src=None):
        start_remote(
            ring(a, zz, h) if src is None else src,
            ring(a, zz, h),
            ring_s.at[a, zz, h],
            ring_r.at[a, zz, h],
            to_next(h),
            head,
        )

    def opposite(a, zz, h):
        return pairs.at[zz, h, 2, a]

    def opposite_on(a, zz, h):
        ref = opposite(a, zz, h)
        start_remote(ref, ref, opp_s.at[a, zz, h], opp_r.at[a, zz, h], to_next(h), head)

    def opposite_wait(a, zz, h):
        wait_recv(opposite(a, zz, h), opp_r.at[a, zz, h], me, head)

    def column_on(a, zz, h, up, dn):
        start_remote(up, pairs.at[zz, h, 0, a], up_s.at[a, zz, h], col_r.at[a, zz, h, 0], above, head)
        start_remote(dn, pairs.at[zz, h, 1, a], dn_s.at[a, zz, h], col_r.at[a, zz, h, 1], below, head)

    def column_wait(a, zz, h):
        for k in (0, 1):
            wait_recv(pairs.at[zz, h, k, a], col_r.at[a, zz, h, k], me, head)

    def begin(a):
        for h in range(HL):
            column_on(a, z, h, own.at[h, part_up, a], own.at[h, part_dn, a])
            ring_on(a, z, h, own.at[h, pl.ds(0, 2), a])

    def relay(a, h):
        column_wait(a, z, h)

        @pl.when(inner_row)
        def _():
            for k, to in ((0, above), (1, below)):
                start_remote(
                    pairs.at[z, h, k, a], opposite(a, z, h), rel_s.at[a, h, k], opp_r.at[a, z, h], to, head
                )

    def settle(a, s, last=False):
        for h in range(HL):
            opposite_wait(a, at(s, h), h)
            if not last:
                opposite_on(a, at(s, h), h)
        for h in range(HL):
            column_wait(a, at(s, h), h)

    def lap(a, s, first=False, last=False):
        for h in range(HL):
            zz = at(s, h)
            wait_recv(ring(a, zz, h), ring_r.at[a, zz, h], me, head)
            if not last:
                ring_on(a, zz, h)
            column_on(a, zz, h, pairs.at[zz, h, 3 + part_up, a], pairs.at[zz, h, 3 + part_dn, a])
        if first:
            for h in range(HL):
                relay(a, h)
            for h in range(HL):
                opposite_wait(a, z, h)
                opposite_on(a, z, h)
        else:
            settle(a, s - 1)

    lane = lax.broadcasted_iota(jnp.int32, (1, B), 1)
    causal = iota(0) >= iota(1)

    def kinds(zz, with_row):
        found = []
        for k, off in ((0, NY - 1), (1, 1), (2, 2)):
            r = lax.rem(y + off, NY)
            found.append((k, k, jnp.where(r < y, 1, 0), r))
        if with_row:
            t = jnp.where(zz < z, 1, 0)
            found.append((3, 4 - t, t, y))
        return found

    def score(zz, h, with_row):
        scores = []
        for k, slot, t, _ in kinds(zz, with_row):
            s = mm_t(own[h, t, 0], pairs[zz, h, slot, 0]) * SCALE
            a1[zz, h, k] = s
            scores.append(s + bias[k, pl.ds(zz, 1), :])
        top = functools.reduce(jnp.maximum, scores)
        m = jnp.maximum(mx[h], jnp.broadcast_to(jnp.max(top, axis=1, keepdims=True), (B, B)))
        total = ls[h] * jnp.exp(mx[h] - m)
        for s in scores:
            total = total + jnp.exp(s - m)
        mx[h] = m
        ls[h] = total

    def weigh(zz, h, with_row):
        for k, slot, t, r in kinds(zz, with_row):
            here = jnp.sum(
                jnp.where(lane == me, fin[r, zz, HL : HL + 1, :], 0.0), axis=1, keepdims=True
            )
            theirs = jnp.where(here > 0.5, lse_all[r, zz, h : h + 1, :], BIG)
            lse = jnp.where(t == 1, lcol[h] - bias[k, pl.ds(zz, 1), :], theirs)
            v = pairs[zz, h, slot, 1]
            p = jnp.exp(a1[zz, h, k] - lse)
            a1[zz, h, k] = p
            a2[zz, h, k] = mm_t(own[h, t, 1], v)
            acc[t, h] = acc[t, h] + mm(p.astype(BF16), v)

    begin(0)

    for h in range(HL):
        s = jnp.where(causal, mm_t(own[h, 1, 0], own[h, 0, 0]) * SCALE, NEG)
        m = jnp.broadcast_to(jnp.max(s, axis=1, keepdims=True), (B, B))
        mx[h] = m
        ls[h] = jnp.exp(s - m)
    column = lax.broadcasted_iota(jnp.int32, (nz, B), 0)
    named = jnp.zeros((1, B), F32)
    for e in range(NSEL):
        named = jnp.where((lane == lists[0, e]) & (e < count[0]), 1.0, named)
    for k, off in ((0, NY - 1), (1, 1), (2, 2), (3, 0)):
        block = lax.rem(y + off, NY) * nz + column
        b = jnp.full((nz, B), NEG, F32)
        for e in range(NSEL):
            b = jnp.where((block == lists[0, e]) & (e < count[0]), 0.0, b)
        bias[k] = b
    heads(lk, lin_at(1))
    heads(lv, lin_at(2))
    heads(lq, lin_at(0))
    run = running_of(dec[...])
    finish = run[:, B - 1 : B]
    fin_own[...] = jnp.concatenate(
        [jnp.broadcast_to(finish, (HL, B)), named, jnp.zeros((HL - 1, B), F32)], axis=0
    )
    trailing = jnp.exp(finish - run)
    for h in range(HL):
        k = lin[h, 1].astype(F32) * col_of(trailing[h : h + 1])
        state[pl.ds(h * B, B), :] = t_mm(k.astype(BF16), lin[h, 2]).astype(BF16)

    lap(0, 1, first=True)
    small_start(nz, head, fin_own, fin, fsem)
    scan_start(nz, head, state, fwd)
    for h in range(HL):
        score(z, h, False)
    lap(0, 2)
    for h in range(HL):
        score(at(1, h), h, True)
    small_rows(nz, head, fin_own, fin, fsem)
    scan_rows(nz, head, state, fin, fwd, False)

    @pl.loop(3, nz - 1)
    def _(s):
        lap(0, s)
        for h in range(HL):
            score(at(s - 1, h), h, True)

    begin(1)
    lap(0, nz - 1, last=True)
    for h in range(HL):
        score(at(nz - 2, h), h, True)
    lap(1, 1, first=True)
    settle(0, nz - 1, last=True)
    for h in range(HL):
        score(at(nz - 1, h), h, True)
    lse_own[...] = jnp.zeros_like(lse_own)
    for h in range(HL):
        lse = mx[h] + jnp.log(jnp.sum(ls[h], axis=1, keepdims=True))
        lcol[h] = lse
        lse_own[h : h + 1, :] = jnp.transpose(lse)[0:1]
    small_start(nz, head, lse_own, lse_all, lsem)
    small_finish(nz, head, fin_own, fin, fsem)
    scan_spread(nz, head, fin, state_in, fwd, False)
    lap(1, 2)
    small_rows(nz, head, lse_own, lse_all, lsem)
    for h in range(HL):
        p = jnp.where(causal, jnp.exp(mm_t(own[h, 1, 0], own[h, 0, 0]) * SCALE - lcol[h]), 0.0)
        dp = mm_t(own[h, 1, 1], own[h, 0, 1])
        a1[z, h, 3] = p
        a2[z, h, 3] = dp
        low = p.astype(BF16)
        acc[1, h] = mm(low, own[h, 0, 1])
        acc[0, h] = t_mm(low, own[h, 1, 1])
    lap(1, 3, last=nz == 4)
    small_finish(nz, head, lse_own, lse_all, lsem)
    for h in range(HL):
        weigh(z, h, False)
    for s in (1, 2):
        for h in range(HL):
            weigh(at(s, h), h, True)

    def heads_start(k):
        for d in range(1, nh):
            hh = lax.rem(head + d, nh)
            start_remote(hsrc.at[k], hbuf.at[k, head], hsem.at[2 * k, hh], hsem.at[2 * k + 1, head], me, hh)

    def heads_total(k):
        total = hsrc[k]
        for d in range(1, nh):
            hh = lax.rem(head + d, nh)
            wait_recv(hbuf.at[k, hh], hsem.at[2 * k + 1, hh], me, head)
            total = total + hbuf[k, hh]
            wait_send(hsrc.at[k], hsem.at[2 * k, hh], me, head)
        return total[0:1]

    if nz > 4:
        lap(1, 4)
        for h in range(HL):
            weigh(at(3, h), h, True)

    scan_finish(nz, head, state_in, fwd)
    squares = jnp.zeros((B, 1), F32)
    for h in range(HL):
        row = run[h : h + 1]
        col = col_of(row)
        w = (mm_t(lin[h, 0], lin[h, 1]) * within_of(row, col)).astype(BF16)
        o = mm(w, lin[h, 2]) + jnp.exp(col) * mm(lin[h, 0], state_in[pl.ds(h * B, B), :])
        lo[h] = o
        squares = squares + jnp.sum(o * o, axis=1, keepdims=True)
    hsrc[0] = jnp.broadcast_to(row_of(squares), (8, B))
    heads_start(0)

    if nz > 4:

        @pl.loop(5, nz - 1)
        def _(s):
            lap(1, s)
            for h in range(HL):
                weigh(at(s - 1, h), h, True)

        lap(1, nz - 1, last=True)
        for h in range(HL):
            weigh(at(nz - 2, h), h, True)
    settle(1, nz - 1, last=True)
    for h in range(HL):
        weigh(at(nz - 1, h), h, True)

    partial = jnp.zeros((B, 1), F32)
    for h in range(HL):
        c = (acc[0, h] + own[h, 1, 1].astype(F32)) * gain[h : h + 1, :]
        cot[h] = c
        partial = partial + jnp.sum(c * lo[h], axis=1, keepdims=True)
    hsrc[1] = jnp.broadcast_to(row_of(partial), (8, B))
    heads_start(1)

    del_own[...] = jnp.zeros_like(del_own)
    for h in range(HL):
        dv_out[h] = acc[0, h].astype(BF16)
        delta = jnp.sum(own[h, 1, 1].astype(F32) * acc[1, h], axis=1, keepdims=True)
        delta = jnp.broadcast_to(delta, (B, B))
        dcol[h] = delta
        del_own[h : h + 1, :] = jnp.transpose(delta)[0:1]
    small_start(nz, head, del_own, del_all, dsem)
    for h in range(HL):
        ds = (a1[z, h, 3] * (a2[z, h, 3] - dcol[h])).astype(BF16)
        dkq[1, h] = mm(ds, own[h, 0, 0])
        dkq[0, h] = t_mm(ds, own[h, 1, 0])

    def key_grads(lo_i, hi_i):
        @pl.loop(lo_i, jnp.minimum(hi_i, me))
        def _(i):
            r, zz = i // nz, lax.rem(i, nz)
            k = jnp.where(r == y, 3, slot_of(r, y))
            for h in range(HL):
                ds = (a1[zz, h, k] * (a2[zz, h, k] - dcol[h])).astype(BF16)
                dkq[1, h] = dkq[1, h] + mm(ds, pairs[zz, h, k, 0])

    def query_grads(lo_i, hi_i):
        @pl.loop(jnp.maximum(lo_i, me + 1), hi_i)
        def _(i):
            r, zz = i // nz, lax.rem(i, nz)
            k = jnp.where(r == y, 3, slot_of(r, y))
            slot = jnp.where(r == y, 4, k)
            for h in range(HL):
                ds = (a1[zz, h, k] * (a2[zz, h, k] - del_all[r, zz, h : h + 1, :])).astype(BF16)
                dkq[0, h] = dkq[0, h] + mm(ds, pairs[zz, h, slot, 0])

    width = HL * nh * B
    root = jnp.sqrt(heads_total(0) / width + EPS)
    inner = heads_total(1)
    factor = col_of(inner / (width * root * root * root))
    inv = col_of(1.0 / root)
    leading = jnp.exp(run)
    for h in range(HL):
        lc = cot[h] * inv - lo[h] * factor
        cot[h] = lc
        q = (lin[h, 0].astype(F32) * col_of(leading[h : h + 1])).astype(BF16)
        state[pl.ds(h * B, B), :] = t_mm(q, lc.astype(BF16)).astype(BF16)
    scan_start(nz, head, state, bwd)
    key_grads(0, n // 2)
    small_rows(nz, head, del_own, del_all, dsem)
    scan_rows(nz, head, state, fin, bwd, True)
    for h in range(HL):
        row = run[h : h + 1]
        col = col_of(row)
        within = within_of(row, col)
        c = cot[h].astype(BF16)
        pair = (mm_t(c, lin[h, 2]) * within).astype(BF16)
        w = (mm_t(lin[h, 0], lin[h, 1]) * within).astype(BF16)
        o = mm(pair, lin[h, 1]) + jnp.exp(col) * mm_t(c, state_in[pl.ds(h * B, B), :])
        lin_dq[h] = o.astype(BF16)
        part_dk[h] = t_mm(pair, lin[h, 0])
        part_dv[h] = t_mm(w, c)
    small_finish(nz, head, del_own, del_all, dsem)
    scan_spread(nz, head, fin, rev_out, bwd, True)
    key_grads(n // 2, n)
    query_grads(0, n)
    for h in range(HL):
        dk_out[h] = (dkq[0, h] * SCALE).astype(BF16)
        dq_out[h] = (dkq[1, h] * SCALE).astype(BF16)
    scan_finish(nz, head, rev_out, bwd)

    small_drain(nz, head, fin_own, fin, fsem)
    small_drain(nz, head, lse_own, lse_all, lsem)
    small_drain(nz, head, del_own, del_all, dsem)

    for a in range(2):

        def column_left(zz, h):
            wait_send(pairs.at[zz, h, 0, a], up_s.at[a, zz, h], me, head)
            wait_send(pairs.at[zz, h, 1, a], dn_s.at[a, zz, h], me, head)

        for h in range(HL):
            column_left(z, h)

            @pl.when(inner_row)
            def _():
                for k in (0, 1):
                    wait_send(pairs.at[z, h, k, a], rel_s.at[a, h, k], me, head)

        @pl.loop(0, nz - 1)
        def _(s):
            for h in range(HL):
                zz = at(s, h)
                wait_send(ring(a, zz, h), ring_s.at[a, zz, h], me, head)
                wait_send(opposite(a, zz, h), opp_s.at[a, zz, h], me, head)
                column_left(at(s + 1, h), h)


def fused(nz, nh, lists, counts, arrays, decay, gain):
    full = pl.BlockSpec(memory_space=pltpu.VMEM)
    smem = pl.BlockSpec(memory_space=pltpu.SMEM)
    sem = pltpu.SemaphoreType.DMA
    per_head = pltpu.VMEM((HL, B, B), F32)
    small = pltpu.VMEM((2 * HL, B), F32)
    small_all = pltpu.VMEM((NY, nz, 2 * HL, B), F32)
    low = jax.ShapeDtypeStruct((HL, B, B), BF16)
    wide = jax.ShapeDtypeStruct((HL, B, B), F32)
    return pl.pallas_call(
        functools.partial(fused_kernel, nz, nh),
        out_shape=(low,) * 4
        + (wide,) * 2
        + (jax.ShapeDtypeStruct((HL * B, B), BF16), jax.ShapeDtypeStruct((HL, 3, B, B), BF16)),
        in_specs=[smem, smem] + [full] * 9,
        out_specs=(full,) * 8,
        scratch_shapes=[
            pltpu.VMEM((HL, 2, 2, B, B), BF16),
            pltpu.VMEM((nz, HL, 5, 2, B, B), BF16),
            pltpu.VMEM((nz, HL, 4, B, B), F32),
            pltpu.VMEM((nz, HL, 4, B, B), F32),
            per_head,
            per_head,
            pltpu.VMEM((2, HL, B, B), F32),
            pltpu.VMEM((2, HL, B, B), F32),
            per_head,
            per_head,
            per_head,
            per_head,
            pltpu.VMEM((4, nz, B), F32),
            pltpu.VMEM((HL * B, B), BF16),
            pltpu.VMEM((HL * B, B), BF16),
            small,
            small_all,
            small,
            small_all,
            small,
            small_all,
            pltpu.VMEM((2, nh, 8, B), F32),
            pltpu.VMEM((2, 8, B), F32),
            pltpu.VMEM((HL * B, B), F32),
            sem((2, nz, HL)),
            sem((2, nz, HL)),
            sem((2, nz, HL)),
            sem((2, nz, HL)),
            sem((2, nz, HL)),
            sem((2, nz, HL)),
            sem((2, nz, HL, 2)),
            sem((2, HL, 2)),
            sem((5, max(nz, NY))),
            sem((5, max(nz, NY))),
            sem((5, max(nz, NY))),
            sem((4, nh)),
        ]
        + scan_scratch(nz) * 2,
        compiler_params=pltpu.CompilerParams(
            collective_id=0, has_side_effects=True, vmem_limit_bytes=56 << 20
        ),
    )(lists, counts, *arrays, decay, gain)


def last_kernel(lin, dec, rev, dq, dk, dv, lq, pdk, pdv, o_lq, o_lk, o_lv, o_q, o_k, o_v, tmp):
    run = running_of(dec[...])
    trail = jnp.exp(run[:, B - 1 : B] - run)

    def put(ref, value):
        for h in range(HL):
            tmp[pl.ds(h, B, stride=HL), :] = value(h)
        ref[...] = tmp[...].astype(BF16)

    def lin_dk(h):
        return pdk[h] + col_of(trail[h : h + 1]) * mm_t(lin[h, 2], rev[pl.ds(h * B, B), :])

    def lin_dv(h):
        return pdv[h] + col_of(trail[h : h + 1]) * mm(lin[h, 1], rev[pl.ds(h * B, B), :])

    put(o_lq, lambda h: lq[h].astype(F32))
    put(o_lk, lin_dk)
    put(o_lv, lin_dv)
    put(o_q, lambda h: dq[h].astype(F32))
    put(o_k, lambda h: dk[h].astype(F32))
    put(o_v, lambda h: dv[h].astype(F32))


def last(lin, decay, rev, *parts):
    full = pl.BlockSpec(memory_space=pltpu.VMEM)
    return pl.pallas_call(
        last_kernel,
        out_shape=(jax.ShapeDtypeStruct((HL * B, B), BF16),) * 6,
        in_specs=[full] * 9,
        out_specs=(full,) * 6,
        scratch_shapes=[pltpu.VMEM((HL * B, B), F32)],
    )(lin, decay, rev, *parts)


def local(nz, nh, lin_q, lin_k, lin_v, decay, gain, soft_q, soft_k, soft_v, out_grad, lists, counts):
    flat = [a.reshape(B * HL, B) for a in (lin_q, lin_k, lin_v, soft_q, soft_k, soft_v, out_grad)]
    dq, dk, dv, lin_dq, part_dk, part_dv, rev, lin = fused(nz, nh, lists, counts, flat, decay, gain)
    grads = last(lin, decay, rev, dq, dk, dv, lin_dq, part_dk, part_dv)
    return tuple(a.reshape(B, HL, B) for a in grads)


def solution(mesh):
    nz = mesh.shape["ctx"] // NY
    tokens = P("ctx", "head", None)
    in_specs = (
        (tokens,) * 3 + (P("head", "ctx"), P("head", None)) + (tokens,) * 4 + (P("ctx", None), P("ctx"))
    )
    return jax.shard_map(
        functools.partial(local, nz, mesh.shape["head"]),
        mesh=mesh,
        in_specs=in_specs,
        out_specs=(tokens,) * 6,
        check_vma=False,
    )
```

```python
import functools

import jax
import jax.numpy as jnp
from jax import lax
from jax.experimental import pallas as pl
from jax.experimental.pallas import tpu as pltpu
from jax.sharding import PartitionSpec as P

NY = 4
HL = 4
B = 128
NSEL = 16
EPS = 1e-05
SCALE = 128 ** (-0.5)
NEG = -1e30
BIG = 1e30
F32 = jnp.float32
BF16 = jnp.bfloat16
MESH = pl.DeviceIdType.MESH
HIGH = lax.Precision.HIGHEST


def mm(a, b):
    return lax.dot_general(a, b, (((1,), (0,)), ((), ())), preferred_element_type=F32)


def mm_t(a, b):
    return lax.dot_general(a, b, (((1,), (1,)), ((), ())), preferred_element_type=F32)


def t_mm(a, b):
    return lax.dot_general(a, b, (((0,), (0,)), ((), ())), preferred_element_type=F32)


def iota(dim):
    return lax.broadcasted_iota(jnp.int32, (B, B), dim)


def col_of(row):
    return jnp.transpose(jnp.broadcast_to(row, (B, B)))


def row_of(col):
    return jnp.transpose(jnp.broadcast_to(col, (B, B)))[0:1]


def running_of(decay):
    upper = (iota(0) <= iota(1)).astype(F32)
    return lax.dot_general(
        decay, upper, (((1,), (0,)), ((), ())), precision=HIGH, preferred_element_type=F32
    )


def within_of(row, col):
    keep = iota(0) >= iota(1)
    return jnp.where(keep, jnp.exp(jnp.where(keep, col - row, 0.0)), 0.0)


def slot_of(r, y):
    return jnp.where(lax.rem(y + NY - 1, NY) == r, 0, jnp.where(lax.rem(y + 1, NY) == r, 1, 2))


def far_first(n):
    return sorted(range(1, n), key=lambda d: (-min(d, n - d), d))


def place(nz):
    own = lax.axis_index("ctx")
    return own // nz, lax.rem(own, nz)


def start_remote(src, dst, send, recv, ctx, head):
    pltpu.make_async_remote_copy(
        src_ref=src, dst_ref=dst, send_sem=send, recv_sem=recv, device_id=(ctx, head), device_id_type=MESH
    ).start()


def wait_recv(ref, recv, ctx, head):
    pltpu.make_async_remote_copy(
        src_ref=ref, dst_ref=ref, send_sem=recv, recv_sem=recv, device_id=(ctx, head), device_id_type=MESH
    ).wait_recv()


def wait_send(ref, send, ctx, head):
    pltpu.make_async_remote_copy(
        src_ref=ref, dst_ref=ref, send_sem=send, recv_sem=send, device_id=(ctx, head), device_id_type=MESH
    ).wait_send()


def scan_scratch(nz):
    rs = HL * B // nz
    return [
        pltpu.VMEM((nz, rs, B), BF16),
        pltpu.VMEM((nz, rs, B), F32),
        pltpu.VMEM((NY, rs, B), BF16),
        pltpu.VMEM((rs, B), BF16),
        pltpu.VMEM((nz, rs, B), BF16),
        pltpu.SemaphoreType.DMA((6, max(nz, NY))),
        pltpu.SemaphoreType.DMA((2,)),
        pltpu.VMEM((rs, B), F32),
    ]


def scan_start(nz, head, local, bufs):
    zbuf, sems, lsem = bufs[0], bufs[5], bufs[6]
    rs = HL * B // nz
    y, z = place(nz)
    for d in far_first(nz):
        zz = lax.rem(z + d, nz)
        start_remote(
            local.at[pl.ds(zz * rs, rs)], zbuf.at[z], sems.at[0, zz], sems.at[1, z], y * nz + zz, head
        )
    pltpu.make_async_copy(local.at[pl.ds(z * rs, rs)], zbuf.at[z], lsem.at[0]).start()


def scan_rows(nz, head, local, fin, bufs, reverse):
    zbuf, ebuf, tbuf, tsrc, _, sems, lsem, _ = bufs
    rs = HL * B // nz
    y, z = place(nz)
    own = y * nz + z
    hz = z * rs // B
    pltpu.make_async_copy(local.at[pl.ds(z * rs, rs)], zbuf.at[z], lsem.at[0]).wait()
    for d in range(1, nz):
        zz = lax.rem(z + d, nz)
        wait_recv(zbuf.at[zz], sems.at[1, zz], own, head)

    total = jnp.zeros((rs, B), F32)
    for lap in range(nz):
        m = nz - 1 - lap if reverse else lap
        ebuf[m] = total
        total = total * jnp.exp(fin[y, m, pl.ds(hz, 1), :]) + zbuf[m].astype(F32)
    tsrc[...] = total.astype(BF16)
    for yy in range(NY):

        @pl.when((yy < y) if reverse else (yy > y))
        def _():
            start_remote(tsrc, tbuf.at[y], sems.at[2, yy], sems.at[3, y], yy * nz + z, head)

    for d in range(1, nz):
        zz = lax.rem(z + d, nz)
        wait_send(zbuf.at[0], sems.at[0, zz], own, head)


def scan_spread(nz, head, fin, out, bufs, reverse):
    _, ebuf, tbuf, tsrc, sbuf, sems, lsem, cbuf = bufs
    rs = HL * B // nz
    y, z = place(nz)
    own = y * nz + z
    hz = z * rs // B
    for yy in range(NY):

        @pl.when((yy > y) if reverse else (yy < y))
        def _():
            wait_recv(tbuf.at[yy], sems.at[3, yy], own, head)

        @pl.when((yy < y) if reverse else (yy > y))
        def _():
            wait_send(tsrc, sems.at[2, yy], own, head)

    cbuf[...] = jnp.zeros_like(cbuf)
    for lap in range(NY):
        r = NY - 1 - lap if reverse else lap

        @pl.when((r > y) if reverse else (r < y))
        def _():
            span = jnp.zeros((1, B), F32)
            for m in range(nz):
                span = span + fin[r, m, pl.ds(hz, 1), :]
            cbuf[...] = cbuf[...] * jnp.exp(span) + tbuf[r].astype(F32)

    carry = cbuf[...]
    for lap in range(nz):
        m = nz - 1 - lap if reverse else lap
        sbuf[m] = (ebuf[m] + carry).astype(BF16)
        carry = carry * jnp.exp(fin[y, m, pl.ds(hz, 1), :])
    for d in far_first(nz):
        zz = lax.rem(z + d, nz)
        start_remote(
            sbuf.at[zz], out.at[pl.ds(z * rs, rs)], sems.at[4, zz], sems.at[5, z], y * nz + zz, head
        )
    pltpu.make_async_copy(sbuf.at[z], out.at[pl.ds(z * rs, rs)], lsem.at[1]).start()


def scan_finish(nz, head, out, bufs):
    sbuf, sems, lsem = bufs[4], bufs[5], bufs[6]
    rs = HL * B // nz
    y, z = place(nz)
    own = y * nz + z
    for d in range(1, nz):
        zz = lax.rem(z + d, nz)
        wait_recv(out.at[pl.ds(zz * rs, rs)], sems.at[5, zz], own, head)
        wait_send(sbuf.at[zz], sems.at[4, zz], own, head)
    pltpu.make_async_copy(sbuf.at[z], out.at[pl.ds(z * rs, rs)], lsem.at[1]).wait()


def small_start(nz, head, src, dst, sems):
    y, z = place(nz)
    for d in far_first(nz):
        zz = lax.rem(z + d, nz)
        start_remote(src, dst.at[y, z], sems.at[0, zz], sems.at[1, z], y * nz + zz, head)
    pltpu.make_async_copy(src, dst.at[y, z], sems.at[2, 0]).start()


def small_rows(nz, head, src, dst, sems):
    y, z = place(nz)
    own = y * nz + z
    for d in range(1, nz):
        zz = lax.rem(z + d, nz)
        wait_recv(dst.at[y, zz], sems.at[1, zz], own, head)
    pltpu.make_async_copy(src, dst.at[y, z], sems.at[2, 0]).wait()
    for d in range(1, NY):
        yy = lax.rem(y + d, NY)
        start_remote(dst.at[y], dst.at[y], sems.at[3, yy], sems.at[4, y], yy * nz + z, head)


def small_finish(nz, head, src, dst, sems):
    y, z = place(nz)
    own = y * nz + z
    for d in range(1, NY):
        yy = lax.rem(y + d, NY)
        wait_recv(dst.at[yy], sems.at[4, yy], own, head)


def small_drain(nz, head, src, dst, sems):
    y, z = place(nz)
    own = y * nz + z
    for d in range(1, nz):
        zz = lax.rem(z + d, nz)
        wait_send(src, sems.at[0, zz], own, head)
    for d in range(1, NY):
        yy = lax.rem(y + d, NY)
        wait_send(dst.at[y], sems.at[3, yy], own, head)


def greet(nz, head, nh):
    y, z = place(nz)
    barrier = pltpu.get_barrier_semaphore()
    for d in range(1, nz):
        pl.semaphore_signal(
            barrier, inc=1, device_id=(y * nz + lax.rem(z + d, nz), head), device_id_type=MESH
        )
    for d in range(1, NY):
        pl.semaphore_signal(
            barrier, inc=1, device_id=(lax.rem(y + d, NY) * nz + z, head), device_id_type=MESH
        )
    for d in range(1, nh):
        pl.semaphore_signal(
            barrier, inc=1, device_id=(y * nz + z, lax.rem(head + d, nh)), device_id_type=MESH
        )


def greeted(nz, nh):
    pl.semaphore_wait(pltpu.get_barrier_semaphore(), nz - 1 + NY - 1 + nh - 1)


def fused_kernel(
    nz,
    nh,
    lists,
    count,
    lq,
    lk,
    lv,
    sq,
    sk,
    sv,
    og,
    dec,
    gain,
    dq_out,
    dk_out,
    dv_out,
    lin_dq,
    part_dk,
    part_dv,
    rev_out,
    lin,
    own,
    pairs,
    a1,
    a2,
    mx,
    ls,
    acc,
    dkq,
    lcol,
    dcol,
    lo,
    cot,
    bias,
    state,
    state_in,
    fin_own,
    fin,
    lse_own,
    lse_all,
    del_own,
    del_all,
    hbuf,
    hsrc,
    tmp,
    query_t,
    ring_s,
    ring_r,
    opp_s,
    opp_r,
    up_s,
    dn_s,
    col_r,
    rel_s,
    fsem,
    lsem,
    dsem,
    hsem,
    *scans,
):
    fwd, bwd = scans[: len(scans) // 2], scans[len(scans) // 2 :]
    head = lax.axis_index("head")
    y, z = place(nz)
    me = y * nz + z
    right, left = y * nz + lax.rem(z + 1, nz), y * nz + lax.rem(z + nz - 1, nz)
    above, below = lax.rem(y + 1, NY) * nz + z, lax.rem(y + NY - 1, NY) * nz + z
    part_up = jnp.where(y < NY - 1, 0, 1)
    part_dn = jnp.where(y > 0, 1, 0)
    inner_row = (y == 1) | (y == 2)
    greet(nz, head, nh)

    def heads(ref, store):
        tmp[...] = ref[...].astype(F32)
        for h in range(HL):
            store(h, tmp[pl.ds(h, B, stride=HL), :].astype(BF16))

    def own_at(t, a):
        def store(h, value):
            own[h, t, a] = value

        return store

    def lin_at(i):
        def store(h, value):
            lin[h, i] = value

        return store

    heads(sk, own_at(0, 0))
    heads(sq, own_at(1, 0))
    greeted(nz, nh)

    def at(s, h):
        return lax.rem(z + nz - s, nz) if h % 2 == 0 else lax.rem(z + s, nz)

    def to_next(h):
        return right if h % 2 == 0 else left

    def ring(a, zz, h):
        return pairs.at[zz, h, pl.ds(3, 2), a]

    def ring_on(a, zz, h, src=None):
        start_remote(
            ring(a, zz, h) if src is None else src,
            ring(a, zz, h),
            ring_s.at[a, zz, h],
            ring_r.at[a, zz, h],
            to_next(h),
            head,
        )

    def opposite(a, zz, h):
        return pairs.at[zz, h, 2, a]

    def opposite_on(a, zz, h):
        ref = opposite(a, zz, h)
        start_remote(ref, ref, opp_s.at[a, zz, h], opp_r.at[a, zz, h], to_next(h), head)

    def opposite_wait(a, zz, h):
        wait_recv(opposite(a, zz, h), opp_r.at[a, zz, h], me, head)

    def column_on(a, zz, h, up, dn):
        start_remote(up, pairs.at[zz, h, 0, a], up_s.at[a, zz, h], col_r.at[a, zz, h, 0], above, head)
        start_remote(dn, pairs.at[zz, h, 1, a], dn_s.at[a, zz, h], col_r.at[a, zz, h, 1], below, head)

    def column_wait(a, zz, h):
        for k in (0, 1):
            wait_recv(pairs.at[zz, h, k, a], col_r.at[a, zz, h, k], me, head)

    def begin(a):
        for h in range(HL):
            column_on(a, z, h, own.at[h, part_up, a], own.at[h, part_dn, a])
            ring_on(a, z, h, own.at[h, pl.ds(0, 2), a])

    def relay(a, h):
        column_wait(a, z, h)

        @pl.when(inner_row)
        def _():
            for k, to in ((0, above), (1, below)):
                start_remote(
                    pairs.at[z, h, k, a], opposite(a, z, h), rel_s.at[a, h, k], opp_r.at[a, z, h], to, head
                )

    def settle(a, s, last=False):
        for h in range(HL):
            opposite_wait(a, at(s, h), h)
            if not last:
                opposite_on(a, at(s, h), h)
        for h in range(HL):
            column_wait(a, at(s, h), h)

    def lap(a, s, first=False, last=False, mid=None):
        for h in range(HL):
            zz = at(s, h)
            wait_recv(ring(a, zz, h), ring_r.at[a, zz, h], me, head)
            if not last:
                ring_on(a, zz, h)
            column_on(a, zz, h, pairs.at[zz, h, 3 + part_up, a], pairs.at[zz, h, 3 + part_dn, a])
        if mid is not None:
            mid()
        if first:
            for h in range(HL):
                relay(a, h)
            for h in range(HL):
                opposite_wait(a, z, h)
                opposite_on(a, z, h)
        else:
            settle(a, s - 1)

    lane = lax.broadcasted_iota(jnp.int32, (1, B), 1)
    causal = iota(0) >= iota(1)

    def kinds(zz, with_row):
        found = []
        for k, off in ((0, NY - 1), (1, 1), (2, 2)):
            r = lax.rem(y + off, NY)
            found.append((k, k, jnp.where(r < y, 1, 0), r))
        if with_row:
            t = jnp.where(zz < z, 1, 0)
            found.append((3, 4 - t, t, y))
        return found

    def score(zz, h, with_row):
        scores = []
        for k, slot, t, _ in kinds(zz, with_row):
            s = mm_t(own[h, t, 0], pairs[zz, h, slot, 0]) * SCALE
            a1[zz, h, k] = s
            scores.append(s + bias[k, pl.ds(zz, 1), :])
        top = functools.reduce(jnp.maximum, scores)
        m = jnp.maximum(mx[h], jnp.broadcast_to(jnp.max(top, axis=1, keepdims=True), (B, B)))
        total = ls[h] * jnp.exp(mx[h] - m)
        for s in scores:
            total = total + jnp.exp(s - m)
        mx[h] = m
        ls[h] = total

    def weigh(zz, h, with_row):
        for k, slot, t, r in kinds(zz, with_row):
            here = jnp.sum(
                jnp.where(lane == me, fin[r, zz, HL : HL + 1, :], 0.0), axis=1, keepdims=True
            )
            theirs = jnp.where(here > 0.5, lse_all[r, zz, h : h + 1, :], BIG)
            lse = jnp.where(t == 1, lcol[h] - bias[k, pl.ds(zz, 1), :], theirs)
            v = pairs[zz, h, slot, 1]
            p = jnp.exp(a1[zz, h, k] - lse)
            a1[zz, h, k] = p
            a2[zz, h, k] = mm_t(own[h, t, 1], v)
            acc[t, h] = acc[t, h] + mm(p.astype(BF16), v)

    begin(0)

    def start_scores():
        for h in range(HL):
            s = jnp.where(causal, mm_t(own[h, 1, 0], own[h, 0, 0]) * SCALE, NEG)
            m = jnp.broadcast_to(jnp.max(s, axis=1, keepdims=True), (B, B))
            mx[h] = m
            ls[h] = jnp.exp(s - m)
        column = lax.broadcasted_iota(jnp.int32, (nz, B), 0)
        for k, off in ((0, NY - 1), (1, 1), (2, 2), (3, 0)):
            block = lax.rem(y + off, NY) * nz + column
            b = jnp.full((nz, B), NEG, F32)
            for e in range(NSEL):
                b = jnp.where((block == lists[0, e]) & (e < count[0]), 0.0, b)
            bias[k] = b

    lap(0, 1, first=True, mid=start_scores)
    heads(sv, own_at(0, 1))
    heads(og, own_at(1, 1))
    heads(lk, lin_at(1))
    heads(lv, lin_at(2))
    heads(lq, lin_at(0))
    run = running_of(dec[...])
    named = jnp.zeros((1, B), F32)
    for e in range(NSEL):
        named = jnp.where((lane == lists[0, e]) & (e < count[0]), 1.0, named)
    finish = run[:, B - 1 : B]
    fin_own[...] = jnp.concatenate(
        [jnp.broadcast_to(finish, (HL, B)), named, jnp.zeros((HL - 1, B), F32)], axis=0
    )
    trailing = jnp.exp(finish - run)
    for h in range(HL):
        k = lin[h, 1].astype(F32) * col_of(trailing[h : h + 1])
        state[pl.ds(h * B, B), :] = t_mm(k.astype(BF16), lin[h, 2]).astype(BF16)
    small_start(nz, head, fin_own, fin, fsem)
    scan_start(nz, head, state, fwd)
    for h in range(HL):
        score(z, h, False)
    lap(0, 2)
    for h in (0, 1):
        score(at(1, h), h, True)
    small_rows(nz, head, fin_own, fin, fsem)
    scan_rows(nz, head, state, fin, fwd, False)

    @pl.loop(3, nz - 1)
    def _(s):
        def rest():
            for h in (2, 3):
                score(at(s - 2, h), h, True)

        lap(0, s, mid=rest)
        for h in (0, 1):
            score(at(s - 1, h), h, True)

    begin(1)

    def rest(s):
        for h in (2, 3):
            score(at(s, h), h, True)

    lap(0, nz - 1, last=True, mid=lambda: rest(nz - 3))
    for h in (0, 1):
        score(at(nz - 2, h), h, True)
    lap(1, 1, first=True, mid=lambda: rest(nz - 2))
    settle(0, nz - 1, last=True)
    for h in range(HL):
        score(at(nz - 1, h), h, True)
    lse_own[...] = jnp.zeros_like(lse_own)
    for h in range(HL):
        lse = mx[h] + jnp.log(jnp.sum(ls[h], axis=1, keepdims=True))
        lcol[h] = lse
        lse_own[h : h + 1, :] = jnp.transpose(lse)[0:1]
    small_start(nz, head, lse_own, lse_all, lsem)
    small_finish(nz, head, fin_own, fin, fsem)
    scan_spread(nz, head, fin, state_in, fwd, False)
    lap(1, 2)
    small_rows(nz, head, lse_own, lse_all, lsem)
    for h in range(HL):
        p = jnp.where(causal, jnp.exp(mm_t(own[h, 1, 0], own[h, 0, 0]) * SCALE - lcol[h]), 0.0)
        dp = mm_t(own[h, 1, 1], own[h, 0, 1])
        a1[z, h, 3] = p
        a2[z, h, 3] = dp
        low = p.astype(BF16)
        acc[1, h] = mm(low, own[h, 0, 1])
        acc[0, h] = t_mm(low, own[h, 1, 1])
    lap(1, 3, last=nz == 4)
    small_finish(nz, head, lse_own, lse_all, lsem)
    for h in range(HL):
        weigh(z, h, False)
    for s in (1, 2):
        for h in range(HL):
            weigh(at(s, h), h, True)

    def heads_start(k):
        for d in range(1, nh):
            hh = lax.rem(head + d, nh)
            start_remote(hsrc.at[k], hbuf.at[k, head], hsem.at[2 * k, hh], hsem.at[2 * k + 1, head], me, hh)

    def heads_total(k):
        total = hsrc[k]
        for d in range(1, nh):
            hh = lax.rem(head + d, nh)
            wait_recv(hbuf.at[k, hh], hsem.at[2 * k + 1, hh], me, head)
            total = total + hbuf[k, hh]
            wait_send(hsrc.at[k], hsem.at[2 * k, hh], me, head)
        return total[0:1]

    if nz > 4:
        lap(1, 4)
        for h in (0, 1):
            weigh(at(3, h), h, True)

    scan_finish(nz, head, state_in, fwd)
    squares = jnp.zeros((B, 1), F32)
    for h in range(HL):
        row = run[h : h + 1]
        col = col_of(row)
        w = (mm_t(lin[h, 0], lin[h, 1]) * within_of(row, col)).astype(BF16)
        o = mm(w, lin[h, 2]) + jnp.exp(col) * mm(lin[h, 0], state_in[pl.ds(h * B, B), :])
        lo[h] = o
        query_t[h] = jnp.transpose(lin[h, 0].astype(F32) * jnp.exp(col)).astype(BF16)
        squares = squares + jnp.sum(o * o, axis=1, keepdims=True)
    hsrc[0] = jnp.broadcast_to(row_of(squares), (8, B))
    heads_start(0)

    if nz > 4:

        @pl.loop(5, nz - 1)
        def _(s):
            def rest():
                for h in (2, 3):
                    weigh(at(s - 2, h), h, True)

            lap(1, s, mid=rest)
            for h in (0, 1):
                weigh(at(s - 1, h), h, True)

        lap(1, nz - 1, last=True)
        for s, some in ((nz - 3, (2, 3)), (nz - 2, range(HL))):
            for h in some:
                weigh(at(s, h), h, True)
    settle(1, nz - 1, last=True)
    for h in range(HL):
        weigh(at(nz - 1, h), h, True)

    partial = jnp.zeros((B, 1), F32)
    for h in range(HL):
        c = (acc[0, h] + own[h, 1, 1].astype(F32)) * gain[h : h + 1, :]
        cot[h] = c
        partial = partial + jnp.sum(c * lo[h], axis=1, keepdims=True)
    hsrc[1] = jnp.broadcast_to(row_of(partial), (8, B))
    heads_start(1)

    del_own[...] = jnp.zeros_like(del_own)
    for h in range(HL):
        dv_out[h] = acc[0, h].astype(BF16)
        delta = jnp.sum(own[h, 1, 1].astype(F32) * acc[1, h], axis=1, keepdims=True)
        delta = jnp.broadcast_to(delta, (B, B))
        dcol[h] = delta
        del_own[h : h + 1, :] = jnp.transpose(delta)[0:1]
    small_start(nz, head, del_own, del_all, dsem)
    for h in range(HL):
        ds = (a1[z, h, 3] * (a2[z, h, 3] - dcol[h])).astype(BF16)
        dkq[1, h] = mm(ds, own[h, 0, 0])
        dkq[0, h] = t_mm(ds, own[h, 1, 0])

    def row_grads(k, off, keys):
        r = lax.rem(y + off, NY)
        t = 1 if keys else 0

        @pl.when((r < y) if keys else (r > y))
        def _():
            @pl.loop(0, nz // 4)
            def _(c):
                for h in range(HL):
                    parts, rows = [], []
                    for i in range(4):
                        zz = 4 * c + i
                        delta = dcol[h] if keys else del_all[r, zz, h : h + 1, :]
                        parts.append((a1[zz, h, k] * (a2[zz, h, k] - delta)).astype(BF16))
                        rows.append(pairs[zz, h, k, 0])
                    dkq[t, h] = dkq[t, h] + mm(jnp.concatenate(parts, axis=1), jnp.concatenate(rows, axis=0))

    def near_grads(keys):
        @pl.loop(0 if keys else z + 1, z if keys else nz)
        def _(zz):
            for h in range(HL):
                delta = dcol[h] if keys else del_all[y, zz, h : h + 1, :]
                ds = (a1[zz, h, 3] * (a2[zz, h, 3] - delta)).astype(BF16)
                t, slot = (1, 3) if keys else (0, 4)
                dkq[t, h] = dkq[t, h] + mm(ds, pairs[zz, h, slot, 0])

    width = HL * nh * B
    root = jnp.sqrt(heads_total(0) / width + EPS)
    inv = col_of(1.0 / root)
    for h in range(HL):
        cot[h] = cot[h] * inv
    cube = 1.0 / (width * root * root * root)
    inner = heads_total(1)
    factor = col_of(inner * cube)
    for h in range(HL):
        lc = cot[h] - lo[h] * factor
        cot[h] = lc
        state[pl.ds(h * B, B), :] = mm(query_t[h], lc.astype(BF16)).astype(BF16)
    scan_start(nz, head, state, bwd)
    row_grads(0, NY - 1, True)
    small_rows(nz, head, del_own, del_all, dsem)
    near_grads(True)
    row_grads(1, 1, True)
    scan_rows(nz, head, state, fin, bwd, True)
    near_grads(False)
    row_grads(2, 2, True)
    scan_spread(nz, head, fin, rev_out, bwd, True)
    for h in range(HL):
        row = run[h : h + 1]
        col = col_of(row)
        within = within_of(row, col)
        c = cot[h].astype(BF16)
        pair = (mm_t(c, lin[h, 2]) * within).astype(BF16)
        w = (mm_t(lin[h, 0], lin[h, 1]) * within).astype(BF16)
        o = mm(pair, lin[h, 1]) + jnp.exp(col) * mm_t(c, state_in[pl.ds(h * B, B), :])
        lin_dq[h] = o.astype(BF16)
        part_dk[h] = t_mm(pair, lin[h, 0])
        part_dv[h] = t_mm(w, c)
    small_finish(nz, head, del_own, del_all, dsem)
    for k, off in ((0, NY - 1), (1, 1), (2, 2)):
        row_grads(k, off, False)
    for h in range(HL):
        dk_out[h] = (dkq[0, h] * SCALE).astype(BF16)
        dq_out[h] = (dkq[1, h] * SCALE).astype(BF16)
    scan_finish(nz, head, rev_out, bwd)

    small_drain(nz, head, fin_own, fin, fsem)
    small_drain(nz, head, lse_own, lse_all, lsem)
    small_drain(nz, head, del_own, del_all, dsem)

    for a in range(2):

        def column_left(zz, h):
            wait_send(pairs.at[zz, h, 0, a], up_s.at[a, zz, h], me, head)
            wait_send(pairs.at[zz, h, 1, a], dn_s.at[a, zz, h], me, head)

        for h in range(HL):
            column_left(z, h)

            @pl.when(inner_row)
            def _():
                for k in (0, 1):
                    wait_send(pairs.at[z, h, k, a], rel_s.at[a, h, k], me, head)

        @pl.loop(0, nz - 1)
        def _(s):
            for h in range(HL):
                zz = at(s, h)
                wait_send(ring(a, zz, h), ring_s.at[a, zz, h], me, head)
                wait_send(opposite(a, zz, h), opp_s.at[a, zz, h], me, head)
                column_left(at(s + 1, h), h)


def fused(nz, nh, lists, counts, arrays, decay, gain):
    full = pl.BlockSpec(memory_space=pltpu.VMEM)
    smem = pl.BlockSpec(memory_space=pltpu.SMEM)
    sem = pltpu.SemaphoreType.DMA
    per_head = pltpu.VMEM((HL, B, B), F32)
    small = pltpu.VMEM((2 * HL, B), F32)
    small_all = pltpu.VMEM((NY, nz, 2 * HL, B), F32)
    low = jax.ShapeDtypeStruct((HL, B, B), BF16)
    wide = jax.ShapeDtypeStruct((HL, B, B), F32)
    return pl.pallas_call(
        functools.partial(fused_kernel, nz, nh),
        out_shape=(low,) * 4
        + (wide,) * 2
        + (jax.ShapeDtypeStruct((HL * B, B), BF16), jax.ShapeDtypeStruct((HL, 3, B, B), BF16)),
        in_specs=[smem, smem] + [full] * 9,
        out_specs=(full,) * 8,
        scratch_shapes=[
            pltpu.VMEM((HL, 2, 2, B, B), BF16),
            pltpu.VMEM((nz, HL, 5, 2, B, B), BF16),
            pltpu.VMEM((nz, HL, 4, B, B), F32),
            pltpu.VMEM((nz, HL, 4, B, B), F32),
            per_head,
            per_head,
            pltpu.VMEM((2, HL, B, B), F32),
            pltpu.VMEM((2, HL, B, B), F32),
            per_head,
            per_head,
            per_head,
            per_head,
            pltpu.VMEM((4, nz, B), F32),
            pltpu.VMEM((HL * B, B), BF16),
            pltpu.VMEM((HL * B, B), BF16),
            small,
            small_all,
            small,
            small_all,
            small,
            small_all,
            pltpu.VMEM((2, nh, 8, B), F32),
            pltpu.VMEM((2, 8, B), F32),
            pltpu.VMEM((HL * B, B), F32),
            pltpu.VMEM((HL, B, B), BF16),
            sem((2, nz, HL)),
            sem((2, nz, HL)),
            sem((2, nz, HL)),
            sem((2, nz, HL)),
            sem((2, nz, HL)),
            sem((2, nz, HL)),
            sem((2, nz, HL, 2)),
            sem((2, HL, 2)),
            sem((5, max(nz, NY))),
            sem((5, max(nz, NY))),
            sem((5, max(nz, NY))),
            sem((4, nh)),
        ]
        + scan_scratch(nz) * 2,
        compiler_params=pltpu.CompilerParams(
            collective_id=0, has_side_effects=True, vmem_limit_bytes=56 << 20
        ),
    )(lists, counts, *arrays, decay, gain)


def last_kernel(lin, dec, rev, dq, dk, dv, lq, pdk, pdv, o_lq, o_lk, o_lv, o_q, o_k, o_v, tmp):
    run = running_of(dec[...])
    trail = jnp.exp(run[:, B - 1 : B] - run)

    def put(ref, value):
        for h in range(HL):
            tmp[pl.ds(h, B, stride=HL), :] = value(h)
        ref[...] = tmp[...].astype(BF16)

    def lin_dk(h):
        return pdk[h] + col_of(trail[h : h + 1]) * mm_t(lin[h, 2], rev[pl.ds(h * B, B), :])

    def lin_dv(h):
        return pdv[h] + col_of(trail[h : h + 1]) * mm(lin[h, 1], rev[pl.ds(h * B, B), :])

    put(o_lq, lambda h: lq[h].astype(F32))
    put(o_lk, lin_dk)
    put(o_lv, lin_dv)
    put(o_q, lambda h: dq[h].astype(F32))
    put(o_k, lambda h: dk[h].astype(F32))
    put(o_v, lambda h: dv[h].astype(F32))


def last(lin, decay, rev, *parts):
    full = pl.BlockSpec(memory_space=pltpu.VMEM)
    return pl.pallas_call(
        last_kernel,
        out_shape=(jax.ShapeDtypeStruct((HL * B, B), BF16),) * 6,
        in_specs=[full] * 9,
        out_specs=(full,) * 6,
        scratch_shapes=[pltpu.VMEM((HL * B, B), F32)],
    )(lin, decay, rev, *parts)


def local(nz, nh, lin_q, lin_k, lin_v, decay, gain, soft_q, soft_k, soft_v, out_grad, lists, counts):
    flat = [a.reshape(B * HL, B) for a in (lin_q, lin_k, lin_v, soft_q, soft_k, soft_v, out_grad)]
    dq, dk, dv, lin_dq, part_dk, part_dv, rev, lin = fused(nz, nh, lists, counts, flat, decay, gain)
    grads = last(lin, decay, rev, dq, dk, dv, lin_dq, part_dk, part_dv)
    return tuple(a.reshape(B, HL, B) for a in grads)


def solution(mesh):
    nz = mesh.shape["ctx"] // NY
    tokens = P("ctx", "head", None)
    in_specs = (
        (tokens,) * 3 + (P("head", "ctx"), P("head", None)) + (tokens,) * 4 + (P("ctx", None), P("ctx"))
    )
    return jax.shard_map(
        functools.partial(local, nz, mesh.shape["head"]),
        mesh=mesh,
        in_specs=in_specs,
        out_specs=(tokens,) * 6,
        check_vma=False,
    )
```

```python
import functools

import jax
import jax.numpy as jnp
from jax import lax
from jax.experimental import pallas as pl
from jax.experimental.pallas import tpu as pltpu
from jax.sharding import PartitionSpec as P

NY = 4
HL = 4
B = 128
NSEL = 16
EPS = 1e-05
SCALE = 128 ** (-0.5)
NEG = -1e30
BIG = 1e30
F32 = jnp.float32
BF16 = jnp.bfloat16
MESH = pl.DeviceIdType.MESH
HIGH = lax.Precision.HIGHEST


def mm(a, b):
    return lax.dot_general(a, b, (((1,), (0,)), ((), ())), preferred_element_type=F32)


def mm_t(a, b):
    return lax.dot_general(a, b, (((1,), (1,)), ((), ())), preferred_element_type=F32)


def t_mm(a, b):
    return lax.dot_general(a, b, (((0,), (0,)), ((), ())), preferred_element_type=F32)


def iota(dim):
    return lax.broadcasted_iota(jnp.int32, (B, B), dim)


def col_of(row):
    return jnp.transpose(jnp.broadcast_to(row, (B, B)))


def row_of(col):
    return jnp.transpose(jnp.broadcast_to(col, (B, B)))[0:1]


def running_of(decay):
    upper = (iota(0) <= iota(1)).astype(F32)
    return lax.dot_general(
        decay, upper, (((1,), (0,)), ((), ())), precision=HIGH, preferred_element_type=F32
    )


def within_of(row, col):
    keep = iota(0) >= iota(1)
    return jnp.where(keep, jnp.exp(jnp.where(keep, col - row, 0.0)), 0.0)


def slot_of(r, y):
    return jnp.where(lax.rem(y + NY - 1, NY) == r, 0, jnp.where(lax.rem(y + 1, NY) == r, 1, 2))


def far_first(n):
    return sorted(range(1, n), key=lambda d: (-min(d, n - d), d))


def place(nz):
    own = lax.axis_index("ctx")
    return own // nz, lax.rem(own, nz)


def start_remote(src, dst, send, recv, ctx, head):
    pltpu.make_async_remote_copy(
        src_ref=src, dst_ref=dst, send_sem=send, recv_sem=recv, device_id=(ctx, head), device_id_type=MESH
    ).start()


def wait_recv(ref, recv, ctx, head):
    pltpu.make_async_remote_copy(
        src_ref=ref, dst_ref=ref, send_sem=recv, recv_sem=recv, device_id=(ctx, head), device_id_type=MESH
    ).wait_recv()


def wait_send(ref, send, ctx, head):
    pltpu.make_async_remote_copy(
        src_ref=ref, dst_ref=ref, send_sem=send, recv_sem=send, device_id=(ctx, head), device_id_type=MESH
    ).wait_send()


def scan_scratch(nz):
    rs = HL * B // nz
    return [
        pltpu.VMEM((nz, rs, B), BF16),
        pltpu.VMEM((nz, rs, B), F32),
        pltpu.VMEM((NY, rs, B), BF16),
        pltpu.VMEM((rs, B), BF16),
        pltpu.VMEM((nz, rs, B), BF16),
        pltpu.SemaphoreType.DMA((6, max(nz, NY))),
        pltpu.SemaphoreType.DMA((2,)),
        pltpu.VMEM((rs, B), F32),
    ]


def scan_start(nz, head, local, bufs):
    zbuf, sems, lsem = bufs[0], bufs[5], bufs[6]
    rs = HL * B // nz
    y, z = place(nz)
    for d in far_first(nz):
        zz = lax.rem(z + d, nz)
        start_remote(
            local.at[pl.ds(zz * rs, rs)], zbuf.at[z], sems.at[0, zz], sems.at[1, z], y * nz + zz, head
        )
    pltpu.make_async_copy(local.at[pl.ds(z * rs, rs)], zbuf.at[z], lsem.at[0]).start()


def scan_rows(nz, head, local, fin, bufs, reverse):
    zbuf, ebuf, tbuf, tsrc, _, sems, lsem, _ = bufs
    rs = HL * B // nz
    y, z = place(nz)
    own = y * nz + z
    hz = z * rs // B
    pltpu.make_async_copy(local.at[pl.ds(z * rs, rs)], zbuf.at[z], lsem.at[0]).wait()
    for d in range(1, nz):
        zz = lax.rem(z + d, nz)
        wait_recv(zbuf.at[zz], sems.at[1, zz], own, head)

    total = jnp.zeros((rs, B), F32)
    for lap in range(nz):
        m = nz - 1 - lap if reverse else lap
        ebuf[m] = total
        total = total * jnp.exp(fin[y, m, pl.ds(hz, 1), :]) + zbuf[m].astype(F32)
    tsrc[...] = total.astype(BF16)
    for yy in range(NY):

        @pl.when((yy < y) if reverse else (yy > y))
        def _():
            start_remote(tsrc, tbuf.at[y], sems.at[2, yy], sems.at[3, y], yy * nz + z, head)

    for d in range(1, nz):
        zz = lax.rem(z + d, nz)
        wait_send(zbuf.at[0], sems.at[0, zz], own, head)


def scan_spread(nz, head, fin, out, bufs, reverse):
    _, ebuf, tbuf, tsrc, sbuf, sems, lsem, cbuf = bufs
    rs = HL * B // nz
    y, z = place(nz)
    own = y * nz + z
    hz = z * rs // B
    for yy in range(NY):

        @pl.when((yy > y) if reverse else (yy < y))
        def _():
            wait_recv(tbuf.at[yy], sems.at[3, yy], own, head)

        @pl.when((yy < y) if reverse else (yy > y))
        def _():
            wait_send(tsrc, sems.at[2, yy], own, head)

    cbuf[...] = jnp.zeros_like(cbuf)
    for lap in range(NY):
        r = NY - 1 - lap if reverse else lap

        @pl.when((r > y) if reverse else (r < y))
        def _():
            span = jnp.zeros((1, B), F32)
            for m in range(nz):
                span = span + fin[r, m, pl.ds(hz, 1), :]
            cbuf[...] = cbuf[...] * jnp.exp(span) + tbuf[r].astype(F32)

    carry = cbuf[...]
    for lap in range(nz):
        m = nz - 1 - lap if reverse else lap
        sbuf[m] = (ebuf[m] + carry).astype(BF16)
        carry = carry * jnp.exp(fin[y, m, pl.ds(hz, 1), :])
    for d in far_first(nz):
        zz = lax.rem(z + d, nz)
        start_remote(
            sbuf.at[zz], out.at[pl.ds(z * rs, rs)], sems.at[4, zz], sems.at[5, z], y * nz + zz, head
        )
    pltpu.make_async_copy(sbuf.at[z], out.at[pl.ds(z * rs, rs)], lsem.at[1]).start()


def scan_finish(nz, head, out, bufs):
    sbuf, sems, lsem = bufs[4], bufs[5], bufs[6]
    rs = HL * B // nz
    y, z = place(nz)
    own = y * nz + z
    for d in range(1, nz):
        zz = lax.rem(z + d, nz)
        wait_recv(out.at[pl.ds(zz * rs, rs)], sems.at[5, zz], own, head)
        wait_send(sbuf.at[zz], sems.at[4, zz], own, head)
    pltpu.make_async_copy(sbuf.at[z], out.at[pl.ds(z * rs, rs)], lsem.at[1]).wait()


def small_start(nz, head, src, dst, sems):
    y, z = place(nz)
    for d in far_first(nz):
        zz = lax.rem(z + d, nz)
        start_remote(src, dst.at[y, z], sems.at[0, zz], sems.at[1, z], y * nz + zz, head)
    pltpu.make_async_copy(src, dst.at[y, z], sems.at[2, 0]).start()


def small_rows(nz, head, src, dst, sems):
    y, z = place(nz)
    own = y * nz + z
    for d in range(1, nz):
        zz = lax.rem(z + d, nz)
        wait_recv(dst.at[y, zz], sems.at[1, zz], own, head)
    pltpu.make_async_copy(src, dst.at[y, z], sems.at[2, 0]).wait()
    for d in range(1, NY):
        yy = lax.rem(y + d, NY)
        start_remote(dst.at[y], dst.at[y], sems.at[3, yy], sems.at[4, y], yy * nz + z, head)


def small_finish(nz, head, src, dst, sems):
    y, z = place(nz)
    own = y * nz + z
    for d in range(1, NY):
        yy = lax.rem(y + d, NY)
        wait_recv(dst.at[yy], sems.at[4, yy], own, head)


def small_drain(nz, head, src, dst, sems):
    y, z = place(nz)
    own = y * nz + z
    for d in range(1, nz):
        zz = lax.rem(z + d, nz)
        wait_send(src, sems.at[0, zz], own, head)
    for d in range(1, NY):
        yy = lax.rem(y + d, NY)
        wait_send(dst.at[y], sems.at[3, yy], own, head)


def greet(nz, head, nh):
    y, z = place(nz)
    barrier = pltpu.get_barrier_semaphore()
    for d in range(1, nz):
        pl.semaphore_signal(
            barrier, inc=1, device_id=(y * nz + lax.rem(z + d, nz), head), device_id_type=MESH
        )
    for d in range(1, NY):
        pl.semaphore_signal(
            barrier, inc=1, device_id=(lax.rem(y + d, NY) * nz + z, head), device_id_type=MESH
        )
    for d in range(1, nh):
        pl.semaphore_signal(
            barrier, inc=1, device_id=(y * nz + z, lax.rem(head + d, nh)), device_id_type=MESH
        )


def greeted(nz, nh):
    pl.semaphore_wait(pltpu.get_barrier_semaphore(), nz - 1 + NY - 1 + nh - 1)


def fused_kernel(
    nz,
    nh,
    lists,
    count,
    lq,
    lk,
    lv,
    sq,
    sk,
    sv,
    og,
    dec,
    gain,
    dq_out,
    dk_out,
    dv_out,
    lin_dq,
    part_dk,
    part_dv,
    rev_out,
    lin,
    own,
    pairs,
    a1,
    a2,
    mx,
    ls,
    acc,
    dkq,
    lcol,
    dcol,
    lo,
    cot,
    bias,
    state,
    state_in,
    fin_own,
    fin,
    lse_own,
    lse_all,
    del_own,
    del_all,
    hbuf,
    hsrc,
    tmp,
    query_t,
    ring_s,
    ring_r,
    opp_s,
    opp_r,
    up_s,
    dn_s,
    col_r,
    rel_s,
    fsem,
    lsem,
    dsem,
    hsem,
    *scans,
):
    fwd, bwd = scans[: len(scans) // 2], scans[len(scans) // 2 :]
    head = lax.axis_index("head")
    y, z = place(nz)
    me = y * nz + z
    right, left = y * nz + lax.rem(z + 1, nz), y * nz + lax.rem(z + nz - 1, nz)
    above, below = lax.rem(y + 1, NY) * nz + z, lax.rem(y + NY - 1, NY) * nz + z
    part_up = jnp.where(y < NY - 1, 0, 1)
    part_dn = jnp.where(y > 0, 1, 0)
    inner_row = (y == 1) | (y == 2)
    greet(nz, head, nh)

    def heads(ref, store):
        tmp[...] = ref[...].astype(F32)
        for h in range(HL):
            store(h, tmp[pl.ds(h, B, stride=HL), :].astype(BF16))

    def own_at(t, a):
        def store(h, value):
            own[h, t, a] = value

        return store

    def lin_at(i):
        def store(h, value):
            lin[h, i] = value

        return store

    heads(sk, own_at(0, 0))
    heads(sq, own_at(1, 0))
    greeted(nz, nh)

    def at(s, h):
        return lax.rem(z + nz - s, nz) if h % 2 == 0 else lax.rem(z + s, nz)

    def to_next(h):
        return right if h % 2 == 0 else left

    def ring(a, zz, h):
        return pairs.at[zz, h, pl.ds(3, 2), a]

    def ring_on(a, zz, h, src=None):
        start_remote(
            ring(a, zz, h) if src is None else src,
            ring(a, zz, h),
            ring_s.at[a, zz, h],
            ring_r.at[a, zz, h],
            to_next(h),
            head,
        )

    def opposite(a, zz, h):
        return pairs.at[zz, h, 2, a]

    def opposite_on(a, zz, h):
        ref = opposite(a, zz, h)
        start_remote(ref, ref, opp_s.at[a, zz, h], opp_r.at[a, zz, h], to_next(h), head)

    def opposite_wait(a, zz, h):
        wait_recv(opposite(a, zz, h), opp_r.at[a, zz, h], me, head)

    def column_on(a, zz, h, up, dn):
        start_remote(up, pairs.at[zz, h, 0, a], up_s.at[a, zz, h], col_r.at[a, zz, h, 0], above, head)
        start_remote(dn, pairs.at[zz, h, 1, a], dn_s.at[a, zz, h], col_r.at[a, zz, h, 1], below, head)

    def column_wait(a, zz, h):
        for k in (0, 1):
            wait_recv(pairs.at[zz, h, k, a], col_r.at[a, zz, h, k], me, head)

    def begin(a):
        for h in range(HL):
            column_on(a, z, h, own.at[h, part_up, a], own.at[h, part_dn, a])
            ring_on(a, z, h, own.at[h, pl.ds(0, 2), a])

    def relay(a, h):
        column_wait(a, z, h)

        @pl.when(inner_row)
        def _():
            for k, to in ((0, above), (1, below)):
                start_remote(
                    pairs.at[z, h, k, a], opposite(a, z, h), rel_s.at[a, h, k], opp_r.at[a, z, h], to, head
                )

    def settle(a, s, last=False):
        for h in range(HL):
            opposite_wait(a, at(s, h), h)
            if not last:
                opposite_on(a, at(s, h), h)
        for h in range(HL):
            column_wait(a, at(s, h), h)

    def lap(a, s, first=False, last=False, mid=None):
        for h in range(HL):
            zz = at(s, h)
            wait_recv(ring(a, zz, h), ring_r.at[a, zz, h], me, head)
            if not last:
                ring_on(a, zz, h)
            column_on(a, zz, h, pairs.at[zz, h, 3 + part_up, a], pairs.at[zz, h, 3 + part_dn, a])
        if mid is not None:
            mid()
        if first:
            for h in range(HL):
                relay(a, h)
            for h in range(HL):
                opposite_wait(a, z, h)
                opposite_on(a, z, h)
        else:
            settle(a, s - 1)

    lane = lax.broadcasted_iota(jnp.int32, (1, B), 1)
    causal = iota(0) >= iota(1)

    def kinds(zz, with_row):
        found = []
        for k, off in ((0, NY - 1), (1, 1), (2, 2)):
            r = lax.rem(y + off, NY)
            found.append((k, k, jnp.where(r < y, 1, 0), r))
        if with_row:
            t = jnp.where(zz < z, 1, 0)
            found.append((3, 4 - t, t, y))
        return found

    def score(zz, h, with_row):
        scores = []
        for k, slot, t, _ in kinds(zz, with_row):
            s = mm_t(own[h, t, 0], pairs[zz, h, slot, 0]) * SCALE
            a1[zz, h, k] = s
            scores.append(s + bias[k, pl.ds(zz, 1), :])
        top = functools.reduce(jnp.maximum, scores)
        m = jnp.maximum(mx[h], jnp.broadcast_to(jnp.max(top, axis=1, keepdims=True), (B, B)))
        total = ls[h] * jnp.exp(mx[h] - m)
        for s in scores:
            total = total + jnp.exp(s - m)
        mx[h] = m
        ls[h] = total

    def weigh(zz, h, with_row):
        for k, slot, t, r in kinds(zz, with_row):
            here = jnp.sum(
                jnp.where(lane == me, fin[r, zz, HL : HL + 1, :], 0.0), axis=1, keepdims=True
            )
            theirs = jnp.where(here > 0.5, lse_all[r, zz, h : h + 1, :], BIG)
            lse = jnp.where(t == 1, lcol[h] - bias[k, pl.ds(zz, 1), :], theirs)
            v = pairs[zz, h, slot, 1]
            p = jnp.exp(a1[zz, h, k] - lse)
            a1[zz, h, k] = p
            a2[zz, h, k] = mm_t(own[h, t, 1], v)
            acc[t, h] = acc[t, h] + mm(p.astype(BF16), v)

    begin(0)

    def start_scores():
        for h in range(HL):
            s = jnp.where(causal, mm_t(own[h, 1, 0], own[h, 0, 0]) * SCALE, NEG)
            m = jnp.broadcast_to(jnp.max(s, axis=1, keepdims=True), (B, B))
            mx[h] = m
            ls[h] = jnp.exp(s - m)
        column = lax.broadcasted_iota(jnp.int32, (nz, B), 0)
        for k, off in ((0, NY - 1), (1, 1), (2, 2), (3, 0)):
            block = lax.rem(y + off, NY) * nz + column
            b = jnp.full((nz, B), NEG, F32)
            for e in range(NSEL):
                b = jnp.where((block == lists[0, e]) & (e < count[0]), 0.0, b)
            bias[k] = b

    lap(0, 1, first=True, mid=start_scores)
    heads(sv, own_at(0, 1))
    heads(og, own_at(1, 1))
    heads(lk, lin_at(1))
    heads(lv, lin_at(2))
    heads(lq, lin_at(0))
    run = running_of(dec[...])
    named = jnp.zeros((1, B), F32)
    for e in range(NSEL):
        named = jnp.where((lane == lists[0, e]) & (e < count[0]), 1.0, named)
    finish = run[:, B - 1 : B]
    fin_own[...] = jnp.concatenate(
        [jnp.broadcast_to(finish, (HL, B)), named, jnp.zeros((HL - 1, B), F32)], axis=0
    )
    trailing = jnp.exp(finish - run)
    for h in range(HL):
        k = lin[h, 1].astype(F32) * col_of(trailing[h : h + 1])
        state[pl.ds(h * B, B), :] = t_mm(k.astype(BF16), lin[h, 2]).astype(BF16)
    small_start(nz, head, fin_own, fin, fsem)
    scan_start(nz, head, state, fwd)
    for h in range(HL):
        score(z, h, False)
    lap(0, 2)
    for h in (0, 1):
        score(at(1, h), h, True)
    small_rows(nz, head, fin_own, fin, fsem)
    scan_rows(nz, head, state, fin, fwd, False)

    @pl.loop(3, nz - 1)
    def _(s):
        def rest():
            for h in (2, 3):
                score(at(s - 2, h), h, True)

        lap(0, s, mid=rest)
        for h in (0, 1):
            score(at(s - 1, h), h, True)

    begin(1)

    def rest(s):
        for h in (2, 3):
            score(at(s, h), h, True)

    lap(0, nz - 1, last=True, mid=lambda: rest(nz - 3))
    for h in (0, 1):
        score(at(nz - 2, h), h, True)
    lap(1, 1, first=True, mid=lambda: rest(nz - 2))
    settle(0, nz - 1, last=True)
    for h in range(HL):
        score(at(nz - 1, h), h, True)
    lse_own[...] = jnp.zeros_like(lse_own)
    for h in range(HL):
        lse = mx[h] + jnp.log(jnp.sum(ls[h], axis=1, keepdims=True))
        lcol[h] = lse
        lse_own[h : h + 1, :] = jnp.transpose(lse)[0:1]
    small_start(nz, head, lse_own, lse_all, lsem)
    small_finish(nz, head, fin_own, fin, fsem)
    scan_spread(nz, head, fin, state_in, fwd, False)
    lap(1, 2)
    small_rows(nz, head, lse_own, lse_all, lsem)
    for h in range(HL):
        p = jnp.where(causal, jnp.exp(mm_t(own[h, 1, 0], own[h, 0, 0]) * SCALE - lcol[h]), 0.0)
        dp = mm_t(own[h, 1, 1], own[h, 0, 1])
        a1[z, h, 3] = p
        a2[z, h, 3] = dp
        low = p.astype(BF16)
        acc[1, h] = mm(low, own[h, 0, 1])
        acc[0, h] = t_mm(low, own[h, 1, 1])
    lap(1, 3, last=nz == 4)
    small_finish(nz, head, lse_own, lse_all, lsem)
    for h in range(HL):
        weigh(z, h, False)
    for s in (1, 2):
        for h in range(HL):
            weigh(at(s, h), h, True)

    def heads_start(k):
        for d in range(1, nh):
            hh = lax.rem(head + d, nh)
            start_remote(hsrc.at[k], hbuf.at[k, head], hsem.at[2 * k, hh], hsem.at[2 * k + 1, head], me, hh)

    def heads_total(k):
        total = hsrc[k]
        for d in range(1, nh):
            hh = lax.rem(head + d, nh)
            wait_recv(hbuf.at[k, hh], hsem.at[2 * k + 1, hh], me, head)
            total = total + hbuf[k, hh]
            wait_send(hsrc.at[k], hsem.at[2 * k, hh], me, head)
        return total[0:1]

    if nz > 4:
        lap(1, 4)
        for h in (0, 1):
            weigh(at(3, h), h, True)

    scan_finish(nz, head, state_in, fwd)
    squares = jnp.zeros((B, 1), F32)
    for h in range(HL):
        row = run[h : h + 1]
        col = col_of(row)
        w = (mm_t(lin[h, 0], lin[h, 1]) * within_of(row, col)).astype(BF16)
        o = mm(w, lin[h, 2]) + jnp.exp(col) * mm(lin[h, 0], state_in[pl.ds(h * B, B), :])
        lo[h] = o
        query_t[h] = jnp.transpose(lin[h, 0].astype(F32) * jnp.exp(col)).astype(BF16)
        squares = squares + jnp.sum(o * o, axis=1, keepdims=True)
    hsrc[0] = jnp.broadcast_to(row_of(squares), (8, B))
    heads_start(0)

    if nz > 4:

        @pl.loop(5, nz - 1)
        def _(s):
            def rest():
                for h in (2, 3):
                    weigh(at(s - 2, h), h, True)

            lap(1, s, mid=rest)
            for h in (0, 1):
                weigh(at(s - 1, h), h, True)

        lap(1, nz - 1, last=True)
        for s, some in ((nz - 3, (2, 3)), (nz - 2, range(HL))):
            for h in some:
                weigh(at(s, h), h, True)
    for h in range(HL):
        opposite_wait(1, at(nz - 1, h), h)
        column_wait(1, at(nz - 1, h), h)
        weigh(at(nz - 1, h), h, True)

    partial = jnp.zeros((B, 1), F32)
    for h in range(HL):
        c = (acc[0, h] + own[h, 1, 1].astype(F32)) * gain[h : h + 1, :]
        cot[h] = c
        partial = partial + jnp.sum(c * lo[h], axis=1, keepdims=True)
    hsrc[1] = jnp.broadcast_to(row_of(partial), (8, B))
    heads_start(1)

    del_own[...] = jnp.zeros_like(del_own)
    for h in range(HL):
        dv_out[h] = acc[0, h].astype(BF16)
        delta = jnp.sum(own[h, 1, 1].astype(F32) * acc[1, h], axis=1, keepdims=True)
        delta = jnp.broadcast_to(delta, (B, B))
        dcol[h] = delta
        del_own[h : h + 1, :] = jnp.transpose(delta)[0:1]
    small_start(nz, head, del_own, del_all, dsem)
    for h in range(HL):
        ds = (a1[z, h, 3] * (a2[z, h, 3] - dcol[h])).astype(BF16)
        dkq[1, h] = mm(ds, own[h, 0, 0])
        dkq[0, h] = t_mm(ds, own[h, 1, 0])

    def row_grads(k, off, keys):
        r = lax.rem(y + off, NY)
        t = 1 if keys else 0

        @pl.when((r < y) if keys else (r > y))
        def _():
            @pl.loop(0, nz // 4)
            def _(c):
                for h in range(HL):
                    parts, rows = [], []
                    for i in range(4):
                        zz = 4 * c + i
                        delta = dcol[h] if keys else del_all[r, zz, h : h + 1, :]
                        parts.append((a1[zz, h, k] * (a2[zz, h, k] - delta)).astype(BF16))
                        rows.append(pairs[zz, h, k, 0])
                    dkq[t, h] = dkq[t, h] + mm(jnp.concatenate(parts, axis=1), jnp.concatenate(rows, axis=0))

    def near_grads(keys):
        @pl.loop(0 if keys else z + 1, z if keys else nz)
        def _(zz):
            for h in range(HL):
                delta = dcol[h] if keys else del_all[y, zz, h : h + 1, :]
                ds = (a1[zz, h, 3] * (a2[zz, h, 3] - delta)).astype(BF16)
                t, slot = (1, 3) if keys else (0, 4)
                dkq[t, h] = dkq[t, h] + mm(ds, pairs[zz, h, slot, 0])

    width = HL * nh * B
    root = jnp.sqrt(heads_total(0) / width + EPS)
    inv = col_of(1.0 / root)
    for h in range(HL):
        cot[h] = cot[h] * inv
    cube = 1.0 / (width * root * root * root)
    inner = heads_total(1)
    factor = col_of(inner * cube)
    for h in range(HL):
        lc = cot[h] - lo[h] * factor
        cot[h] = lc
        state[pl.ds(h * B, B), :] = mm(query_t[h], lc.astype(BF16)).astype(BF16)
    scan_start(nz, head, state, bwd)
    row_grads(0, NY - 1, True)
    small_rows(nz, head, del_own, del_all, dsem)
    near_grads(True)
    row_grads(1, 1, True)
    scan_rows(nz, head, state, fin, bwd, True)
    near_grads(False)
    row_grads(2, 2, True)
    scan_spread(nz, head, fin, rev_out, bwd, True)
    for h in range(HL):
        row = run[h : h + 1]
        col = col_of(row)
        within = within_of(row, col)
        c = cot[h].astype(BF16)
        pair = (mm_t(c, lin[h, 2]) * within).astype(BF16)
        w = (mm_t(lin[h, 0], lin[h, 1]) * within).astype(BF16)
        o = mm(pair, lin[h, 1]) + jnp.exp(col) * mm_t(c, state_in[pl.ds(h * B, B), :])
        lin_dq[h] = o.astype(BF16)
        part_dk[h] = t_mm(pair, lin[h, 0])
        part_dv[h] = t_mm(w, c)
    small_finish(nz, head, del_own, del_all, dsem)
    for k, off in ((0, NY - 1), (1, 1), (2, 2)):
        row_grads(k, off, False)
    for h in range(HL):
        dk_out[h] = (dkq[0, h] * SCALE).astype(BF16)
        dq_out[h] = (dkq[1, h] * SCALE).astype(BF16)
    scan_finish(nz, head, rev_out, bwd)

    small_drain(nz, head, fin_own, fin, fsem)
    small_drain(nz, head, lse_own, lse_all, lsem)
    small_drain(nz, head, del_own, del_all, dsem)

    for a in range(2):

        def column_left(zz, h):
            wait_send(pairs.at[zz, h, 0, a], up_s.at[a, zz, h], me, head)
            wait_send(pairs.at[zz, h, 1, a], dn_s.at[a, zz, h], me, head)

        for h in range(HL):
            column_left(z, h)

            @pl.when(inner_row)
            def _():
                for k in (0, 1):
                    wait_send(pairs.at[z, h, k, a], rel_s.at[a, h, k], me, head)

        @pl.loop(0, nz - 1)
        def _(s):
            for h in range(HL):
                zz = at(s, h)
                wait_send(ring(a, zz, h), ring_s.at[a, zz, h], me, head)
                wait_send(opposite(a, zz, h), opp_s.at[a, zz, h], me, head)
                column_left(at(s + 1, h), h)


def fused(nz, nh, lists, counts, arrays, decay, gain):
    full = pl.BlockSpec(memory_space=pltpu.VMEM)
    smem = pl.BlockSpec(memory_space=pltpu.SMEM)
    sem = pltpu.SemaphoreType.DMA
    per_head = pltpu.VMEM((HL, B, B), F32)
    small = pltpu.VMEM((2 * HL, B), F32)
    small_all = pltpu.VMEM((NY, nz, 2 * HL, B), F32)
    low = jax.ShapeDtypeStruct((HL, B, B), BF16)
    wide = jax.ShapeDtypeStruct((HL, B, B), F32)
    return pl.pallas_call(
        functools.partial(fused_kernel, nz, nh),
        out_shape=(low,) * 4
        + (wide,) * 2
        + (jax.ShapeDtypeStruct((HL * B, B), BF16), jax.ShapeDtypeStruct((HL, 3, B, B), BF16)),
        in_specs=[smem, smem] + [full] * 9,
        out_specs=(full,) * 8,
        scratch_shapes=[
            pltpu.VMEM((HL, 2, 2, B, B), BF16),
            pltpu.VMEM((nz, HL, 5, 2, B, B), BF16),
            pltpu.VMEM((nz, HL, 4, B, B), F32),
            pltpu.VMEM((nz, HL, 4, B, B), F32),
            per_head,
            per_head,
            pltpu.VMEM((2, HL, B, B), F32),
            pltpu.VMEM((2, HL, B, B), F32),
            per_head,
            per_head,
            per_head,
            per_head,
            pltpu.VMEM((4, nz, B), F32),
            pltpu.VMEM((HL * B, B), BF16),
            pltpu.VMEM((HL * B, B), BF16),
            small,
            small_all,
            small,
            small_all,
            small,
            small_all,
            pltpu.VMEM((2, nh, 8, B), F32),
            pltpu.VMEM((2, 8, B), F32),
            pltpu.VMEM((HL * B, B), F32),
            pltpu.VMEM((HL, B, B), BF16),
            sem((2, nz, HL)),
            sem((2, nz, HL)),
            sem((2, nz, HL)),
            sem((2, nz, HL)),
            sem((2, nz, HL)),
            sem((2, nz, HL)),
            sem((2, nz, HL, 2)),
            sem((2, HL, 2)),
            sem((5, max(nz, NY))),
            sem((5, max(nz, NY))),
            sem((5, max(nz, NY))),
            sem((4, nh)),
        ]
        + scan_scratch(nz) * 2,
        compiler_params=pltpu.CompilerParams(
            collective_id=0, has_side_effects=True, vmem_limit_bytes=56 << 20
        ),
    )(lists, counts, *arrays, decay, gain)


def last_kernel(lin, dec, rev, dq, dk, dv, lq, pdk, pdv, o_lq, o_lk, o_lv, o_q, o_k, o_v, tmp):
    run = running_of(dec[...])
    trail = jnp.exp(run[:, B - 1 : B] - run)

    def put(ref, value):
        for h in range(HL):
            tmp[pl.ds(h, B, stride=HL), :] = value(h)
        ref[...] = tmp[...].astype(BF16)

    def lin_dk(h):
        return pdk[h] + col_of(trail[h : h + 1]) * mm_t(lin[h, 2], rev[pl.ds(h * B, B), :])

    def lin_dv(h):
        return pdv[h] + col_of(trail[h : h + 1]) * mm(lin[h, 1], rev[pl.ds(h * B, B), :])

    put(o_lq, lambda h: lq[h].astype(F32))
    put(o_lk, lin_dk)
    put(o_lv, lin_dv)
    put(o_q, lambda h: dq[h].astype(F32))
    put(o_k, lambda h: dk[h].astype(F32))
    put(o_v, lambda h: dv[h].astype(F32))


def last(lin, decay, rev, *parts):
    full = pl.BlockSpec(memory_space=pltpu.VMEM)
    return pl.pallas_call(
        last_kernel,
        out_shape=(jax.ShapeDtypeStruct((HL * B, B), BF16),) * 6,
        in_specs=[full] * 9,
        out_specs=(full,) * 6,
        scratch_shapes=[pltpu.VMEM((HL * B, B), F32)],
    )(lin, decay, rev, *parts)


def local(nz, nh, lin_q, lin_k, lin_v, decay, gain, soft_q, soft_k, soft_v, out_grad, lists, counts):
    flat = [a.reshape(B * HL, B) for a in (lin_q, lin_k, lin_v, soft_q, soft_k, soft_v, out_grad)]
    dq, dk, dv, lin_dq, part_dk, part_dv, rev, lin = fused(nz, nh, lists, counts, flat, decay, gain)
    grads = last(lin, decay, rev, dq, dk, dv, lin_dq, part_dk, part_dv)
    return tuple(a.reshape(B, HL, B) for a in grads)


def solution(mesh):
    nz = mesh.shape["ctx"] // NY
    tokens = P("ctx", "head", None)
    in_specs = (
        (tokens,) * 3 + (P("head", "ctx"), P("head", None)) + (tokens,) * 4 + (P("ctx", None), P("ctx"))
    )
    return jax.shard_map(
        functools.partial(local, nz, mesh.shape["head"]),
        mesh=mesh,
        in_specs=in_specs,
        out_specs=(tokens,) * 6,
        check_vma=False,
    )
```
